32 devices in a mesh: patch: 8 (over z, core), visit: 4 (over y, x).
Axes of the slice: x: 2, y: 2, z: 4, core: 2. Of those that a mesh axis runs over, the one named last changes fastest.
Arguments:
- blocks: bfloat16 [8, 4, 16, 256, 256], P('patch', 'visit'), may hold values from -6 to 6
- block_patch: int32 [8, 4, 16, 1], P('patch', 'visit'), may hold values from 0 to 7; in each aligned block of 16 rows (0 to 15, 16 to 31, ..., all dimensions but the last counted through in order) at most 2 rows name the same one
- block_slot: int32 [8, 4, 16], P('patch', 'visit'), may hold values from 0 to 7
- block_count: int32 [8, 4], P('patch', 'visit'), may hold values from 12 to 16, as said below
- template: bfloat16 [8, 512, 1024], P('patch', 'visit'), may hold values from -6 to 6
- basis_rows: bfloat16 [9, 21], replicated, may hold values from -1.25 to 1.25
- basis_cols: float32 [9, 21], replicated, may hold values from -1.25 to 1.25
- coeffs: float32 [4, 9], P('visit'), may hold values from -2 to 2
- psf_rows: bfloat16 [4, 2, 25], P('visit'), may hold values from -1.25 to 1.25
- psf_cols: bfloat16 [4, 2, 25], P('visit'), may hold values from -1.25 to 1.25
Outputs:
- filtered: float32 [8, 4, 512, 1024], P('patch', 'visit')
The draws below stay inside these ranges and needn't reach their ends.
Inputs may be any that keep to these rules, and one draw needn't show every extreme that they name: `block_patch`: among the 16 entries of one list (one patch index and visit) no patch is named more than 2 times, and some list names a patch exactly 2 times. Entries at positions block_count and beyond are unused.
All inputs are finite; a program needn't handle non-finite values.
Results may differ from the reference program's by a relative error of at most 0.005.
Values may be sent and summed in bfloat16 or wider, within the bound.
A program may use at most 128 MiB of HBM per device.

```python
import math
import jax
import jax.numpy as jnp
import numpy as np
from jax import lax

BLK = 256
PATCH_ROWS = 512
PATCH_COLS = 1024
NB_DEV = 16
CAP = 2
NBASIS = 9
KBASIS = 21
KPSF = 25
NPSF = 2
SLOTS = 8
N_PATCH = 8
N_VISIT = 4


def draw_block_count(key, part):
    counts = jax.random.randint(key, (N_PATCH, N_VISIT), 3 * NB_DEV // 4, NB_DEV + 1)
    counts = counts.at[0, 0].set(NB_DEV)
    counts = counts.at[N_PATCH - 1, N_VISIT - 1].set(3 * NB_DEV // 4)
    return counts.astype(jnp.int32)


def plant(array, rng, smallest, high):
    index_at = [jax.random.randint(jax.random.fold_in(rng, axis), (), 0, length) for axis, length in enumerate(array.shape)]
    longest = array.shape.index(max(array.shape))
    beside = index_at[:longest] + [(index_at[longest] + 1) % array.shape[longest]] + index_at[longest + 1:]
    return array.at[tuple(index_at)].set(smallest).at[tuple(beside)].set(high)


def steps_of(rng, dims, split, least, high):
    factor_of = 1.0
    for position, blocks in split:
        draws = jax.random.uniform(jax.random.fold_in(jax.random.fold_in(rng, 6), position), (blocks,), jnp.float32, least / len(split), high / len(split))
        factor_of = factor_of * jnp.repeat(jnp.exp(draws), dims[position] // blocks).reshape((-1,) + (1,) * (len(dims) - 1 - position))
    return factor_of


def assign_block(own_key, own, number, rows, amount, top, limit, lean):
    order = jax.random.permutation(own_key, amount)
    crowded, ordinary = shares(amount, rows * top, limit, lean, True), shares(amount, rows * top, limit, lean, False)
    places = jnp.arange(amount)

    def named(sizes, offset_by):
        used = int((sizes > 0).sum())
        fixed = max(1, used // 4)
        shifted = fixed + (places - fixed + offset_by * (used - fixed)) % max(1, amount - fixed)
        return jnp.zeros((amount,), jnp.int32).at[order[jnp.where(places < fixed, places, shifted)]].set(jnp.asarray(sizes, jnp.int32))

    sizes = jnp.where(number % 4 == 0, named(crowded, number // 4), named(ordinary, number - number // 4 - 1))
    mixed = jax.random.permutation(jax.random.fold_in(own, 3), amount)
    giver, taker = mixed[0:amount // 2 * 2:2], mixed[1:amount // 2 * 2:2]
    slack = jnp.minimum(sizes[giver] - 1, limit - sizes[taker]) // 2
    slack = jnp.where((giver == order[0]) | (taker == order[0]) | (sizes[taker] == 0), 0, jnp.maximum(slack, 0))
    shifted = jax.random.randint(jax.random.fold_in(own, 4), (amount // 2,), 0, 1 << 20) % (slack + 1)
    sizes = sizes.at[giver].add(-shifted).at[taker].add(shifted)
    labels = jnp.searchsorted(jnp.cumsum(sizes), jnp.arange(rows * top), side="right").astype(jnp.int32)
    listing = labels.reshape(top, rows).T
    listing = listing[jax.random.permutation(jax.random.fold_in(own, 1), rows)]
    offset_by = jax.random.randint(jax.random.fold_in(own, 2), (rows, 1), 0, top)
    return jnp.take_along_axis(listing, (jnp.arange(top)[None, :] + offset_by) % top, axis=1)


def shares(count, total, bound, skew, full):
    loads = [(1 << 20) // math.isqrt(grade ** skew) + 1 for grade in range(1, count + 1)]
    largest = bound if full else min(bound, max(-(-total // count), total * loads[0] // sum(loads)))
    least = 1 if total - largest >= count - 1 else 0
    given, rest = [largest] + [least] * (count - 1), total - largest - least * (count - 1)
    while rest > 0:
        free = [i for i in range(1, count) if given[i] < largest] or [i for i in range(1, count) if given[i] < bound]
        mass, remaining = sum([loads[i] for i in free]), rest
        for i in free:
            addition = min(bound - given[i], max(1, remaining * loads[i] // mass), rest)
            given[i] = given[i] + addition
            rest = rest - addition
    return np.array(given)


def noise(rng, shape, scale, most, shards=(), held_as=jnp.bfloat16):
    values = scale * jax.random.normal(rng, shape, jnp.float32)
    if shards:
        values = values * steps_of(rng, shape, shards, -0.22, 0.18)
    return jnp.clip(values, -most, most).astype(held_as)


def setup_inputs(seed: int = 0) -> dict:
    seeds = jax.random.split(jax.random.key(seed), 11)
    blocks = noise(seeds[0], (N_PATCH, N_VISIT, NB_DEV, BLK, BLK), 1.0, 6.0, ((0, 8), (1, 4)))
    block_patch_keys = jax.random.split(jax.random.fold_in(seeds[1], 1), N_PATCH * N_VISIT * NB_DEV // NB_DEV)
    block_patch_turns = jax.random.permutation(jax.random.fold_in(seeds[1], 3), N_PATCH * N_VISIT * NB_DEV // NB_DEV)
    block_patch = jax.vmap(lambda own, number: assign_block(jax.random.fold_in(seeds[1], 2), own, number, NB_DEV, N_PATCH, 1, CAP, 2))(block_patch_keys, block_patch_turns).reshape((N_PATCH, N_VISIT, NB_DEV, 1))
    block_slot = plant(jax.random.randint(seeds[2], (N_PATCH, N_VISIT, NB_DEV), 0, SLOTS), jax.random.fold_in(seeds[2], 1), 0, SLOTS - 1).astype(jnp.int32)
    block_count = draw_block_count(jax.random.fold_in(seeds[10], 71), 0)
    template = noise(seeds[4], (N_PATCH, PATCH_ROWS, PATCH_COLS), 1.0, 6.0, ((0, 8), (1, 4)))
    basis_rows = noise(seeds[5], (NBASIS, KBASIS), KBASIS ** -0.5, 1.25)
    basis_cols = noise(seeds[6], (NBASIS, KBASIS), KBASIS ** -0.5, 1.25, (), jnp.float32)
    coeffs = noise(seeds[7], (N_VISIT, NBASIS), 0.33, 2.0, ((0, 4),), jnp.float32)
    psf_rows = noise(seeds[8], (N_VISIT, NPSF, KPSF), KPSF ** -0.5, 1.25, ((0, 4),))
    psf_cols = noise(seeds[9], (N_VISIT, NPSF, KPSF), KPSF ** -0.5, 1.25, ((0, 4),))
    return {"blocks": blocks, "block_patch": block_patch, "block_slot": block_slot, "block_count": block_count, "template": template, "basis_rows": basis_rows, "basis_cols": basis_cols, "coeffs": coeffs, "psf_rows": psf_rows, "psf_cols": psf_cols}


def rounded(values):
    return lax.optimization_barrier(values.astype(jnp.bfloat16)).astype(jnp.float32)


def correlate(source, kernel_taps, along_axis):
    length = kernel_taps.shape[-1]
    half_len = length // 2
    extent = source.shape[along_axis]
    padding = [(0, 0)] * source.ndim
    padding[along_axis] = (half_len, half_len)
    padded = jnp.pad(source, padding)
    summed = jnp.zeros(source.shape, jnp.float32)
    for offset in range(length):
        summed = summed + kernel_taps[:, offset][:, None, None] * lax.slice_in_dim(padded, offset, offset + extent, axis=along_axis)
    return summed


def reference(blocks, block_patch, block_slot, block_count, template, basis_rows, basis_cols, coeffs, psf_rows, psf_cols):
    tall_count = PATCH_ROWS // BLK
    wide_count = PATCH_COLS // BLK
    live_mask = jnp.arange(NB_DEV, dtype=jnp.int32)[None, None, :] < block_count[:, :, None]
    destination = block_patch[..., 0]
    row_taps = basis_rows.astype(jnp.float32)

    def one_patch(patch_id):
        source = jnp.broadcast_to(template[patch_id].astype(jnp.float32)[None], (NBASIS, PATCH_ROWS, PATCH_COLS))
        smoothed = rounded(correlate(source, row_taps, 2))

        def one_visit(visit_id):
            chosen = live_mask[:, visit_id] & (destination[:, visit_id] == patch_id)
            segment_ids = jnp.where(chosen, block_slot[:, visit_id], SLOTS).reshape(-1).astype(jnp.int32)
            pieces = blocks[:, visit_id].astype(jnp.float32).reshape(N_PATCH * NB_DEV, BLK * BLK)
            slot_images = jax.ops.segment_sum(pieces, segment_ids, num_segments=SLOTS)
            science = slot_images.reshape(tall_count, wide_count, BLK, BLK).transpose(0, 2, 1, 3).reshape(PATCH_ROWS, PATCH_COLS)
            scaled = rounded(coeffs[visit_id][:, None] * basis_cols)
            model_image = jnp.sum(correlate(smoothed, scaled, 1), axis=0)
            difference = rounded(science - model_image)
            spread = jnp.broadcast_to(difference[None], (NPSF, PATCH_ROWS, PATCH_COLS))
            blurred = rounded(correlate(spread, psf_rows[visit_id].astype(jnp.float32), 2))
            return jnp.sum(correlate(blurred, psf_cols[visit_id].astype(jnp.float32), 1), axis=0)

        return lax.map(one_visit, jnp.arange(N_VISIT, dtype=jnp.int32))

    return lax.map(one_patch, jnp.arange(N_PATCH, dtype=jnp.int32))
```

```python
import functools

import jax
import jax.numpy as jnp
from jax import lax
from jax.experimental import pallas as pl
from jax.experimental.pallas import tpu as pltpu
from jax.sharding import PartitionSpec as P

CAP = 2
LANE = 128
HALF = 64
EDGE = 16
WIN = 256
F32 = jnp.float32
BF16 = jnp.bfloat16
VMEM_LIMIT = 32 * 1024 * 1024


def toeplitz(row, half_len):
    wide = jnp.broadcast_to(row, (LANE, WIN))
    return pltpu.roll(wide, (HALF - half_len) // 8 * 8, 1, stride=1, stride_axis=0)


def spread(taps, staged):
    count, length = taps.shape
    staged[...] = jnp.zeros(staged.shape, F32)
    staged[:count, :length] = taps
    lead = (HALF - length // 2) % 8
    if lead:
        staged[...] = pltpu.roll(staged[...], lead, 1)


def shift_into(load_tile, shifted, height, tiles, step):
    def body(r, carry):
        rows = pl.ds(pl.multiple_of(r * step, step), step)
        lane = lax.broadcasted_iota(jnp.int32, (step, LANE), 1)
        before = jnp.zeros((step, LANE), F32)
        for t in range(tiles):
            rolled = pltpu.roll(load_tile(rows, t), HALF, 1)
            shifted[rows, t * LANE : (t + 1) * LANE] = jnp.where(lane < HALF, before, rolled).astype(BF16)
            before = rolled
        shifted[rows, tiles * LANE :] = jnp.where(lane < HALF, before, 0.0).astype(BF16)
        return carry

    lax.fori_loop(0, height // step, body, 0)


def columns_pass(shifted, tables, smooth, pair, count, height, margin=HALF):
    for side in range(2):
        start = pl.multiple_of((2 * pair + side) * LANE, LANE)
        window = shifted[:, pl.ds(start, WIN)]
        for group in range(0, count, 2):
            taken = min(2, count - group)
            got = jnp.dot(
                window, tables[:, group * LANE : (group + taken) * LANE], preferred_element_type=F32
            ).astype(BF16)
            for k in range(taken):
                smooth[group + k, margin : margin + height, side * LANE : (side + 1) * LANE] = got[
                    :, k * LANE : (k + 1) * LANE
                ]


def rows_pass(smooth, tables, count, r):
    start = pl.multiple_of(r * LANE, LANE)
    total = jnp.zeros((LANE, WIN), F32)
    for k in range(count):
        total = total + jnp.dot(tables[k], smooth[k, pl.ds(start, WIN), :], preferred_element_type=F32)
    return total


def spread_table(staged, half_len, reach, count):
    wide_rows = reach + 2 * EDGE
    lane = lax.broadcasted_iota(jnp.int32, (wide_rows, WIN), 1)
    joined = jnp.zeros((wide_rows, WIN), F32)
    for k in range(count):
        shift = (k * reach - EDGE - half_len - (HALF - half_len) % 8) % WIN
        wide = jnp.broadcast_to(staged[k : k + 1, :], (wide_rows, WIN))
        rolled = pltpu.roll(wide, shift, 1, stride=1, stride_axis=0)
        joined = jnp.where((lane >= k * reach) & (lane < (k + 1) * reach), rolled, joined)
    return joined[:, : count * reach].astype(BF16)


def build_tables(column_taps, row_taps, column_tables, row_tables, staged):
    spread(column_taps, staged)
    for k in range(column_taps.shape[0]):
        table = toeplitz(staged[k : k + 1, :], column_taps.shape[1] // 2)
        column_tables[:, k * LANE : (k + 1) * LANE] = table.T.astype(BF16)
    spread(row_taps, staged)
    half_len = row_taps.shape[1] // 2
    if isinstance(row_tables, dict):
        for reach, table in row_tables.items():
            table[...] = spread_table(staged, half_len, reach, row_taps.shape[0])
    else:
        for k in range(row_taps.shape[0]):
            row_tables[k] = toeplitz(staged[k : k + 1, :], half_len).astype(BF16)


def clear_edges(smooth, count, height):
    for k in range(count):
        smooth[k, :HALF, :] = jnp.zeros((HALF, smooth.shape[2]), BF16)
        smooth[k, HALF + height :, :] = jnp.zeros((HALF, smooth.shape[2]), BF16)


def cuts(edge):
    return [edge // 2, edge // 4, edge // 8, edge // 8]


def blur_rows(difference, tables, blur, reach, count, halves, t):
    start = pl.multiple_of(t * LANE, LANE)
    got = jnp.dot(
        difference[: halves * reach, pl.ds(start, WIN)], tables[...], preferred_element_type=F32
    ).astype(BF16)
    for h in range(halves):
        for k in range(count):
            blur[h, k * reach : (k + 1) * reach, pl.ds(start, LANE)] = got[
                h * reach : (h + 1) * reach, k * LANE : (k + 1) * LANE
            ]


def exchange_kernel(
    n_patch, n_visit,
    live, patch_in, slot_in, coeffs_in, basis_rows_in, basis_cols_in, psf_rows_in, psf_cols_in, blocks, template,
    filtered, last_difference, psf_column_tables, last_table,
    patch, slot, coeffs, basis_rows, basis_cols, psf_rows, psf_cols, small_sems, sources, staged, raw, outgoing, arrived, labels_out, labels_in, masks, whole, total, shifted, column_tables, row_tables, smooth, blur, part_difference, *rest,
):
    sizes = cuts(blocks.shape[1])
    reaches = sorted(set(sizes[:-1]) - {sizes[-1]})
    tables_of = dict(zip(reaches, rest[: len(reaches)]))
    tables_of[sizes[-1]] = last_table
    load_sem, own_sem, block_send, block_recv, label_send, label_recv, rows_send, rows_recv, told = rest[len(reaches) :]
    me = lax.axis_index("patch")
    my_visit = lax.axis_index("visit")
    local_rows, breadth = template.shape
    height = local_rows * n_visit
    entries, edge = blocks.shape[:2]
    places = n_patch * CAP
    count = basis_rows.shape[0]
    psf_count = psf_rows.shape[1]
    wide = breadth // edge
    halves = height // edge
    slots = halves * wide
    chips = n_patch // 2
    chip, core = me // 2, lax.rem(me, 2)
    sibling = 2 * chip + 1 - core
    starts = [sum(sizes[:c]) for c in range(len(sizes))]
    visits = [lax.rem(my_visit + hop, n_visit) for hop in range(1, n_visit)]

    def tell(semaphore, peer):
        pl.semaphore_signal(semaphore, inc=1, device_id={"patch": peer}, device_id_type=pl.DeviceIdType.MESH)

    small = [
        pltpu.make_async_copy(source, held, small_sems.at[i])
        for i, (source, held) in enumerate(
            (
                (patch_in, patch), (slot_in, slot), (coeffs_in, coeffs),
                (basis_rows_in, basis_rows), (basis_cols_in, basis_cols),
                (psf_rows_in, psf_rows), (psf_cols_in, psf_cols),
            )
        )
    ]
    staged_entry = chips == 4
    near_side = chip < chips // 2
    middle = (chip == chips // 2) | (chip == chips // 2 - 1)
    inner = jnp.where(near_side, chip + 1, chip - 1)
    outer = jnp.where(near_side, chip - 1, chip + 1)
    other = jnp.where(near_side, chip + 2, chip - 2)
    mirror = chips - 1 - chip
    barrier = pltpu.get_barrier_semaphore()
    if staged_entry:
        tell(barrier, sibling)

        @pl.when(middle)
        def _():
            for c in range(2):
                tell(barrier, 2 * inner + c)
                tell(barrier, 2 * outer + c)

        line_signals = 3
    else:
        for hop in range(1, n_patch):
            tell(barrier, lax.rem(me + hop, n_patch))
        line_signals = n_patch - 1
    for visit in visits:
        pl.semaphore_signal(barrier, inc=1, device_id={"visit": visit}, device_id_type=pl.DeviceIdType.MESH)
    for copy in small:
        copy.start()
    load = pltpu.make_async_copy(blocks, raw, load_sem)
    load.start()
    my_rows = pl.ds(pl.multiple_of(my_visit * local_rows, local_rows), local_rows)
    own = pltpu.make_async_copy(template, whole.at[my_rows], own_sem)
    own.start()

    for copy in small[:2]:
        copy.wait()
    targets = [patch[i] for i in range(entries)]
    place_of = []
    for i in range(entries):
        earlier = jnp.int32(0)
        for before in range(i):
            earlier = earlier + jnp.where(targets[before] == targets[i], 1, 0)
        place_of.append(targets[i] * CAP + earlier)
    marks = [jnp.where(i < live[0, 0], slot[i] + 1, 0) for i in range(entries)]

    def find(d, carry):
        for c in range(CAP):
            source = jnp.int32(0)
            label = jnp.int32(-1)
            for i in range(entries):
                source = source + jnp.where(place_of[i] == d * CAP + c, i, 0)
                label = label + jnp.where(place_of[i] == d * CAP + c, marks[i], 0)
            sources[d * CAP + c] = source
            labels_out[d, c : c + 1, :] = jnp.full((1, LANE), label, jnp.int32)
        return carry

    lax.fori_loop(0, n_patch, find, 0)
    load.wait()

    def rows_of(c, place, number=1):
        return pl.ds(pl.multiple_of(places * starts[c] + place * sizes[c], 2 * EDGE), number * sizes[c])

    for c in range(len(sizes)):

        def pack(d, carry, c=c):
            outgoing[rows_of(c, d), :] = raw[sources[d], starts[c] : starts[c] + sizes[c], :]
            return carry

        lax.fori_loop(0, places, pack, 0)
    pl.semaphore_wait(barrier, line_signals + n_visit - 1)

    row_copies = [
        pltpu.make_async_remote_copy(
            src_ref=template, dst_ref=whole.at[my_rows],
            send_sem=rows_send.at[hop], recv_sem=rows_recv.at[my_visit],
            device_id={"visit": visit}, device_id_type=pl.DeviceIdType.MESH,
        )
        for hop, visit in enumerate(visits)
    ]

    def label_copy(peer):
        return pltpu.make_async_remote_copy(
            src_ref=labels_out.at[peer], dst_ref=labels_in.at[me],
            send_sem=label_send.at[peer], recv_sem=label_recv.at[me],
            device_id={"patch": peer}, device_id_type=pl.DeviceIdType.MESH,
        )

    def block_copy(peer, c):
        return pltpu.make_async_remote_copy(
            src_ref=outgoing.at[rows_of(c, peer * CAP, CAP)], dst_ref=arrived.at[rows_of(c, me * CAP, CAP)],
            send_sem=block_send.at[peer, c], recv_sem=block_recv.at[me, c],
            device_id={"patch": peer}, device_id_type=pl.DeviceIdType.MESH,
        )

    def send(peer, c):
        if c == 0:
            label_copy(peer).start()
        block_copy(peer, c).start()

    def send_chip(there, c):
        send(2 * there + core, c)
        send(2 * there + 1 - core, c)

    if staged_entry:

        @pl.when(middle)
        def _():
            send_chip(inner, 0)
            for copy in row_copies:
                copy.start()
            pl.semaphore_wait(told.at[0], 2)
            tell(told.at[1], 2 * outer + core)
            tell(told.at[1], 2 * inner + core)
            pl.semaphore_wait(told.at[1], 1)
            tell(told.at[2], 2 * outer + core)
            for c in range(len(sizes)):
                send_chip(other, c)
                if c:
                    send_chip(inner, c)
                send_chip(outer, c)
                send(sibling, c)

        @pl.when(jnp.logical_not(middle))
        def _():
            for c in range(2):
                tell(told.at[0], 2 * inner + c)
            for copy in row_copies:
                copy.start()
            pl.semaphore_wait(told.at[1], 1)
            send_chip(other, 0)
            pl.semaphore_wait(told.at[2], 1)
            for c in range(len(sizes)):
                send_chip(mirror, c)
                if c:
                    send_chip(other, c)
                send_chip(inner, c)
                send(sibling, c)

    else:
        turn = jnp.where(near_side, 1, -1)
        for copy in row_copies:
            copy.start()
        for c in range(len(sizes)):
            for hop in range(chips - 1, 0, -1):
                send_chip(lax.rem(chip + turn * hop + chips, chips), c)
            send(sibling, c)
    peers = [lax.rem(me + hop, n_patch) for hop in range(1, n_patch)]

    labels_in[me] = labels_out[me]
    for c in range(len(sizes)):
        arrived[rows_of(c, me * CAP, CAP), :] = outgoing[rows_of(c, me * CAP, CAP), :]
    for copy in small[2:]:
        copy.wait()
    scaled = jnp.concatenate(
        [(coeffs[0, k] * basis_cols[k : k + 1, :]).astype(BF16).astype(F32) for k in range(count)], axis=0
    )
    build_tables(basis_rows[...].astype(F32), scaled, column_tables, row_tables, staged)
    build_tables(psf_rows[0].astype(F32), psf_cols[0].astype(F32), psf_column_tables, tables_of, staged)
    clear_edges(smooth, count, height)

    def clear(r, carry):
        filtered[pl.ds(pl.multiple_of(r * EDGE, EDGE), EDGE), :] = jnp.zeros((EDGE, breadth), F32)
        return carry

    lax.fori_loop(0, height // EDGE + 2, clear, 0)
    own.wait()
    for visit in visits:
        rows = pl.ds(pl.multiple_of(visit * local_rows, local_rows), local_rows)
        pltpu.make_async_copy(whole.at[rows], whole.at[rows], rows_recv.at[visit]).wait()
    shift_into(
        lambda rows, t: whole[rows, t * LANE : (t + 1) * LANE].astype(F32),
        shifted, height, breadth // LANE, 32,
    )

    def per_pair(pair, carry):
        columns_pass(shifted, column_tables, smooth, pair, count, height)

        def per_row(r, inside):
            rows = pl.ds(pl.multiple_of(r * LANE, LANE), LANE)
            columns = pl.ds(pl.multiple_of(pair * WIN, WIN), WIN)
            total[rows, columns] = -rows_pass(smooth, row_tables, count, r)
            return inside

        return lax.fori_loop(0, height // LANE, per_row, carry)

    lax.fori_loop(0, breadth // WIN, per_pair, 0)

    for peer in peers:
        pltpu.make_async_copy(labels_in.at[peer], labels_in.at[peer], label_recv.at[peer]).wait()
    for place in range(places):
        mark = jnp.broadcast_to(labels_in[place // CAP, place % CAP : place % CAP + 1, :], (8, LANE))
        for s in range(slots):
            masks[s * places + place] = jnp.where(mark == s, 1.0, 0.0)

    for c, reach in enumerate(sizes):
        for peer in peers:
            rows = rows_of(c, peer * CAP, CAP)
            pltpu.make_async_copy(arrived.at[rows], arrived.at[rows], block_recv.at[peer, c]).wait()

        def add(r, carry, c=c):
            for lane in range(0, edge, LANE):
                for first in range(0, places, 16):
                    taken = range(first, min(first + 16, places))
                    pieces = [
                        arrived[
                            pl.ds(pl.multiple_of(places * starts[c] + p * sizes[c] + r * EDGE, EDGE), EDGE),
                            lane : lane + LANE,
                        ].astype(F32).reshape(EDGE // 8, 8, LANE)
                        for p in taken
                    ]
                    for s in range(slots):
                        rows = pl.ds(pl.multiple_of(s // wide * edge + starts[c] + r * EDGE, EDGE), EDGE)
                        columns = slice(s % wide * edge + lane, s % wide * edge + lane + LANE)
                        value = total[rows, columns].reshape(EDGE // 8, 8, LANE)
                        for p, piece in zip(taken, pieces):
                            value = value + masks[s * places + p][None] * piece
                        total[rows, columns] = value.reshape(EDGE, LANE)
            return carry

        lax.fori_loop(0, reach // EDGE, add, 0)
        last = c == len(sizes) - 1
        held = last_difference if last else part_difference

        def shift(r, carry, c=c, held=held):
            lane = lax.broadcasted_iota(jnp.int32, (EDGE, LANE), 1)
            for h in range(halves):
                source = pl.ds(pl.multiple_of(h * edge + starts[c] + r * EDGE, EDGE), EDGE)
                rows = pl.ds(pl.multiple_of(h * sizes[c] + r * EDGE, EDGE), EDGE)
                before = jnp.zeros((EDGE, LANE), F32)
                for t in range(breadth // LANE):
                    rolled = pltpu.roll(total[source, t * LANE : (t + 1) * LANE], HALF, 1)
                    held[rows, t * LANE : (t + 1) * LANE] = jnp.where(lane < HALF, before, rolled).astype(BF16)
                    before = rolled
                held[rows, breadth:] = jnp.where(lane < HALF, before, 0.0).astype(BF16)
            return carry

        lax.fori_loop(0, reach // EDGE, shift, 0)
        if last:
            continue

        def blur_tile(t, carry, reach=reach):
            blur_rows(part_difference, psf_column_tables, blur, reach, psf_count, halves, t)
            return carry

        lax.fori_loop(0, breadth // LANE, blur_tile, 0)

        def gather(t, carry, c=c, reach=reach):
            columns = pl.ds(pl.multiple_of(t * WIN, WIN), WIN)
            for h in range(halves):
                rows = slice(h * edge + starts[c], h * edge + starts[c] + reach + 2 * EDGE)
                filtered[rows, columns] += jnp.dot(
                    tables_of[reach][...], blur[h, : psf_count * reach, columns], preferred_element_type=F32
                )
            return carry

        lax.fori_loop(0, breadth // WIN, gather, 0)

    for copy in row_copies:
        copy.wait_send()
    for peer in peers:
        label_copy(peer).wait_send()
        for c in range(len(sizes)):
            block_copy(peer, c).wait_send()


def finish_kernel(edge, filtered, difference, column_tables, table, out, blur, ends, sems):
    height, breadth = out.shape
    halves = height // edge
    psf_count = column_tables.shape[1] // LANE
    reach = difference.shape[0] // halves
    copies = []

    def put(source, first, rows):
        copies.append(pltpu.make_async_copy(source, out.at[pl.ds(first, rows)], sems.at[len(copies)]))
        copies[-1].start()

    done = 0
    for h in range(halves):
        upto = (h + 1) * edge - reach - EDGE
        put(filtered.at[pl.ds(EDGE + done, upto - done)], done, upto - done)
        done = upto + reach + 2 * EDGE
    for t in range(breadth // LANE):
        blur_rows(difference, column_tables, blur, reach, psf_count, halves, t)
    for h in range(halves):
        first = (h + 1) * edge - reach
        for t in range(breadth // WIN):
            columns = slice(t * WIN, (t + 1) * WIN)
            ends[h, :, columns] = filtered[first : first + reach + 2 * EDGE, columns] + jnp.dot(
                table[...], blur[h, :, columns], preferred_element_type=F32
            )
        rows = reach + 2 * EDGE if h < halves - 1 else reach + EDGE
        put(ends.at[h, pl.ds(0, rows)], first - EDGE, rows)
    for copy in copies:
        copy.wait()


SMEM = pl.BlockSpec(memory_space=pltpu.SMEM)
HBM = pl.BlockSpec(memory_space=pltpu.HBM)
VMEM = pl.BlockSpec(memory_space=pltpu.VMEM)


def stencil_scratch(count, height, breadth):
    return [
        pltpu.VMEM((height, breadth + LANE), BF16),
        pltpu.VMEM((WIN, count * LANE), BF16),
        pltpu.VMEM((count, LANE, WIN), BF16),
        pltpu.VMEM((count, height + 2 * HALF, WIN), BF16),
    ]


def per_device(blocks, block_patch, block_slot, block_count, template, basis_rows, basis_cols, coeffs, psf_rows, psf_cols):
    n_patch = lax.axis_size("patch")
    n_visit = lax.axis_size("visit")
    local_rows, breadth = template.shape[1:]
    height = local_rows * n_visit
    entries, edge = blocks.shape[2:4]
    halves = height // edge
    slots = halves * (breadth // edge)
    places = n_patch * CAP
    count = basis_rows.shape[0]
    psf_count = psf_rows.shape[1]
    sizes = cuts(edge)
    reaches = sorted(set(sizes[:-1]) - {sizes[-1]})
    most = max(sizes)
    final = sizes[-1]
    dma = pltpu.SemaphoreType.DMA
    handed = pl.pallas_call(
        functools.partial(exchange_kernel, n_patch, n_visit),
        out_shape=(
            jax.ShapeDtypeStruct((height + 2 * EDGE, breadth), F32),
            jax.ShapeDtypeStruct((halves * final, breadth + LANE), BF16),
            jax.ShapeDtypeStruct((WIN, psf_count * LANE), BF16),
            jax.ShapeDtypeStruct((final + 2 * EDGE, psf_count * final), BF16),
        ),
        in_specs=[SMEM] + [HBM] * 9,
        out_specs=(VMEM,) * 4,
        scratch_shapes=[
            pltpu.SMEM((entries,), jnp.int32),
            pltpu.SMEM((entries,), jnp.int32),
            pltpu.SMEM(coeffs.shape, F32),
            pltpu.VMEM(basis_rows.shape, BF16),
            pltpu.VMEM(basis_cols.shape, F32),
            pltpu.VMEM(psf_rows.shape, BF16),
            pltpu.VMEM(psf_cols.shape, BF16),
            dma((7,)),
            pltpu.SMEM((places,), jnp.int32),
            pltpu.VMEM((pl.cdiv(max(count, psf_count), 8) * 8, WIN), F32),
            pltpu.VMEM((entries, edge, edge), BF16),
            pltpu.VMEM((places * edge, edge), BF16),
            pltpu.VMEM((places * edge, edge), BF16),
            pltpu.VMEM((n_patch, CAP, LANE), jnp.int32),
            pltpu.VMEM((n_patch, CAP, LANE), jnp.int32),
            pltpu.VMEM((slots * places, 8, LANE), F32),
            pltpu.VMEM((height, breadth), BF16),
            pltpu.VMEM((height, breadth), F32),
        ]
        + stencil_scratch(count, height, breadth)
        + [
            pltpu.VMEM((halves, psf_count * most, breadth), BF16),
            pltpu.VMEM((halves * most, breadth + LANE), BF16),
        ]
        + [pltpu.VMEM((reach + 2 * EDGE, psf_count * reach), BF16) for reach in reaches]
        + [
            dma(()),
            dma(()),
            dma((n_patch, len(sizes))),
            dma((n_patch, len(sizes))),
            dma((n_patch,)),
            dma((n_patch,)),
            dma((n_visit - 1,)),
            dma((n_visit,)),
            pltpu.SemaphoreType.REGULAR((3,)),
        ],
        compiler_params=pltpu.CompilerParams(
            collective_id=0, has_side_effects=True, vmem_limit_bytes=VMEM_LIMIT
        ),
    )(
        block_count,
        *(
            pltpu.with_memory_space_constraint(value, pltpu.HBM)
            for value in (
                block_patch.reshape(entries), block_slot.reshape(entries), coeffs,
                basis_rows, basis_cols, psf_rows, psf_cols, blocks[0, 0], template[0],
            )
        )
    )
    filtered = pl.pallas_call(
        functools.partial(finish_kernel, edge),
        out_shape=jax.ShapeDtypeStruct((height, breadth), F32),
        in_specs=[VMEM] * 4,
        out_specs=HBM,
        scratch_shapes=[
            pltpu.VMEM((halves, psf_count * final, breadth), BF16),
            pltpu.VMEM((halves, final + 2 * EDGE, breadth), F32),
            dma((2 * halves,)),
        ],
        compiler_params=pltpu.CompilerParams(vmem_limit_bytes=16 * 1024 * 1024),
    )(*handed)
    return filtered[None, None]


def solution(mesh):
    return jax.shard_map(
        per_device,
        mesh=mesh,
        in_specs=(
            P("patch", "visit", None, None, None),
            P("patch", "visit", None, None),
            P("patch", "visit", None),
            P("patch", "visit"),
            P("patch", "visit", None),
            P(),
            P(),
            P("visit", None),
            P("visit", None, None),
            P("visit", None, None),
        ),
        out_specs=P("patch", "visit", None, None),
        check_vma=False,
    )
```

```python
import functools

import jax
import jax.numpy as jnp
from jax import lax
from jax.experimental import pallas as pl
from jax.experimental.pallas import tpu as pltpu
from jax.sharding import PartitionSpec as P

CAP = 2
MOST_ROWS = 512
LANE = 128
HALF = 64
EDGE = 16
WIN = 256
F32 = jnp.float32
BF16 = jnp.bfloat16
VMEM_LIMIT = 32 * 1024 * 1024


def toeplitz(row, half_len):
    wide = jnp.broadcast_to(row, (LANE, WIN))
    return pltpu.roll(wide, (HALF - half_len) // 8 * 8, 1, stride=1, stride_axis=0)


def spread(taps, staged):
    count, length = taps.shape
    staged[...] = jnp.zeros(staged.shape, F32)
    staged[:count, :length] = taps
    lead = (HALF - length // 2) % 8
    if lead:
        staged[...] = pltpu.roll(staged[...], lead, 1)


def shift_into(load_tile, shifted, height, tiles, step):
    def body(r, carry):
        rows = pl.ds(pl.multiple_of(r * step, step), step)
        lane = lax.broadcasted_iota(jnp.int32, (step, LANE), 1)
        before = jnp.zeros((step, LANE), F32)
        for t in range(tiles):
            rolled = pltpu.roll(load_tile(rows, t), HALF, 1)
            shifted[rows, t * LANE : (t + 1) * LANE] = jnp.where(lane < HALF, before, rolled).astype(BF16)
            before = rolled
        shifted[rows, tiles * LANE :] = jnp.where(lane < HALF, before, 0.0).astype(BF16)
        return carry

    lax.fori_loop(0, height // step, body, 0)


def columns_pass(shifted, tables, smooth, pair, count, height, margin=HALF):
    for side in range(2):
        start = pl.multiple_of((2 * pair + side) * LANE, LANE)
        window = shifted[:, pl.ds(start, WIN)]
        for group in range(0, count, 2):
            taken = min(2, count - group)
            got = jnp.dot(
                window, tables[:, group * LANE : (group + taken) * LANE], preferred_element_type=F32
            ).astype(BF16)
            for k in range(taken):
                smooth[group + k, margin : margin + height, side * LANE : (side + 1) * LANE] = got[
                    :, k * LANE : (k + 1) * LANE
                ]


def rows_pass(smooth, tables, count, r):
    start = pl.multiple_of(r * LANE, LANE)
    total = jnp.zeros((LANE, WIN), F32)
    for k in range(count):
        total = total + jnp.dot(tables[k], smooth[k, pl.ds(start, WIN), :], preferred_element_type=F32)
    return total


def spread_table(staged, half_len, reach, count):
    wide_rows = reach + 2 * EDGE
    lane = lax.broadcasted_iota(jnp.int32, (wide_rows, WIN), 1)
    joined = jnp.zeros((wide_rows, WIN), F32)
    for k in range(count):
        shift = (k * reach - EDGE - half_len - (HALF - half_len) % 8) % WIN
        wide = jnp.broadcast_to(staged[k : k + 1, :], (wide_rows, WIN))
        rolled = pltpu.roll(wide, shift, 1, stride=1, stride_axis=0)
        joined = jnp.where((lane >= k * reach) & (lane < (k + 1) * reach), rolled, joined)
    return joined[:, : count * reach].astype(BF16)


def build_tables(column_taps, row_taps, column_tables, row_tables, staged):
    spread(column_taps, staged)
    for k in range(column_taps.shape[0]):
        table = toeplitz(staged[k : k + 1, :], column_taps.shape[1] // 2)
        column_tables[:, k * LANE : (k + 1) * LANE] = table.T.astype(BF16)
    spread(row_taps, staged)
    half_len = row_taps.shape[1] // 2
    if isinstance(row_tables, dict):
        for reach, table in row_tables.items():
            table[...] = spread_table(staged, half_len, reach, row_taps.shape[0])
    else:
        for k in range(row_taps.shape[0]):
            row_tables[k] = toeplitz(staged[k : k + 1, :], half_len).astype(BF16)


def clear_edges(smooth, count, height):
    for k in range(count):
        smooth[k, :HALF, :] = jnp.zeros((HALF, smooth.shape[2]), BF16)
        smooth[k, HALF + height :, :] = jnp.zeros((HALF, smooth.shape[2]), BF16)


def cuts(edge):
    return [edge // 2, edge // 4, edge // 4]


def blur_rows(difference, tables, blur, reach, count, halves, tiles):
    high = halves * reach
    group = max(1, min(tiles, MOST_ROWS // high))

    def some(g, carry):
        begin = [pl.multiple_of((g * group + n) * LANE, LANE) for n in range(group)]
        windows = jnp.concatenate([difference[:high, pl.ds(start, WIN)] for start in begin], axis=0)
        got = jnp.dot(windows, tables[...], preferred_element_type=F32).astype(BF16)
        for n, start in enumerate(begin):
            for h in range(halves):
                rows = slice(n * high + h * reach, n * high + (h + 1) * reach)
                for k in range(count):
                    blur[h, k * reach : (k + 1) * reach, pl.ds(start, LANE)] = got[rows, k * LANE : (k + 1) * LANE]
        return carry

    lax.fori_loop(0, tiles // group, some, 0, unroll=high < LANE)


def exchange_kernel(
    n_patch, n_visit,
    live_in, patch_in, slot_in, coeffs_in, basis_rows_in, basis_cols_in, psf_rows_in, psf_cols_in, blocks, template,
    filtered, last_difference, psf_column_tables, last_table,
    live, patch, slot, coeffs, basis_rows, basis_cols, psf_rows, psf_cols, small_sems, sources, staged, outgoing, arrived, labels_out, labels_in, picks, whole, total, shifted, column_tables, row_tables, smooth, blur, part_difference, *rest,
):
    sizes = cuts(blocks.shape[1])
    reaches = sorted(set(sizes[:-1]) - {sizes[-1]})
    tables_of = dict(zip(reaches, rest[: len(reaches)]))
    tables_of[sizes[-1]] = last_table
    raw = rest[len(reaches) : len(reaches) + len(sizes)]
    load_sem, own_sem, block_send, block_recv, label_send, label_recv, rows_send, rows_recv, told = rest[
        len(reaches) + len(sizes) :
    ]
    me = lax.axis_index("patch")
    my_visit = lax.axis_index("visit")
    local_rows, breadth = template.shape
    height = local_rows * n_visit
    entries, edge = blocks.shape[:2]
    places = n_patch * CAP
    count = basis_rows.shape[0]
    psf_count = psf_rows.shape[1]
    wide = breadth // edge
    halves = height // edge
    slots = halves * wide
    chips = n_patch // 2
    chip, core = me // 2, lax.rem(me, 2)
    sibling = 2 * chip + 1 - core
    starts = [sum(sizes[:c]) for c in range(len(sizes))]
    visits = [lax.rem(my_visit + hop, n_visit) for hop in range(1, n_visit)]

    def tell(semaphore, peer):
        pl.semaphore_signal(semaphore, inc=1, device_id={"patch": peer}, device_id_type=pl.DeviceIdType.MESH)

    small = [
        pltpu.make_async_copy(source, held, small_sems.at[i])
        for i, (source, held) in enumerate(
            (
                (live_in, live), (patch_in, patch), (slot_in, slot), (coeffs_in, coeffs),
                (basis_rows_in, basis_rows), (basis_cols_in, basis_cols),
                (psf_rows_in, psf_rows), (psf_cols_in, psf_cols),
            )
        )
    ]
    staged_entry = chips == 4
    near_side = chip < chips // 2
    middle = (chip == chips // 2) | (chip == chips // 2 - 1)
    inner = jnp.where(near_side, chip + 1, chip - 1)
    outer = jnp.where(near_side, chip - 1, chip + 1)
    other = jnp.where(near_side, chip + 2, chip - 2)
    mirror = chips - 1 - chip
    barrier = pltpu.get_barrier_semaphore()
    if staged_entry:
        tell(barrier, sibling)

        @pl.when(middle)
        def _():
            for c in range(2):
                tell(barrier, 2 * inner + c)
                tell(barrier, 2 * outer + c)

        line_signals = 3
    else:
        for hop in range(1, n_patch):
            tell(barrier, lax.rem(me + hop, n_patch))
        line_signals = n_patch - 1
    for visit in visits:
        pl.semaphore_signal(barrier, inc=1, device_id={"visit": visit}, device_id_type=pl.DeviceIdType.MESH)
    for copy in small:
        copy.start()
    loads = [
        pltpu.make_async_copy(blocks.at[:, pl.ds(starts[c], sizes[c])], raw[c], load_sem.at[c])
        for c in range(len(sizes))
    ]
    for load in loads:
        load.start()
    my_rows = pl.ds(pl.multiple_of(my_visit * local_rows, local_rows), local_rows)
    own = pltpu.make_async_copy(template, whole.at[my_rows], own_sem)
    own.start()

    for copy in small[:3]:
        copy.wait()
    targets = [patch[i] for i in range(entries)]
    place_of = []
    for i in range(entries):
        earlier = jnp.int32(0)
        for before in range(i):
            earlier = earlier + jnp.where(targets[before] == targets[i], 1, 0)
        place_of.append(targets[i] * CAP + earlier)
    marks = [jnp.where(i < live[0, 0], slot[i] + 1, 0) for i in range(entries)]

    def find(d, carry):
        for c in range(CAP):
            source = jnp.int32(0)
            label = jnp.int32(-1)
            for i in range(entries):
                source = source + jnp.where(place_of[i] == d * CAP + c, i, 0)
                label = label + jnp.where(place_of[i] == d * CAP + c, marks[i], 0)
            sources[d * CAP + c] = source
            labels_out[d, c : c + 1, :] = jnp.full((1, LANE), label, jnp.int32)
        return carry

    def rows_of(c, place, number=1):
        return pl.ds(pl.multiple_of(places * starts[c] + place * sizes[c], EDGE), number * sizes[c])

    def pack(c, first, number):
        def one(i, carry):
            outgoing[rows_of(c, first + i), :] = raw[c][sources[first + i]]
            return carry

        lax.fori_loop(0, number, one, 0)

    if staged_entry:
        turns = [
            jnp.where(middle, inner, other), jnp.where(middle, other, mirror), jnp.where(middle, outer, inner), chip,
        ]
    else:
        turns = [lax.rem(chip + hop, chips) for hop in range(chips - 1, -1, -1)]
    lax.fori_loop(2 * turns[0], 2 * turns[0] + 2, find, 0)
    loads[0].wait()
    pack(0, 2 * turns[0] * CAP, 2 * CAP)
    pl.semaphore_wait(barrier, line_signals + n_visit - 1)

    row_copies = [
        pltpu.make_async_remote_copy(
            src_ref=template, dst_ref=whole.at[my_rows],
            send_sem=rows_send.at[hop], recv_sem=rows_recv.at[my_visit],
            device_id={"visit": visit}, device_id_type=pl.DeviceIdType.MESH,
        )
        for hop, visit in enumerate(visits)
    ]

    def label_copy(peer):
        return pltpu.make_async_remote_copy(
            src_ref=labels_out.at[peer], dst_ref=labels_in.at[me],
            send_sem=label_send.at[peer], recv_sem=label_recv.at[me],
            device_id={"patch": peer}, device_id_type=pl.DeviceIdType.MESH,
        )

    def block_copy(peer, c):
        return pltpu.make_async_remote_copy(
            src_ref=outgoing.at[rows_of(c, peer * CAP, CAP)], dst_ref=arrived.at[rows_of(c, me * CAP, CAP)],
            send_sem=block_send.at[peer, c], recv_sem=block_recv.at[me, c],
            device_id={"patch": peer}, device_id_type=pl.DeviceIdType.MESH,
        )

    def send(peer, c):
        if c == 0:
            label_copy(peer).start()
        block_copy(peer, c).start()

    def send_chip(there, c):
        send(2 * there + core, c)
        send(2 * there + 1 - core, c)

    early, late = range(len(sizes) - 2), range(len(sizes) - 2, len(sizes))

    def pack_rest():
        for turn in turns[1:]:
            lax.fori_loop(2 * turn, 2 * turn + 2, find, 0)
            pack(0, 2 * turn * CAP, 2 * CAP)
        for c in range(1, len(sizes)):
            loads[c].wait()
            pack(c, 0, places)

    if staged_entry:

        @pl.when(middle)
        def _():
            send_chip(inner, 0)
            for copy in row_copies:
                copy.start()

        @pl.when(jnp.logical_not(middle))
        def _():
            for c in range(2):
                tell(told.at[0], 2 * inner + c)
            for copy in row_copies:
                copy.start()

        @pl.when(middle)
        def _():
            pl.semaphore_wait(told.at[0], 2)
            tell(told.at[1], 2 * outer + core)
            tell(told.at[1], 2 * inner + core)

        pack_rest()

        @pl.when(middle)
        def _():
            pl.semaphore_wait(told.at[1], 1)
            tell(told.at[2], 2 * outer + core)
            for steps in early, late:
                for c in steps:
                    send_chip(other, c)
                    send_chip(outer, c)
                    send(sibling, c)
                    if c and steps is early:
                        send_chip(inner, c)
            for c in late:
                send_chip(inner, c)

        @pl.when(jnp.logical_not(middle))
        def _():
            pl.semaphore_wait(told.at[1], 1)
            send_chip(other, 0)
            pl.semaphore_wait(told.at[2], 1)
            for steps in early, late:
                for c in steps:
                    send_chip(mirror, c)
                    if steps is early:
                        if c:
                            send_chip(other, c)
                        send_chip(inner, c)
                    send(sibling, c)
            for c in late:
                send_chip(other, c)
                send_chip(inner, c)

    else:
        for copy in row_copies:
            copy.start()
        for turn in turns[:1]:
            send_chip(turn, 0)
        pack_rest()
        for c in range(len(sizes)):
            for turn in turns[(1 if c == 0 else 0) : -1]:
                send_chip(turn, c)
            send(sibling, c)
    peers = [lax.rem(me + hop, n_patch) for hop in range(1, n_patch)]

    labels_in[me] = labels_out[me]
    for c in range(len(sizes)):
        arrived[rows_of(c, me * CAP, CAP), :] = outgoing[rows_of(c, me * CAP, CAP), :]
    for copy in small[3:]:
        copy.wait()
    scaled = jnp.concatenate(
        [(coeffs[0, k] * basis_cols[k : k + 1, :]).astype(BF16).astype(F32) for k in range(count)], axis=0
    )
    build_tables(basis_rows[...].astype(F32), scaled, column_tables, row_tables, staged)
    build_tables(psf_rows[0].astype(F32), psf_cols[0].astype(F32), psf_column_tables, tables_of, staged)
    clear_edges(smooth, count, height)

    def clear(r, carry):
        filtered[pl.ds(pl.multiple_of(r * EDGE, EDGE), EDGE), :] = jnp.zeros((EDGE, breadth), F32)
        return carry

    lax.fori_loop(0, height // EDGE + 2, clear, 0)
    own.wait()
    for visit in visits:
        rows = pl.ds(pl.multiple_of(visit * local_rows, local_rows), local_rows)
        pltpu.make_async_copy(whole.at[rows], whole.at[rows], rows_recv.at[visit]).wait()
    shift_into(
        lambda rows, t: whole[rows, t * LANE : (t + 1) * LANE].astype(F32),
        shifted, height, breadth // LANE, 32,
    )

    def per_pair(pair, carry):
        columns_pass(shifted, column_tables, smooth, pair, count, height)

        def per_row(r, inside):
            rows = pl.ds(pl.multiple_of(r * LANE, LANE), LANE)
            columns = pl.ds(pl.multiple_of(pair * WIN, WIN), WIN)
            total[rows, columns] = -rows_pass(smooth, row_tables, count, r)
            return inside

        return lax.fori_loop(0, height // LANE, per_row, carry)

    lax.fori_loop(0, breadth // WIN, per_pair, 0)

    for peer in peers:
        pltpu.make_async_copy(labels_in.at[peer], labels_in.at[peer], label_recv.at[peer]).wait()
    for first in range(0, places, LANE // EDGE):
        lane = lax.broadcasted_iota(jnp.int32, (8, LANE), 1)
        named = jnp.full((8, LANE), -1, jnp.int32)
        for p in range(LANE // EDGE):
            place = first + p
            mark = jnp.broadcast_to(labels_in[place // CAP, place % CAP : place % CAP + 1, :], (8, LANE))
            named = jnp.where((lane >= p * EDGE) & (lane < (p + 1) * EDGE), mark, named)
        named = jnp.concatenate([named] * (EDGE // 8), axis=0)
        lane = lax.broadcasted_iota(jnp.int32, (EDGE, LANE), 1)
        same = lax.rem(lane, EDGE) == lax.broadcasted_iota(jnp.int32, (EDGE, LANE), 0)
        for s in range(slots):
            picks[s * EDGE : (s + 1) * EDGE, first * EDGE : first * EDGE + LANE] = jnp.where(
                same & (named == s), 1.0, 0.0
            ).astype(BF16)

    for c, reach in enumerate(sizes):
        if c == len(sizes) - 1:
            for copy in row_copies:
                copy.wait_send()
            for peer in peers:
                label_copy(peer).wait_send()
                for before in range(c):
                    block_copy(peer, before).wait_send()
        for peer in peers:
            rows = rows_of(c, peer * CAP, CAP)
            pltpu.make_async_copy(arrived.at[rows], arrived.at[rows], block_recv.at[peer, c]).wait()

        def add(r, carry, c=c):
            pieces = jnp.concatenate(
                [
                    arrived[pl.ds(pl.multiple_of(places * starts[c] + p * sizes[c] + r * EDGE, EDGE), EDGE), :]
                    for p in range(places)
                ],
                axis=0,
            )
            summed = jnp.dot(picks[...], pieces, preferred_element_type=F32)
            for s in range(slots):
                rows = pl.ds(pl.multiple_of(s // wide * edge + starts[c] + r * EDGE, EDGE), EDGE)
                columns = slice(s % wide * edge, (s % wide + 1) * edge)
                total[rows, columns] += summed[s * EDGE : (s + 1) * EDGE]
            return carry

        lax.fori_loop(0, reach // EDGE, add, 0, unroll=reach < LANE)
        last = c == len(sizes) - 1
        held = last_difference if last else part_difference

        def shift(r, carry, c=c, held=held):
            lane = lax.broadcasted_iota(jnp.int32, (EDGE, LANE), 1)
            for h in range(halves):
                source = pl.ds(pl.multiple_of(h * edge + starts[c] + r * EDGE, EDGE), EDGE)
                rows = pl.ds(pl.multiple_of(h * sizes[c] + r * EDGE, EDGE), EDGE)
                before = jnp.zeros((EDGE, LANE), F32)
                for t in range(breadth // LANE):
                    rolled = pltpu.roll(total[source, t * LANE : (t + 1) * LANE], HALF, 1)
                    held[rows, t * LANE : (t + 1) * LANE] = jnp.where(lane < HALF, before, rolled).astype(BF16)
                    before = rolled
                held[rows, breadth:] = jnp.where(lane < HALF, before, 0.0).astype(BF16)
            return carry

        lax.fori_loop(0, reach // EDGE, shift, 0, unroll=reach < LANE)
        if last:
            continue

        blur_rows(part_difference, psf_column_tables, blur, reach, psf_count, halves, breadth // LANE)

        def gather(t, carry, c=c, reach=reach):
            columns = pl.ds(pl.multiple_of(t * WIN, WIN), WIN)
            for h in range(halves):
                rows = slice(h * edge + starts[c], h * edge + starts[c] + reach + 2 * EDGE)
                filtered[rows, columns] += jnp.dot(
                    tables_of[reach][...], blur[h, : psf_count * reach, columns], preferred_element_type=F32
                )
            return carry

        lax.fori_loop(0, breadth // WIN, gather, 0, unroll=halves * reach <= LANE)

    for peer in peers:
        block_copy(peer, len(sizes) - 1).wait_send()


def finish_kernel(edge, filtered, difference, column_tables, table, out, blur, ends, sems):
    height, breadth = out.shape
    halves = height // edge
    psf_count = column_tables.shape[1] // LANE
    reach = difference.shape[0] // halves
    copies = []

    def put(source, first, rows):
        copies.append(pltpu.make_async_copy(source, out.at[pl.ds(first, rows)], sems.at[len(copies)]))
        copies[-1].start()

    done = 0
    for h in range(halves):
        upto = (h + 1) * edge - reach - EDGE
        put(filtered.at[pl.ds(EDGE + done, upto - done)], done, upto - done)
        done = upto + reach + 2 * EDGE
    blur_rows(difference, column_tables, blur, reach, psf_count, halves, breadth // LANE)
    for h in range(halves):
        first = (h + 1) * edge - reach
        for t in range(breadth // WIN):
            columns = slice(t * WIN, (t + 1) * WIN)
            ends[h, :, columns] = filtered[first : first + reach + 2 * EDGE, columns] + jnp.dot(
                table[...], blur[h, :, columns], preferred_element_type=F32
            )
        rows = reach + 2 * EDGE if h < halves - 1 else reach + EDGE
        put(ends.at[h, pl.ds(0, rows)], first - EDGE, rows)
    for copy in copies:
        copy.wait()


SMEM = pl.BlockSpec(memory_space=pltpu.SMEM)
HBM = pl.BlockSpec(memory_space=pltpu.HBM)
VMEM = pl.BlockSpec(memory_space=pltpu.VMEM)


def stencil_scratch(count, height, breadth):
    return [
        pltpu.VMEM((height, breadth + LANE), BF16),
        pltpu.VMEM((WIN, count * LANE), BF16),
        pltpu.VMEM((count, LANE, WIN), BF16),
        pltpu.VMEM((count, height + 2 * HALF, WIN), BF16),
    ]


def per_device(blocks, block_patch, block_slot, block_count, template, basis_rows, basis_cols, coeffs, psf_rows, psf_cols):
    n_patch = lax.axis_size("patch")
    n_visit = lax.axis_size("visit")
    local_rows, breadth = template.shape[1:]
    height = local_rows * n_visit
    entries, edge = blocks.shape[2:4]
    halves = height // edge
    slots = halves * (breadth // edge)
    places = n_patch * CAP
    count = basis_rows.shape[0]
    psf_count = psf_rows.shape[1]
    sizes = cuts(edge)
    reaches = sorted(set(sizes[:-1]) - {sizes[-1]})
    most = max(sizes)
    final = sizes[-1]
    dma = pltpu.SemaphoreType.DMA
    handed = pl.pallas_call(
        functools.partial(exchange_kernel, n_patch, n_visit),
        out_shape=(
            jax.ShapeDtypeStruct((height + 2 * EDGE, breadth), F32),
            jax.ShapeDtypeStruct((halves * final, breadth + LANE), BF16),
            jax.ShapeDtypeStruct((WIN, psf_count * LANE), BF16),
            jax.ShapeDtypeStruct((final + 2 * EDGE, psf_count * final), BF16),
        ),
        in_specs=[pl.BlockSpec(memory_space=pl.ANY)] + [HBM] * 9,
        out_specs=(VMEM,) * 4,
        scratch_shapes=[
            pltpu.SMEM((1, 1), jnp.int32),
            pltpu.SMEM((entries,), jnp.int32),
            pltpu.SMEM((entries,), jnp.int32),
            pltpu.SMEM(coeffs.shape, F32),
            pltpu.VMEM(basis_rows.shape, BF16),
            pltpu.VMEM(basis_cols.shape, F32),
            pltpu.VMEM(psf_rows.shape, BF16),
            pltpu.VMEM(psf_cols.shape, BF16),
            dma((8,)),
            pltpu.SMEM((places,), jnp.int32),
            pltpu.VMEM((pl.cdiv(max(count, psf_count), 8) * 8, WIN), F32),
            pltpu.VMEM((places * edge, edge), BF16),
            pltpu.VMEM((places * edge, edge), BF16),
            pltpu.VMEM((n_patch, CAP, LANE), jnp.int32),
            pltpu.VMEM((n_patch, CAP, LANE), jnp.int32),
            pltpu.VMEM((slots * EDGE, places * EDGE), BF16),
            pltpu.VMEM((height, breadth), BF16),
            pltpu.VMEM((height, breadth), F32),
        ]
        + stencil_scratch(count, height, breadth)
        + [
            pltpu.VMEM((halves, psf_count * most, breadth), BF16),
            pltpu.VMEM((halves * most, breadth + LANE), BF16),
        ]
        + [pltpu.VMEM((reach + 2 * EDGE, psf_count * reach), BF16) for reach in reaches]
        + [pltpu.VMEM((entries, size, edge), BF16) for size in sizes]
        + [
            dma((len(sizes),)),
            dma(()),
            dma((n_patch, len(sizes))),
            dma((n_patch, len(sizes))),
            dma((n_patch,)),
            dma((n_patch,)),
            dma((n_visit - 1,)),
            dma((n_visit,)),
            pltpu.SemaphoreType.REGULAR((3,)),
        ],
        compiler_params=pltpu.CompilerParams(
            collective_id=0, has_side_effects=True, vmem_limit_bytes=VMEM_LIMIT
        ),
    )(
        block_count,
        *(
            pltpu.with_memory_space_constraint(value, pltpu.HBM)
            for value in (
                block_patch.reshape(entries), block_slot.reshape(entries), coeffs,
                basis_rows, basis_cols, psf_rows, psf_cols, blocks[0, 0], template[0],
            )
        )
    )
    filtered = pl.pallas_call(
        functools.partial(finish_kernel, edge),
        out_shape=jax.ShapeDtypeStruct((height, breadth), F32),
        in_specs=[VMEM] * 4,
        out_specs=HBM,
        scratch_shapes=[
            pltpu.VMEM((halves, psf_count * final, breadth), BF16),
            pltpu.VMEM((halves, final + 2 * EDGE, breadth), F32),
            dma((2 * halves,)),
        ],
        compiler_params=pltpu.CompilerParams(vmem_limit_bytes=16 * 1024 * 1024),
    )(*handed)
    return filtered[None, None]


def solution(mesh):
    return jax.shard_map(
        per_device,
        mesh=mesh,
        in_specs=(
            P("patch", "visit", None, None, None),
            P("patch", "visit", None, None),
            P("patch", "visit", None),
            P("patch", "visit"),
            P("patch", "visit", None),
            P(),
            P(),
            P("visit", None),
            P("visit", None, None),
            P("visit", None, None),
        ),
        out_specs=P("patch", "visit", None, None),
        check_vma=False,
    )
```

```python
import functools

import jax
import jax.numpy as jnp
from jax import lax
from jax.experimental import pallas as pl
from jax.experimental.pallas import tpu as pltpu
from jax.sharding import PartitionSpec as P

CAP = 2
MOST_ROWS = 512
LANE = 128
HALF = 64
EDGE = 16
WIN = 256
F32 = jnp.float32
BF16 = jnp.bfloat16
VMEM_LIMIT = 32 * 1024 * 1024


def toeplitz(row, half_len):
    wide = jnp.broadcast_to(row, (LANE, WIN))
    return pltpu.roll(wide, (HALF - half_len) // 8 * 8, 1, stride=1, stride_axis=0)


def spread(taps, staged):
    count, length = taps.shape
    staged[...] = jnp.zeros(staged.shape, F32)
    staged[:count, :length] = taps
    lead = (HALF - length // 2) % 8
    if lead:
        staged[...] = pltpu.roll(staged[...], lead, 1)


def shift_into(load_tile, shifted, height, tiles, step):
    def body(r, carry):
        rows = pl.ds(pl.multiple_of(r * step, step), step)
        lane = lax.broadcasted_iota(jnp.int32, (step, LANE), 1)
        before = jnp.zeros((step, LANE), F32)
        for t in range(tiles):
            rolled = pltpu.roll(load_tile(rows, t), HALF, 1)
            shifted[rows, t * LANE : (t + 1) * LANE] = jnp.where(lane < HALF, before, rolled).astype(BF16)
            before = rolled
        shifted[rows, tiles * LANE :] = jnp.where(lane < HALF, before, 0.0).astype(BF16)
        return carry

    lax.fori_loop(0, height // step, body, 0)


def columns_pass(shifted, tables, smooth, pair, count, height, margin=HALF):
    for side in range(2):
        start = pl.multiple_of((2 * pair + side) * LANE, LANE)
        window = shifted[:, pl.ds(start, WIN)]
        for group in range(0, count, 2):
            taken = min(2, count - group)
            got = jnp.dot(
                window, tables[:, group * LANE : (group + taken) * LANE], preferred_element_type=F32
            ).astype(BF16)
            for k in range(taken):
                smooth[group + k, margin : margin + height, side * LANE : (side + 1) * LANE] = got[
                    :, k * LANE : (k + 1) * LANE
                ]


def rows_pass(smooth, tables, count, r):
    start = pl.multiple_of(r * LANE, LANE)
    total = jnp.zeros((LANE, WIN), F32)
    for k in range(count):
        total = total + jnp.dot(tables[k], smooth[k, pl.ds(start, WIN), :], preferred_element_type=F32)
    return total


def spread_table(staged, half_len, reach, count):
    wide_rows = reach + 2 * EDGE
    lane = lax.broadcasted_iota(jnp.int32, (wide_rows, WIN), 1)
    joined = jnp.zeros((wide_rows, WIN), F32)
    for k in range(count):
        shift = (k * reach - EDGE - half_len - (HALF - half_len) % 8) % WIN
        wide = jnp.broadcast_to(staged[k : k + 1, :], (wide_rows, WIN))
        rolled = pltpu.roll(wide, shift, 1, stride=1, stride_axis=0)
        joined = jnp.where((lane >= k * reach) & (lane < (k + 1) * reach), rolled, joined)
    return joined[:, : count * reach].astype(BF16)


def build_tables(column_taps, row_taps, column_tables, row_tables, staged):
    spread(column_taps, staged)
    for k in range(column_taps.shape[0]):
        table = toeplitz(staged[k : k + 1, :], column_taps.shape[1] // 2)
        column_tables[:, k * LANE : (k + 1) * LANE] = table.T.astype(BF16)
    spread(row_taps, staged)
    half_len = row_taps.shape[1] // 2
    if isinstance(row_tables, dict):
        for reach, table in row_tables.items():
            table[...] = spread_table(staged, half_len, reach, row_taps.shape[0])
    else:
        for k in range(row_taps.shape[0]):
            row_tables[k] = toeplitz(staged[k : k + 1, :], half_len).astype(BF16)


def clear_edges(smooth, count, height):
    for k in range(count):
        smooth[k, :HALF, :] = jnp.zeros((HALF, smooth.shape[2]), BF16)
        smooth[k, HALF + height :, :] = jnp.zeros((HALF, smooth.shape[2]), BF16)


def cuts(edge):
    return [edge // 2, edge // 4, edge // 8, edge // 8]


def blur_rows(difference, tables, blur, reach, count, halves, tiles):
    high = halves * reach
    group = max(1, min(tiles, MOST_ROWS // high))

    def some(g, carry):
        begin = [pl.multiple_of((g * group + n) * LANE, LANE) for n in range(group)]
        windows = jnp.concatenate([difference[:high, pl.ds(start, WIN)] for start in begin], axis=0)
        got = jnp.dot(windows, tables[...], preferred_element_type=F32).astype(BF16)
        for n, start in enumerate(begin):
            for h in range(halves):
                rows = slice(n * high + h * reach, n * high + (h + 1) * reach)
                for k in range(count):
                    blur[h, k * reach : (k + 1) * reach, pl.ds(start, LANE)] = got[rows, k * LANE : (k + 1) * LANE]
        return carry

    lax.fori_loop(0, tiles // group, some, 0, unroll=high < LANE)


def exchange_kernel(
    n_patch, n_visit,
    live_in, patch_in, slot_in, coeffs_in, basis_rows_in, basis_cols_in, psf_rows_in, psf_cols_in, blocks, template,
    filtered, last_difference, psf_column_tables, last_table,
    live, patch, slot, coeffs, basis_rows, basis_cols, psf_rows, psf_cols, small_sems, sources, staged, outgoing, arrived, labels_out, labels_in, picks, whole, total, shifted, column_tables, row_tables, smooth, blur, part_difference, *rest,
):
    sizes = cuts(blocks.shape[1])
    reaches = sorted(set(sizes[:-1]) - {sizes[-1]})
    tables_of = dict(zip(reaches, rest[: len(reaches)]))
    tables_of[sizes[-1]] = last_table
    raw = rest[len(reaches) : len(reaches) + len(sizes)]
    load_sem, own_sem, block_send, block_recv, label_send, label_recv, rows_send, rows_recv, told = rest[
        len(reaches) + len(sizes) :
    ]
    me = lax.axis_index("patch")
    my_visit = lax.axis_index("visit")
    local_rows, breadth = template.shape
    height = local_rows * n_visit
    entries, edge = blocks.shape[:2]
    places = n_patch * CAP
    count = basis_rows.shape[0]
    psf_count = psf_rows.shape[1]
    wide = breadth // edge
    halves = height // edge
    slots = halves * wide
    chips = n_patch // 2
    chip, core = me // 2, lax.rem(me, 2)
    sibling = 2 * chip + 1 - core
    starts = [sum(sizes[:c]) for c in range(len(sizes))]
    visits = [lax.rem(my_visit + hop, n_visit) for hop in range(1, n_visit)]

    def tell(semaphore, peer):
        pl.semaphore_signal(semaphore, inc=1, device_id={"patch": peer}, device_id_type=pl.DeviceIdType.MESH)

    def tell_visit(semaphore, visit):
        pl.semaphore_signal(semaphore, inc=1, device_id={"visit": visit}, device_id_type=pl.DeviceIdType.MESH)

    small = [
        pltpu.make_async_copy(source, held, small_sems.at[i])
        for i, (source, held) in enumerate(
            (
                (live_in, live), (patch_in, patch), (slot_in, slot), (coeffs_in, coeffs),
                (basis_rows_in, basis_rows), (basis_cols_in, basis_cols),
                (psf_rows_in, psf_rows), (psf_cols_in, psf_cols),
            )
        )
    ]
    staged_entry = chips == 4
    near_side = chip < chips // 2
    middle = (chip == chips // 2) | (chip == chips // 2 - 1)
    inner = jnp.where(near_side, chip + 1, chip - 1)
    outer = jnp.where(near_side, chip - 1, chip + 1)
    other = jnp.where(near_side, chip + 2, chip - 2)
    mirror = chips - 1 - chip
    barrier = pltpu.get_barrier_semaphore()
    if staged_entry:
        tell(barrier, sibling)

        @pl.when(middle)
        def _():
            for c in range(2):
                tell(barrier, 2 * inner + c)
                tell(barrier, 2 * outer + c)

        @pl.when(jnp.logical_not(middle))
        def _():
            for visit in visits:
                tell_visit(barrier, visit)

        greeted = 3 + jnp.where(middle, 0, n_visit - 1)
    else:
        for hop in range(1, n_patch):
            tell(barrier, lax.rem(me + hop, n_patch))
        for visit in visits:
            tell_visit(barrier, visit)
        greeted = n_patch + n_visit - 2
    for copy in small:
        copy.start()
    loads = [
        pltpu.make_async_copy(blocks.at[:, pl.ds(starts[c], sizes[c])], raw[c], load_sem.at[c])
        for c in range(len(sizes))
    ]
    for load in loads:
        load.start()
    my_rows = pl.ds(pl.multiple_of(my_visit * local_rows, local_rows), local_rows)
    own = pltpu.make_async_copy(template, whole.at[my_rows], own_sem)
    own.start()

    for copy in small[:3]:
        copy.wait()
    targets = [patch[i] for i in range(entries)]
    marks = [jnp.where(i < live[0, 0], slot[i], -1) for i in range(entries)]

    def find(d, carry):
        first, last, first_mark, last_mark = (jnp.int32(0), jnp.int32(-1), jnp.int32(-1), jnp.int32(-1))
        for i in range(entries):
            last = jnp.where(targets[i] == d, i, last)
            last_mark = jnp.where(targets[i] == d, marks[i], last_mark)
        for i in reversed(range(entries)):
            first = jnp.where(targets[i] == d, i, first)
            first_mark = jnp.where(targets[i] == d, marks[i], first_mark)
        labels = (first_mark, jnp.where(first < last, last_mark, -1))
        for c, (source, label) in enumerate(zip((first, jnp.maximum(last, 0)), labels)):
            sources[d * CAP + c] = source
            labels_out[d, c : c + 1, :] = jnp.full((1, LANE), label, jnp.int32)
        return carry

    def rows_of(c, place, number=1):
        return pl.ds(pl.multiple_of(places * starts[c] + place * sizes[c], EDGE), number * sizes[c])

    def pack(c, first, number):
        def one(i, carry):
            outgoing[rows_of(c, first + i), :] = raw[c][sources[first + i]]
            return carry

        lax.fori_loop(0, number, one, 0)

    if staged_entry:
        turns = [
            jnp.where(middle, inner, other), jnp.where(middle, other, mirror), jnp.where(middle, outer, inner), chip,
        ]
    else:
        turns = [lax.rem(chip + hop, chips) for hop in range(chips - 1, -1, -1)]
    lax.fori_loop(2 * turns[0], 2 * turns[0] + 2, find, 0)
    loads[0].wait()
    pack(0, 2 * turns[0] * CAP, 2 * CAP)
    pl.semaphore_wait(barrier, greeted)

    row_copies = [
        pltpu.make_async_remote_copy(
            src_ref=template, dst_ref=whole.at[my_rows],
            send_sem=rows_send, recv_sem=rows_recv,
            device_id={"visit": visit}, device_id_type=pl.DeviceIdType.MESH,
        )
        for hop, visit in enumerate(visits)
    ]

    def landed(held, semaphore):
        pltpu.make_async_copy(held, held, semaphore).wait()

    def label_copy(peer):
        return pltpu.make_async_remote_copy(
            src_ref=labels_out.at[peer], dst_ref=labels_in.at[me],
            send_sem=label_send, recv_sem=label_recv,
            device_id={"patch": peer}, device_id_type=pl.DeviceIdType.MESH,
        )

    def block_copy(peer, c):
        return pltpu.make_async_remote_copy(
            src_ref=outgoing.at[rows_of(c, peer * CAP, CAP)], dst_ref=arrived.at[rows_of(c, me * CAP, CAP)],
            send_sem=block_send, recv_sem=block_recv.at[c],
            device_id={"patch": peer}, device_id_type=pl.DeviceIdType.MESH,
        )

    def send(peer, c):
        if c == 0:
            label_copy(peer).start()
        block_copy(peer, c).start()

    def send_chip(there, c):
        send(2 * there + core, c)
        send(2 * there + 1 - core, c)

    early, late = range(len(sizes) - 3), range(len(sizes) - 3, len(sizes))

    def pack_rest():
        for turn in turns[1:]:
            lax.fori_loop(2 * turn, 2 * turn + 2, find, 0)
            pack(0, 2 * turn * CAP, 2 * CAP)
        for c in range(1, len(sizes)):
            loads[c].wait()
            pack(c, 0, places)

    if staged_entry:

        @pl.when(middle)
        def _():
            send_chip(inner, 0)

        @pl.when(jnp.logical_not(middle))
        def _():
            for c in range(2):
                tell(told.at[0], 2 * inner + c)
            for visit in visits:
                tell_visit(told.at[3], visit)
            for copy in row_copies:
                copy.start()

        @pl.when(middle)
        def _():
            pl.semaphore_wait(told.at[0], 2)
            tell(told.at[1], 2 * outer + core)
            tell(told.at[1], 2 * inner + core)

        pack_rest()

        @pl.when(middle)
        def _():
            pl.semaphore_wait(told.at[1], 1)
            tell(told.at[2], 2 * outer + core)
            for steps in early, late:
                for c in steps:
                    send_chip(other, c)
                    send_chip(outer, c)
                    send(sibling, c)
                    if c and steps is early:
                        send_chip(inner, c)
            for c in late:
                send_chip(inner, c)
            pl.semaphore_wait(told.at[4], 1)
            for copy in row_copies:
                copy.start()

        @pl.when(jnp.logical_not(middle))
        def _():
            pl.semaphore_wait(told.at[1], 1)
            send_chip(other, 0)
            pl.semaphore_wait(told.at[3], n_visit - 1)
            tell(told.at[4], 2 * inner + core)
            pl.semaphore_wait(told.at[2], 1)
            for steps in early, late:
                for c in steps:
                    send_chip(mirror, c)
                    if steps is early:
                        if c:
                            send_chip(other, c)
                        send_chip(inner, c)
                    send(sibling, c)
            for c in late:
                send_chip(other, c)
                send_chip(inner, c)

    else:
        for copy in row_copies:
            copy.start()
        for turn in turns[:1]:
            send_chip(turn, 0)
        pack_rest()
        for c in range(len(sizes)):
            for turn in turns[(1 if c == 0 else 0) : -1]:
                send_chip(turn, c)
            send(sibling, c)

    labels_in[me] = labels_out[me]
    for c in range(len(sizes)):
        arrived[rows_of(c, me * CAP, CAP), :] = outgoing[rows_of(c, me * CAP, CAP), :]
    for copy in small[3:]:
        copy.wait()
    scaled = jnp.concatenate(
        [(coeffs[0, k] * basis_cols[k : k + 1, :]).astype(BF16).astype(F32) for k in range(count)], axis=0
    )
    build_tables(basis_rows[...].astype(F32), scaled, column_tables, row_tables, staged)
    build_tables(psf_rows[0].astype(F32), psf_cols[0].astype(F32), psf_column_tables, tables_of, staged)
    clear_edges(smooth, count, height)

    def clear(r, carry):
        filtered[pl.ds(pl.multiple_of(r * EDGE, EDGE), EDGE), :] = jnp.zeros((EDGE, breadth), F32)
        return carry

    lax.fori_loop(0, height // EDGE + 2, clear, 0)
    own.wait()
    landed(whole.at[pl.ds(0, (n_visit - 1) * local_rows)], rows_recv)
    shift_into(
        lambda rows, t: whole[rows, t * LANE : (t + 1) * LANE].astype(F32),
        shifted, height, breadth // LANE, 32,
    )

    def per_pair(pair, carry):
        columns_pass(shifted, column_tables, smooth, pair, count, height)

        def per_row(r, inside):
            rows = pl.ds(pl.multiple_of(r * LANE, LANE), LANE)
            columns = pl.ds(pl.multiple_of(pair * WIN, WIN), WIN)
            total[rows, columns] = -rows_pass(smooth, row_tables, count, r)
            return inside

        return lax.fori_loop(0, height // LANE, per_row, carry)

    lax.fori_loop(0, breadth // WIN, per_pair, 0)

    landed(labels_in.at[pl.ds(0, n_patch - 1)], label_recv)
    for first in range(0, places, LANE // EDGE):
        lane = lax.broadcasted_iota(jnp.int32, (8, LANE), 1)
        named = jnp.full((8, LANE), -1, jnp.int32)
        for p in range(LANE // EDGE):
            place = first + p
            mark = jnp.broadcast_to(labels_in[place // CAP, place % CAP : place % CAP + 1, :], (8, LANE))
            named = jnp.where((lane >= p * EDGE) & (lane < (p + 1) * EDGE), mark, named)
        named = jnp.concatenate([named] * (EDGE // 8), axis=0)
        lane = lax.broadcasted_iota(jnp.int32, (EDGE, LANE), 1)
        same = lax.rem(lane, EDGE) == lax.broadcasted_iota(jnp.int32, (EDGE, LANE), 0)
        for s in range(slots):
            picks[s * EDGE : (s + 1) * EDGE, first * EDGE : first * EDGE + LANE] = jnp.where(
                same & (named == s), 1.0, 0.0
            ).astype(BF16)

    for c, reach in enumerate(sizes):
        landed(arrived.at[rows_of(c, 0, places - CAP)], block_recv.at[c])

        def add(r, carry, c=c):
            pieces = jnp.concatenate(
                [
                    arrived[pl.ds(pl.multiple_of(places * starts[c] + p * sizes[c] + r * EDGE, EDGE), EDGE), :]
                    for p in range(places)
                ],
                axis=0,
            )
            summed = jnp.dot(picks[...], pieces, preferred_element_type=F32)
            for s in range(slots):
                rows = pl.ds(pl.multiple_of(s // wide * edge + starts[c] + r * EDGE, EDGE), EDGE)
                columns = slice(s % wide * edge, (s % wide + 1) * edge)
                total[rows, columns] += summed[s * EDGE : (s + 1) * EDGE]
            return carry

        lax.fori_loop(0, reach // EDGE, add, 0, unroll=reach < LANE)
        last = c == len(sizes) - 1
        held = last_difference if last else part_difference

        def shift(r, carry, c=c, held=held):
            lane = lax.broadcasted_iota(jnp.int32, (EDGE, LANE), 1)
            for h in range(halves):
                source = pl.ds(pl.multiple_of(h * edge + starts[c] + r * EDGE, EDGE), EDGE)
                rows = pl.ds(pl.multiple_of(h * sizes[c] + r * EDGE, EDGE), EDGE)
                before = jnp.zeros((EDGE, LANE), F32)
                for t in range(breadth // LANE):
                    rolled = pltpu.roll(total[source, t * LANE : (t + 1) * LANE], HALF, 1)
                    held[rows, t * LANE : (t + 1) * LANE] = jnp.where(lane < HALF, before, rolled).astype(BF16)
                    before = rolled
                held[rows, breadth:] = jnp.where(lane < HALF, before, 0.0).astype(BF16)
            return carry

        lax.fori_loop(0, reach // EDGE, shift, 0, unroll=reach < LANE)
        if last:
            continue

        blur_rows(part_difference, psf_column_tables, blur, reach, psf_count, halves, breadth // LANE)

        def gather(t, carry, c=c, reach=reach):
            columns = pl.ds(pl.multiple_of(t * WIN, WIN), WIN)
            for h in range(halves):
                rows = slice(h * edge + starts[c], h * edge + starts[c] + reach + 2 * EDGE)
                filtered[rows, columns] += jnp.dot(
                    tables_of[reach][...], blur[h, : psf_count * reach, columns], preferred_element_type=F32
                )
            return carry

        lax.fori_loop(0, breadth // WIN, gather, 0, unroll=halves * reach <= LANE)

    landed(whole.at[pl.ds(0, (n_visit - 1) * local_rows)], rows_send)
    landed(labels_out.at[pl.ds(0, n_patch - 1)], label_send)
    landed(outgoing.at[pl.ds(0, (places - CAP) * edge)], block_send)


def finish_kernel(edge, filtered, difference, column_tables, table, out, blur, ends, sems):
    height, breadth = out.shape
    halves = height // edge
    psf_count = column_tables.shape[1] // LANE
    reach = difference.shape[0] // halves
    copies = []

    def put(source, first, rows):
        copies.append(pltpu.make_async_copy(source, out.at[pl.ds(first, rows)], sems.at[len(copies)]))
        copies[-1].start()

    done = 0
    for h in range(halves):
        upto = (h + 1) * edge - reach - EDGE
        put(filtered.at[pl.ds(EDGE + done, upto - done)], done, upto - done)
        done = upto + reach + 2 * EDGE
    blur_rows(difference, column_tables, blur, reach, psf_count, halves, breadth // LANE)
    for h in range(halves):
        first = (h + 1) * edge - reach
        for t in range(breadth // WIN):
            columns = slice(t * WIN, (t + 1) * WIN)
            ends[h, :, columns] = filtered[first : first + reach + 2 * EDGE, columns] + jnp.dot(
                table[...], blur[h, :, columns], preferred_element_type=F32
            )
        rows = reach + 2 * EDGE if h < halves - 1 else reach + EDGE
        put(ends.at[h, pl.ds(0, rows)], first - EDGE, rows)
    for copy in copies:
        copy.wait()


SMEM = pl.BlockSpec(memory_space=pltpu.SMEM)
HBM = pl.BlockSpec(memory_space=pltpu.HBM)
VMEM = pl.BlockSpec(memory_space=pltpu.VMEM)


def stencil_scratch(count, height, breadth):
    return [
        pltpu.VMEM((height, breadth + LANE), BF16),
        pltpu.VMEM((WIN, count * LANE), BF16),
        pltpu.VMEM((count, LANE, WIN), BF16),
        pltpu.VMEM((count, height + 2 * HALF, WIN), BF16),
    ]


def per_device(blocks, block_patch, block_slot, block_count, template, basis_rows, basis_cols, coeffs, psf_rows, psf_cols):
    n_patch = lax.axis_size("patch")
    n_visit = lax.axis_size("visit")
    local_rows, breadth = template.shape[1:]
    height = local_rows * n_visit
    entries, edge = blocks.shape[2:4]
    halves = height // edge
    slots = halves * (breadth // edge)
    places = n_patch * CAP
    count = basis_rows.shape[0]
    psf_count = psf_rows.shape[1]
    sizes = cuts(edge)
    reaches = sorted(set(sizes[:-1]) - {sizes[-1]})
    most = max(sizes)
    final = sizes[-1]
    dma = pltpu.SemaphoreType.DMA
    handed = pl.pallas_call(
        functools.partial(exchange_kernel, n_patch, n_visit),
        out_shape=(
            jax.ShapeDtypeStruct((height + 2 * EDGE, breadth), F32),
            jax.ShapeDtypeStruct((halves * final, breadth + LANE), BF16),
            jax.ShapeDtypeStruct((WIN, psf_count * LANE), BF16),
            jax.ShapeDtypeStruct((final + 2 * EDGE, psf_count * final), BF16),
        ),
        in_specs=[pl.BlockSpec(memory_space=pl.ANY)] + [HBM] * 9,
        out_specs=(VMEM,) * 4,
        scratch_shapes=[
            pltpu.SMEM((1, 1), jnp.int32),
            pltpu.SMEM((entries,), jnp.int32),
            pltpu.SMEM((entries,), jnp.int32),
            pltpu.SMEM(coeffs.shape, F32),
            pltpu.VMEM(basis_rows.shape, BF16),
            pltpu.VMEM(basis_cols.shape, F32),
            pltpu.VMEM(psf_rows.shape, BF16),
            pltpu.VMEM(psf_cols.shape, BF16),
            dma((8,)),
            pltpu.SMEM((places,), jnp.int32),
            pltpu.VMEM((pl.cdiv(max(count, psf_count), 8) * 8, WIN), F32),
            pltpu.VMEM((places * edge, edge), BF16),
            pltpu.VMEM((places * edge, edge), BF16),
            pltpu.VMEM((n_patch, CAP, LANE), jnp.int32),
            pltpu.VMEM((n_patch, CAP, LANE), jnp.int32),
            pltpu.VMEM((slots * EDGE, places * EDGE), BF16),
            pltpu.VMEM((height, breadth), BF16),
            pltpu.VMEM((height, breadth), F32),
        ]
        + stencil_scratch(count, height, breadth)
        + [
            pltpu.VMEM((halves, psf_count * most, breadth), BF16),
            pltpu.VMEM((halves * most, breadth + LANE), BF16),
        ]
        + [pltpu.VMEM((reach + 2 * EDGE, psf_count * reach), BF16) for reach in reaches]
        + [pltpu.VMEM((entries, size, edge), BF16) for size in sizes]
        + [
            dma((len(sizes),)),
            dma(()),
            dma(()),
            dma((len(sizes),)),
            dma(()),
            dma(()),
            dma(()),
            dma(()),
            pltpu.SemaphoreType.REGULAR((5,)),
        ],
        compiler_params=pltpu.CompilerParams(
            collective_id=0, has_side_effects=True, vmem_limit_bytes=VMEM_LIMIT
        ),
    )(
        block_count,
        *(
            pltpu.with_memory_space_constraint(value, pltpu.HBM)
            for value in (
                block_patch.reshape(entries), block_slot.reshape(entries), coeffs,
                basis_rows, basis_cols, psf_rows, psf_cols, blocks[0, 0], template[0],
            )
        )
    )
    filtered = pl.pallas_call(
        functools.partial(finish_kernel, edge),
        out_shape=jax.ShapeDtypeStruct((height, breadth), F32),
        in_specs=[VMEM] * 4,
        out_specs=HBM,
        scratch_shapes=[
            pltpu.VMEM((halves, psf_count * final, breadth), BF16),
            pltpu.VMEM((halves, final + 2 * EDGE, breadth), F32),
            dma((2 * halves,)),
        ],
        compiler_params=pltpu.CompilerParams(vmem_limit_bytes=16 * 1024 * 1024),
    )(*handed)
    return filtered[None, None]


def solution(mesh):
    return jax.shard_map(
        per_device,
        mesh=mesh,
        in_specs=(
            P("patch", "visit", None, None, None),
            P("patch", "visit", None, None),
            P("patch", "visit", None),
            P("patch", "visit"),
            P("patch", "visit", None),
            P(),
            P(),
            P("visit", None),
            P("visit", None, None),
            P("visit", None, None),
        ),
        out_specs=P("patch", "visit", None, None),
        check_vma=False,
    )
```

```python
import functools

import jax
import jax.numpy as jnp
from jax import lax
from jax.experimental import pallas as pl
from jax.experimental.pallas import tpu as pltpu
from jax.sharding import PartitionSpec as P

CAP = 2
MOST_ROWS = 512
LANE = 128
HALF = 64
EDGE = 16
WIN = 256
F32 = jnp.float32
BF16 = jnp.bfloat16
VMEM_LIMIT = 32 * 1024 * 1024


def toeplitz(row, half_len):
    wide = jnp.broadcast_to(row, (LANE, WIN))
    return pltpu.roll(wide, (HALF - half_len) // 8 * 8, 1, stride=1, stride_axis=0)


def spread(taps, staged):
    count, length = taps.shape
    staged[...] = jnp.zeros(staged.shape, F32)
    staged[:count, :length] = taps
    lead = (HALF - length // 2) % 8
    if lead:
        staged[...] = pltpu.roll(staged[...], lead, 1)


def shift_into(load_tile, shifted, height, tiles, step):
    def body(r, carry):
        rows = pl.ds(pl.multiple_of(r * step, step), step)
        lane = lax.broadcasted_iota(jnp.int32, (step, LANE), 1)
        before = jnp.zeros((step, LANE), F32)
        for t in range(tiles):
            rolled = pltpu.roll(load_tile(rows, t), HALF, 1)
            shifted[rows, t * LANE : (t + 1) * LANE] = jnp.where(lane < HALF, before, rolled).astype(BF16)
            before = rolled
        shifted[rows, tiles * LANE :] = jnp.where(lane < HALF, before, 0.0).astype(BF16)
        return carry

    lax.fori_loop(0, height // step, body, 0)


def columns_pass(shifted, tables, smooth, pair, count, height, margin=HALF):
    for side in range(2):
        start = pl.multiple_of((2 * pair + side) * LANE, LANE)
        window = shifted[:, pl.ds(start, WIN)]
        for group in range(0, count, 2):
            taken = min(2, count - group)
            got = jnp.dot(
                window, tables[:, group * LANE : (group + taken) * LANE], preferred_element_type=F32
            ).astype(BF16)
            for k in range(taken):
                smooth[group + k, margin : margin + height, side * LANE : (side + 1) * LANE] = got[
                    :, k * LANE : (k + 1) * LANE
                ]


def rows_pass(smooth, tables, count, r):
    start = pl.multiple_of(r * LANE, LANE)
    total = jnp.zeros((LANE, WIN), F32)
    for k in range(count):
        total = total + jnp.dot(tables[k], smooth[k, pl.ds(start, WIN), :], preferred_element_type=F32)
    return total


def spread_table(staged, half_len, reach, count):
    wide_rows = reach + 2 * EDGE
    lane = lax.broadcasted_iota(jnp.int32, (wide_rows, WIN), 1)
    joined = jnp.zeros((wide_rows, WIN), F32)
    for k in range(count):
        shift = (k * reach - EDGE - half_len - (HALF - half_len) % 8) % WIN
        wide = jnp.broadcast_to(staged[k : k + 1, :], (wide_rows, WIN))
        rolled = pltpu.roll(wide, shift, 1, stride=1, stride_axis=0)
        joined = jnp.where((lane >= k * reach) & (lane < (k + 1) * reach), rolled, joined)
    return joined[:, : count * reach].astype(BF16)


def build_tables(column_taps, row_taps, column_tables, row_tables, staged):
    spread(column_taps, staged)
    for k in range(column_taps.shape[0]):
        table = toeplitz(staged[k : k + 1, :], column_taps.shape[1] // 2)
        column_tables[:, k * LANE : (k + 1) * LANE] = table.T.astype(BF16)
    spread(row_taps, staged)
    half_len = row_taps.shape[1] // 2
    if isinstance(row_tables, dict):
        for reach, table in row_tables.items():
            table[...] = spread_table(staged, half_len, reach, row_taps.shape[0])
    else:
        for k in range(row_taps.shape[0]):
            row_tables[k] = toeplitz(staged[k : k + 1, :], half_len).astype(BF16)


def clear_edges(smooth, count, height):
    for k in range(count):
        smooth[k, :HALF, :] = jnp.zeros((HALF, smooth.shape[2]), BF16)
        smooth[k, HALF + height :, :] = jnp.zeros((HALF, smooth.shape[2]), BF16)


def cuts(edge):
    return [edge // 4, edge // 4, edge // 4, edge // 8, edge // 8]


def blur_rows(difference, tables, blur, reach, count, halves, tiles):
    high = halves * reach
    group = max(1, min(tiles, MOST_ROWS // high))

    def some(g, carry):
        begin = [pl.multiple_of((g * group + n) * LANE, LANE) for n in range(group)]
        windows = jnp.concatenate([difference[:high, pl.ds(start, WIN)] for start in begin], axis=0)
        got = jnp.dot(windows, tables[...], preferred_element_type=F32).astype(BF16)
        for n, start in enumerate(begin):
            for h in range(halves):
                rows = slice(n * high + h * reach, n * high + (h + 1) * reach)
                for k in range(count):
                    blur[h, k * reach : (k + 1) * reach, pl.ds(start, LANE)] = got[rows, k * LANE : (k + 1) * LANE]
        return carry

    lax.fori_loop(0, tiles // group, some, 0, unroll=high < LANE)


def exchange_kernel(
    n_patch, n_visit,
    live_in, patch_in, slot_in, coeffs_in, basis_rows_in, basis_cols_in, psf_rows_in, psf_cols_in, blocks, template,
    filtered, last_difference, psf_column_tables, last_table,
    live, patch, slot, coeffs, basis_rows, basis_cols, psf_rows, psf_cols, small_sems, sources, staged, outgoing, arrived, labels_out, labels_in, picks, whole, total, shifted, column_tables, row_tables, smooth, blur, part_difference, *rest,
):
    sizes = cuts(blocks.shape[1])
    reaches = sorted(set(sizes[:-1]) - {sizes[-1]})
    tables_of = dict(zip(reaches, rest[: len(reaches)]))
    tables_of[sizes[-1]] = last_table
    raw = rest[len(reaches) : len(reaches) + len(sizes)]
    load_sem, own_sem, block_send, block_recv, label_send, label_recv, rows_send, rows_recv, told = rest[
        len(reaches) + len(sizes) :
    ]
    me = lax.axis_index("patch")
    my_visit = lax.axis_index("visit")
    local_rows, breadth = template.shape
    height = local_rows * n_visit
    entries, edge = blocks.shape[:2]
    places = n_patch * CAP
    count = basis_rows.shape[0]
    psf_count = psf_rows.shape[1]
    wide = breadth // edge
    halves = height // edge
    slots = halves * wide
    chips = n_patch // 2
    chip, core = me // 2, lax.rem(me, 2)
    sibling = 2 * chip + 1 - core
    starts = [sum(sizes[:c]) for c in range(len(sizes))]
    visits = [lax.rem(my_visit + hop, n_visit) for hop in range(1, n_visit)]

    def tell(semaphore, peer):
        pl.semaphore_signal(semaphore, inc=1, device_id={"patch": peer}, device_id_type=pl.DeviceIdType.MESH)

    def tell_visit(semaphore, visit):
        pl.semaphore_signal(semaphore, inc=1, device_id={"visit": visit}, device_id_type=pl.DeviceIdType.MESH)

    small = [
        pltpu.make_async_copy(source, held, small_sems.at[i])
        for i, (source, held) in enumerate(
            (
                (live_in, live), (patch_in, patch), (slot_in, slot), (coeffs_in, coeffs),
                (basis_rows_in, basis_rows), (basis_cols_in, basis_cols),
                (psf_rows_in, psf_rows), (psf_cols_in, psf_cols),
            )
        )
    ]
    staged_entry = chips == 4
    near_side = chip < chips // 2
    middle = (chip == chips // 2) | (chip == chips // 2 - 1)
    inner = jnp.where(near_side, chip + 1, chip - 1)
    outer = jnp.where(near_side, chip - 1, chip + 1)
    other = jnp.where(near_side, chip + 2, chip - 2)
    mirror = chips - 1 - chip
    barrier = pltpu.get_barrier_semaphore()
    if staged_entry:
        tell(barrier, sibling)

        @pl.when(middle)
        def _():
            for c in range(2):
                tell(barrier, 2 * inner + c)
                tell(barrier, 2 * outer + c)

        @pl.when(jnp.logical_not(middle))
        def _():
            for visit in visits:
                tell_visit(barrier, visit)

        greeted = 3 + jnp.where(middle, 0, n_visit - 1)
    else:
        for hop in range(1, n_patch):
            tell(barrier, lax.rem(me + hop, n_patch))
        for visit in visits:
            tell_visit(barrier, visit)
        greeted = n_patch + n_visit - 2
    for copy in small[:3]:
        copy.start()
    loads = [
        pltpu.make_async_copy(blocks.at[:, pl.ds(starts[c], sizes[c])], raw[c], load_sem.at[c])
        for c in range(len(sizes))
    ]
    for copy in loads + small[3:]:
        copy.start()
    my_rows = pl.ds(pl.multiple_of(my_visit * local_rows, local_rows), local_rows)
    own = pltpu.make_async_copy(template, whole.at[my_rows], own_sem)
    own.start()

    for copy in small[:3]:
        copy.wait()
    targets = [patch[i] for i in range(entries)]
    marks = [jnp.where(i < live[0, 0], slot[i], -1) for i in range(entries)]

    def find(d, carry):
        first, last, first_mark, last_mark = (jnp.int32(0), jnp.int32(-1), jnp.int32(-1), jnp.int32(-1))
        for i in range(entries):
            last = jnp.where(targets[i] == d, i, last)
            last_mark = jnp.where(targets[i] == d, marks[i], last_mark)
        for i in reversed(range(entries)):
            first = jnp.where(targets[i] == d, i, first)
            first_mark = jnp.where(targets[i] == d, marks[i], first_mark)
        labels = (first_mark, jnp.where(first < last, last_mark, -1))
        for c, (source, label) in enumerate(zip((first, jnp.maximum(last, 0)), labels)):
            sources[d * CAP + c] = source
            labels_out[d, c : c + 1, :] = jnp.full((1, LANE), label, jnp.int32)
        return carry

    def rows_of(c, place, number=1):
        return pl.ds(pl.multiple_of(places * starts[c] + place * sizes[c], EDGE), number * sizes[c])

    def pack(c, first, number):
        def one(i, carry):
            outgoing[rows_of(c, first + i), :] = raw[c][sources[first + i]]
            return carry

        lax.fori_loop(0, number, one, 0)

    if staged_entry:
        turns = [
            jnp.where(middle, inner, other), jnp.where(middle, other, mirror), jnp.where(middle, outer, inner), chip,
        ]
    else:
        turns = [lax.rem(chip + hop, chips) for hop in range(chips - 1, -1, -1)]
    find(2 * turns[0], 0)
    find(2 * turns[0] + 1, 0)
    loads[0].wait()
    pack(0, 2 * turns[0] * CAP, 2 * CAP)
    pl.semaphore_wait(barrier, greeted)

    row_copies = [
        pltpu.make_async_remote_copy(
            src_ref=template, dst_ref=whole.at[my_rows],
            send_sem=rows_send, recv_sem=rows_recv,
            device_id={"visit": visit}, device_id_type=pl.DeviceIdType.MESH,
        )
        for hop, visit in enumerate(visits)
    ]

    def landed(held, semaphore):
        pltpu.make_async_copy(held, held, semaphore).wait()

    def label_copy(peer):
        return pltpu.make_async_remote_copy(
            src_ref=labels_out.at[peer], dst_ref=labels_in.at[me],
            send_sem=label_send, recv_sem=label_recv,
            device_id={"patch": peer}, device_id_type=pl.DeviceIdType.MESH,
        )

    def block_copy(peer, c):
        return pltpu.make_async_remote_copy(
            src_ref=outgoing.at[rows_of(c, peer * CAP, CAP)], dst_ref=arrived.at[rows_of(c, me * CAP, CAP)],
            send_sem=block_send, recv_sem=block_recv.at[c],
            device_id={"patch": peer}, device_id_type=pl.DeviceIdType.MESH,
        )

    def send(peer, c):
        if c == 0:
            label_copy(peer).start()
        block_copy(peer, c).start()

    def send_chip(there, c):
        send(2 * there + 1, c)
        send(2 * there, c)

    early, late = range(len(sizes) - 3), range(len(sizes) - 3, len(sizes))

    def pack_rest():
        for turn in turns[1:]:
            lax.fori_loop(2 * turn, 2 * turn + 2, find, 0)
            pack(0, 2 * turn * CAP, 2 * CAP)
            if staged_entry:
                pack(1, 2 * turn * CAP, 2 * CAP)
        for c in range(2 if staged_entry else 1, len(sizes)):
            loads[c].wait()
            pack(c, 0, places)

    if staged_entry:

        @pl.when(middle)
        def _():
            send_chip(inner, 0)

        loads[1].wait()
        pack(1, 2 * turns[0] * CAP, 2 * CAP)

        @pl.when(middle)
        def _():
            send_chip(inner, 1)

        @pl.when(jnp.logical_not(middle))
        def _():
            for c in range(2):
                tell(told.at[0], 2 * inner + c)
            for visit in visits:
                tell_visit(told.at[3], visit)
            for copy in row_copies:
                copy.start()

        @pl.when(middle)
        def _():
            pl.semaphore_wait(told.at[0], 2)
            tell(told.at[1], 2 * outer + core)
            tell(told.at[1], 2 * inner + core)

        pack_rest()

        @pl.when(middle)
        def _():
            pl.semaphore_wait(told.at[1], 1)
            tell(told.at[2], 2 * outer + core)
            for steps in early, late:
                for c in steps:
                    send_chip(other, c)
                    send_chip(outer, c)
                    send(sibling, c)
                    if c > 1 and steps is early:
                        send_chip(inner, c)
            for c in late:
                send_chip(inner, c)
            pl.semaphore_wait(told.at[4], 1)
            for copy in row_copies:
                copy.start()

        @pl.when(jnp.logical_not(middle))
        def _():
            pl.semaphore_wait(told.at[1], 1)
            send_chip(other, 0)
            pl.semaphore_wait(told.at[3], n_visit - 1)
            tell(told.at[4], 2 * inner + core)
            pl.semaphore_wait(told.at[2], 1)
            for steps in early, late:
                for c in steps:
                    send_chip(mirror, c)
                    if steps is early:
                        if c:
                            send_chip(other, c)
                        send_chip(inner, c)
                    send(sibling, c)
            for c in late:
                send_chip(other, c)
                send_chip(inner, c)

    else:
        for copy in row_copies:
            copy.start()
        for turn in turns[:1]:
            send_chip(turn, 0)
        pack_rest()
        for c in range(len(sizes)):
            for turn in turns[(1 if c == 0 else 0) : -1]:
                send_chip(turn, c)
            send(sibling, c)

    labels_in[me] = labels_out[me]
    for c in range(len(sizes)):
        arrived[rows_of(c, me * CAP, CAP), :] = outgoing[rows_of(c, me * CAP, CAP), :]
    for copy in small[3:]:
        copy.wait()
    scaled = jnp.concatenate(
        [(coeffs[0, k] * basis_cols[k : k + 1, :]).astype(BF16).astype(F32) for k in range(count)], axis=0
    )
    build_tables(basis_rows[...].astype(F32), scaled, column_tables, row_tables, staged)
    build_tables(psf_rows[0].astype(F32), psf_cols[0].astype(F32), psf_column_tables, tables_of, staged)
    clear_edges(smooth, count, height)

    def clear(r, carry):
        filtered[pl.ds(pl.multiple_of(r * EDGE, EDGE), EDGE), :] = jnp.zeros((EDGE, breadth), F32)
        return carry

    lax.fori_loop(0, height // EDGE + 2, clear, 0)
    own.wait()
    landed(whole.at[pl.ds(0, (n_visit - 1) * local_rows)], rows_recv)
    shift_into(
        lambda rows, t: whole[rows, t * LANE : (t + 1) * LANE].astype(F32),
        shifted, height, breadth // LANE, 32,
    )

    def per_pair(pair, carry):
        columns_pass(shifted, column_tables, smooth, pair, count, height)

        def per_row(r, inside):
            rows = pl.ds(pl.multiple_of(r * LANE, LANE), LANE)
            columns = pl.ds(pl.multiple_of(pair * WIN, WIN), WIN)
            total[rows, columns] = -rows_pass(smooth, row_tables, count, r)
            return inside

        return lax.fori_loop(0, height // LANE, per_row, carry)

    lax.fori_loop(0, breadth // WIN, per_pair, 0)

    landed(labels_in.at[pl.ds(0, n_patch - 1)], label_recv)
    for first in range(0, places, LANE // EDGE):
        lane = lax.broadcasted_iota(jnp.int32, (8, LANE), 1)
        named = jnp.full((8, LANE), -1, jnp.int32)
        for p in range(LANE // EDGE):
            place = first + p
            mark = jnp.broadcast_to(labels_in[place // CAP, place % CAP : place % CAP + 1, :], (8, LANE))
            named = jnp.where((lane >= p * EDGE) & (lane < (p + 1) * EDGE), mark, named)
        named = jnp.concatenate([named] * (EDGE // 8), axis=0)
        lane = lax.broadcasted_iota(jnp.int32, (EDGE, LANE), 1)
        same = lax.rem(lane, EDGE) == lax.broadcasted_iota(jnp.int32, (EDGE, LANE), 0)
        for s in range(slots):
            picks[s * EDGE : (s + 1) * EDGE, first * EDGE : first * EDGE + LANE] = jnp.where(
                same & (named == s), 1.0, 0.0
            ).astype(BF16)

    for c, reach in enumerate(sizes):
        landed(arrived.at[rows_of(c, 0, places - CAP)], block_recv.at[c])

        def add(r, carry, c=c):
            pieces = jnp.concatenate(
                [
                    arrived[pl.ds(pl.multiple_of(places * starts[c] + p * sizes[c] + r * EDGE, EDGE), EDGE), :]
                    for p in range(places)
                ],
                axis=0,
            )
            summed = jnp.dot(picks[...], pieces, preferred_element_type=F32)
            for s in range(slots):
                rows = pl.ds(pl.multiple_of(s // wide * edge + starts[c] + r * EDGE, EDGE), EDGE)
                columns = slice(s % wide * edge, (s % wide + 1) * edge)
                total[rows, columns] += summed[s * EDGE : (s + 1) * EDGE]
            return carry

        lax.fori_loop(0, reach // EDGE, add, 0, unroll=reach < LANE)
        last = c == len(sizes) - 1
        held = last_difference if last else part_difference

        def shift(r, carry, c=c, held=held):
            lane = lax.broadcasted_iota(jnp.int32, (EDGE, LANE), 1)
            for h in range(halves):
                source = pl.ds(pl.multiple_of(h * edge + starts[c] + r * EDGE, EDGE), EDGE)
                rows = pl.ds(pl.multiple_of(h * sizes[c] + r * EDGE, EDGE), EDGE)
                before = jnp.zeros((EDGE, LANE), F32)
                for t in range(breadth // LANE):
                    rolled = pltpu.roll(total[source, t * LANE : (t + 1) * LANE], HALF, 1)
                    held[rows, t * LANE : (t + 1) * LANE] = jnp.where(lane < HALF, before, rolled).astype(BF16)
                    before = rolled
                held[rows, breadth:] = jnp.where(lane < HALF, before, 0.0).astype(BF16)
            return carry

        lax.fori_loop(0, reach // EDGE, shift, 0, unroll=reach < LANE)
        if last:
            continue

        blur_rows(part_difference, psf_column_tables, blur, reach, psf_count, halves, breadth // LANE)

        def gather(t, carry, c=c, reach=reach):
            columns = pl.ds(pl.multiple_of(t * WIN, WIN), WIN)
            for h in range(halves):
                rows = slice(h * edge + starts[c], h * edge + starts[c] + reach + 2 * EDGE)
                filtered[rows, columns] += jnp.dot(
                    tables_of[reach][...], blur[h, : psf_count * reach, columns], preferred_element_type=F32
                )
            return carry

        lax.fori_loop(0, breadth // WIN, gather, 0, unroll=halves * reach <= LANE)

    landed(whole.at[pl.ds(0, (n_visit - 1) * local_rows)], rows_send)
    landed(labels_out.at[pl.ds(0, n_patch - 1)], label_send)
    landed(outgoing.at[pl.ds(0, (places - CAP) * edge)], block_send)


def finish_kernel(edge, filtered, difference, column_tables, table, out, blur, ends, sems):
    height, breadth = out.shape
    halves = height // edge
    psf_count = column_tables.shape[1] // LANE
    reach = difference.shape[0] // halves
    copies = []

    def put(source, first, rows):
        copies.append(pltpu.make_async_copy(source, out.at[pl.ds(first, rows)], sems.at[len(copies)]))
        copies[-1].start()

    done = 0
    for h in range(halves):
        upto = (h + 1) * edge - reach - EDGE
        put(filtered.at[pl.ds(EDGE + done, upto - done)], done, upto - done)
        done = upto + reach + 2 * EDGE
    blur_rows(difference, column_tables, blur, reach, psf_count, halves, breadth // LANE)
    for h in range(halves):
        first = (h + 1) * edge - reach
        for t in range(breadth // WIN):
            columns = slice(t * WIN, (t + 1) * WIN)
            ends[h, :, columns] = filtered[first : first + reach + 2 * EDGE, columns] + jnp.dot(
                table[...], blur[h, :, columns], preferred_element_type=F32
            )
        rows = reach + 2 * EDGE if h < halves - 1 else reach + EDGE
        put(ends.at[h, pl.ds(0, rows)], first - EDGE, rows)
    for copy in copies:
        copy.wait()


SMEM = pl.BlockSpec(memory_space=pltpu.SMEM)
HBM = pl.BlockSpec(memory_space=pltpu.HBM)
VMEM = pl.BlockSpec(memory_space=pltpu.VMEM)


def stencil_scratch(count, height, breadth):
    return [
        pltpu.VMEM((height, breadth + LANE), BF16),
        pltpu.VMEM((WIN, count * LANE), BF16),
        pltpu.VMEM((count, LANE, WIN), BF16),
        pltpu.VMEM((count, height + 2 * HALF, WIN), BF16),
    ]


def per_device(blocks, block_patch, block_slot, block_count, template, basis_rows, basis_cols, coeffs, psf_rows, psf_cols):
    n_patch = lax.axis_size("patch")
    n_visit = lax.axis_size("visit")
    local_rows, breadth = template.shape[1:]
    height = local_rows * n_visit
    entries, edge = blocks.shape[2:4]
    halves = height // edge
    slots = halves * (breadth // edge)
    places = n_patch * CAP
    count = basis_rows.shape[0]
    psf_count = psf_rows.shape[1]
    sizes = cuts(edge)
    reaches = sorted(set(sizes[:-1]) - {sizes[-1]})
    most = max(sizes)
    final = sizes[-1]
    dma = pltpu.SemaphoreType.DMA
    handed = pl.pallas_call(
        functools.partial(exchange_kernel, n_patch, n_visit),
        out_shape=(
            jax.ShapeDtypeStruct((height + 2 * EDGE, breadth), F32),
            jax.ShapeDtypeStruct((halves * final, breadth + LANE), BF16),
            jax.ShapeDtypeStruct((WIN, psf_count * LANE), BF16),
            jax.ShapeDtypeStruct((final + 2 * EDGE, psf_count * final), BF16),
        ),
        in_specs=[pl.BlockSpec(memory_space=pl.ANY)] + [HBM] * 9,
        out_specs=(VMEM,) * 4,
        scratch_shapes=[
            pltpu.SMEM((1, 1), jnp.int32),
            pltpu.SMEM((entries,), jnp.int32),
            pltpu.SMEM((entries,), jnp.int32),
            pltpu.SMEM(coeffs.shape, F32),
            pltpu.VMEM(basis_rows.shape, BF16),
            pltpu.VMEM(basis_cols.shape, F32),
            pltpu.VMEM(psf_rows.shape, BF16),
            pltpu.VMEM(psf_cols.shape, BF16),
            dma((8,)),
            pltpu.SMEM((places,), jnp.int32),
            pltpu.VMEM((pl.cdiv(max(count, psf_count), 8) * 8, WIN), F32),
            pltpu.VMEM((places * edge, edge), BF16),
            pltpu.VMEM((places * edge, edge), BF16),
            pltpu.VMEM((n_patch, CAP, LANE), jnp.int32),
            pltpu.VMEM((n_patch, CAP, LANE), jnp.int32),
            pltpu.VMEM((slots * EDGE, places * EDGE), BF16),
            pltpu.VMEM((height, breadth), BF16),
            pltpu.VMEM((height, breadth), F32),
        ]
        + stencil_scratch(count, height, breadth)
        + [
            pltpu.VMEM((halves, psf_count * most, breadth), BF16),
            pltpu.VMEM((halves * most, breadth + LANE), BF16),
        ]
        + [pltpu.VMEM((reach + 2 * EDGE, psf_count * reach), BF16) for reach in reaches]
        + [pltpu.VMEM((entries, size, edge), BF16) for size in sizes]
        + [
            dma((len(sizes),)),
            dma(()),
            dma(()),
            dma((len(sizes),)),
            dma(()),
            dma(()),
            dma(()),
            dma(()),
            pltpu.SemaphoreType.REGULAR((5,)),
        ],
        compiler_params=pltpu.CompilerParams(
            collective_id=0, has_side_effects=True, vmem_limit_bytes=VMEM_LIMIT
        ),
    )(
        block_count,
        *(
            pltpu.with_memory_space_constraint(value, pltpu.HBM)
            for value in (
                block_patch.reshape(entries), block_slot.reshape(entries), coeffs,
                basis_rows, basis_cols, psf_rows, psf_cols, blocks[0, 0], template[0],
            )
        )
    )
    filtered = pl.pallas_call(
        functools.partial(finish_kernel, edge),
        out_shape=jax.ShapeDtypeStruct((height, breadth), F32),
        in_specs=[VMEM] * 4,
        out_specs=HBM,
        scratch_shapes=[
            pltpu.VMEM((halves, psf_count * final, breadth), BF16),
            pltpu.VMEM((halves, final + 2 * EDGE, breadth), F32),
            dma((2 * halves,)),
        ],
        compiler_params=pltpu.CompilerParams(vmem_limit_bytes=16 * 1024 * 1024),
    )(*handed)
    return filtered[None, None]


def solution(mesh):
    return jax.shard_map(
        per_device,
        mesh=mesh,
        in_specs=(
            P("patch", "visit", None, None, None),
            P("patch", "visit", None, None),
            P("patch", "visit", None),
            P("patch", "visit"),
            P("patch", "visit", None),
            P(),
            P(),
            P("visit", None),
            P("visit", None, None),
            P("visit", None, None),
        ),
        out_specs=P("patch", "visit", None, None),
        check_vma=False,
    )
```

```python
import functools

import jax
import jax.numpy as jnp
from jax import lax
from jax.experimental import pallas as pl
from jax.experimental.pallas import tpu as pltpu
from jax.sharding import PartitionSpec as P

CAP = 2
MOST_ROWS = 512
LANE = 128
HALF = 64
EDGE = 16
WIN = 256
F32 = jnp.float32
BF16 = jnp.bfloat16
VMEM_LIMIT = 32 * 1024 * 1024


def toeplitz(row, half_len):
    wide = jnp.broadcast_to(row, (LANE, WIN))
    return pltpu.roll(wide, (HALF - half_len) // 8 * 8, 1, stride=1, stride_axis=0)


def spread(taps, staged):
    count, length = taps.shape
    staged[...] = jnp.zeros(staged.shape, F32)
    staged[:count, :length] = taps
    lead = (HALF - length // 2) % 8
    if lead:
        staged[...] = pltpu.roll(staged[...], lead, 1)


def shift_into(load_tile, shifted, height, tiles, step):
    def body(r, carry):
        rows = pl.ds(pl.multiple_of(r * step, step), step)
        lane = lax.broadcasted_iota(jnp.int32, (step, LANE), 1)
        before = jnp.zeros((step, LANE), F32)
        for t in range(tiles):
            rolled = pltpu.roll(load_tile(rows, t), HALF, 1)
            shifted[rows, t * LANE : (t + 1) * LANE] = jnp.where(lane < HALF, before, rolled).astype(BF16)
            before = rolled
        shifted[rows, tiles * LANE :] = jnp.where(lane < HALF, before, 0.0).astype(BF16)
        return carry

    lax.fori_loop(0, height // step, body, 0)


def columns_pass(shifted, tables, smooth, pair, count, height, margin=HALF):
    for side in range(2):
        start = pl.multiple_of((2 * pair + side) * LANE, LANE)
        window = shifted[:, pl.ds(start, WIN)]
        for group in range(0, count, 2):
            taken = min(2, count - group)
            got = jnp.dot(
                window, tables[:, group * LANE : (group + taken) * LANE], preferred_element_type=F32
            ).astype(BF16)
            for k in range(taken):
                smooth[group + k, margin : margin + height, side * LANE : (side + 1) * LANE] = got[
                    :, k * LANE : (k + 1) * LANE
                ]


def rows_pass(smooth, tables, count, r):
    start = pl.multiple_of(r * LANE, LANE)
    total = jnp.zeros((LANE, WIN), F32)
    for k in range(count):
        total = total + jnp.dot(tables[k], smooth[k, pl.ds(start, WIN), :], preferred_element_type=F32)
    return total


def spread_table(staged, half_len, reach, count):
    wide_rows = reach + 2 * EDGE
    lane = lax.broadcasted_iota(jnp.int32, (wide_rows, WIN), 1)
    joined = jnp.zeros((wide_rows, WIN), F32)
    for k in range(count):
        shift = (k * reach - EDGE - half_len - (HALF - half_len) % 8) % WIN
        wide = jnp.broadcast_to(staged[k : k + 1, :], (wide_rows, WIN))
        rolled = pltpu.roll(wide, shift, 1, stride=1, stride_axis=0)
        joined = jnp.where((lane >= k * reach) & (lane < (k + 1) * reach), rolled, joined)
    return joined[:, : count * reach].astype(BF16)


def build_tables(column_taps, row_taps, column_tables, row_tables, staged):
    spread(column_taps, staged)
    for k in range(column_taps.shape[0]):
        table = toeplitz(staged[k : k + 1, :], column_taps.shape[1] // 2)
        column_tables[:, k * LANE : (k + 1) * LANE] = table.T.astype(BF16)
    spread(row_taps, staged)
    half_len = row_taps.shape[1] // 2
    if isinstance(row_tables, dict):
        for reach, table in row_tables.items():
            table[...] = spread_table(staged, half_len, reach, row_taps.shape[0])
    else:
        for k in range(row_taps.shape[0]):
            row_tables[k] = toeplitz(staged[k : k + 1, :], half_len).astype(BF16)


def clear_edges(smooth, count, height):
    for k in range(count):
        smooth[k, :HALF, :] = jnp.zeros((HALF, smooth.shape[2]), BF16)
        smooth[k, HALF + height :, :] = jnp.zeros((HALF, smooth.shape[2]), BF16)


def cuts(edge):
    return [edge // 8, 3 * edge // 8, edge // 4, edge // 8, edge // 8]


def blur_rows(difference, tables, blur, reach, count, halves, tiles):
    high = halves * reach
    group = max(1, min(tiles, MOST_ROWS // high))

    def some(g, carry):
        begin = [pl.multiple_of((g * group + n) * LANE, LANE) for n in range(group)]
        windows = jnp.concatenate([difference[:high, pl.ds(start, WIN)] for start in begin], axis=0)
        got = jnp.dot(windows, tables[...], preferred_element_type=F32).astype(BF16)
        for n, start in enumerate(begin):
            for h in range(halves):
                rows = slice(n * high + h * reach, n * high + (h + 1) * reach)
                for k in range(count):
                    blur[h, k * reach : (k + 1) * reach, pl.ds(start, LANE)] = got[rows, k * LANE : (k + 1) * LANE]
        return carry

    lax.fori_loop(0, tiles // group, some, 0, unroll=high < LANE)


def exchange_kernel(
    n_patch, n_visit,
    live_in, patch_in, slot_in, coeffs_in, basis_rows_in, basis_cols_in, psf_rows_in, psf_cols_in, blocks, template,
    filtered, last_difference, psf_column_tables, last_table,
    live, patch, slot, coeffs, basis_rows, basis_cols, psf_rows, psf_cols, small_sems, sources, staged, outgoing, arrived, labels_out, labels_in, picks, whole, total, shifted, column_tables, row_tables, smooth, blur, part_difference, *rest,
):
    sizes = cuts(blocks.shape[1])
    reaches = sorted(set(sizes[:-1]) - {sizes[-1]})
    tables_of = dict(zip(reaches, rest[: len(reaches)]))
    tables_of[sizes[-1]] = last_table
    raw = rest[len(reaches) : len(reaches) + len(sizes)]
    load_sem, own_sem, block_send, block_recv, label_send, label_recv, rows_send, rows_recv, told = rest[
        len(reaches) + len(sizes) :
    ]
    me = lax.axis_index("patch")
    my_visit = lax.axis_index("visit")
    local_rows, breadth = template.shape
    height = local_rows * n_visit
    entries, edge = blocks.shape[:2]
    places = n_patch * CAP
    count = basis_rows.shape[0]
    psf_count = psf_rows.shape[1]
    wide = breadth // edge
    halves = height // edge
    slots = halves * wide
    chips = n_patch // 2
    chip, core = me // 2, lax.rem(me, 2)
    sibling = 2 * chip + 1 - core
    starts = [sum(sizes[:c]) for c in range(len(sizes))]
    visits = [lax.rem(my_visit + hop, n_visit) for hop in range(1, n_visit)]

    def tell(semaphore, peer):
        pl.semaphore_signal(semaphore, inc=1, device_id={"patch": peer}, device_id_type=pl.DeviceIdType.MESH)

    def tell_visit(semaphore, visit):
        pl.semaphore_signal(semaphore, inc=1, device_id={"visit": visit}, device_id_type=pl.DeviceIdType.MESH)

    small = [
        pltpu.make_async_copy(source, held, small_sems.at[i])
        for i, (source, held) in enumerate(
            (
                (live_in, live), (patch_in, patch), (slot_in, slot), (coeffs_in, coeffs),
                (basis_rows_in, basis_rows), (basis_cols_in, basis_cols),
                (psf_rows_in, psf_rows), (psf_cols_in, psf_cols),
            )
        )
    ]
    staged_entry = chips == 4
    near_side = chip < chips // 2
    middle = (chip == chips // 2) | (chip == chips // 2 - 1)
    inner = jnp.where(near_side, chip + 1, chip - 1)
    outer = jnp.where(near_side, chip - 1, chip + 1)
    other = jnp.where(near_side, chip + 2, chip - 2)
    mirror = chips - 1 - chip
    barrier = pltpu.get_barrier_semaphore()
    if staged_entry:

        @pl.when(middle)
        def _():
            for there in inner, outer:
                for c in range(2):
                    tell(barrier, 2 * there + c)

        tell(barrier, sibling)

        @pl.when(jnp.logical_not(middle))
        def _():
            for visit in visits:
                tell_visit(barrier, visit)

        greeted = 3 + jnp.where(middle, 0, n_visit - 1)
    else:
        for hop in range(1, n_patch):
            tell(barrier, lax.rem(me + hop, n_patch))
        for visit in visits:
            tell_visit(barrier, visit)
        greeted = n_patch + n_visit - 2
    for copy in small[:3]:
        copy.start()
    loads = [
        pltpu.make_async_copy(blocks.at[:, pl.ds(starts[c], sizes[c])], raw[c], load_sem.at[c])
        for c in range(len(sizes))
    ]
    for copy in loads + small[3:]:
        copy.start()
    my_rows = pl.ds(pl.multiple_of(my_visit * local_rows, local_rows), local_rows)
    own = pltpu.make_async_copy(template, whole.at[my_rows], own_sem)
    own.start()

    for copy in small[:3]:
        copy.wait()
    targets = [patch[i] for i in range(entries)]
    marks = [jnp.where(i < live[0, 0], slot[i], -1) for i in range(entries)]

    def find(d, carry):
        first, last, first_mark, last_mark = (jnp.int32(0), jnp.int32(-1), jnp.int32(-1), jnp.int32(-1))
        for i in range(entries):
            last = jnp.where(targets[i] == d, i, last)
            last_mark = jnp.where(targets[i] == d, marks[i], last_mark)
        for i in reversed(range(entries)):
            first = jnp.where(targets[i] == d, i, first)
            first_mark = jnp.where(targets[i] == d, marks[i], first_mark)
        labels = (first_mark, jnp.where(first < last, last_mark, -1))
        for c, (source, label) in enumerate(zip((first, jnp.maximum(last, 0)), labels)):
            sources[d * CAP + c] = source
            labels_out[d, c : c + 1, :] = jnp.full((1, LANE), label, jnp.int32)
        return carry

    def rows_of(c, place, number=1):
        return pl.ds(pl.multiple_of(places * starts[c] + place * sizes[c], EDGE), number * sizes[c])

    def pack(c, first, number):
        def one(i, carry):
            outgoing[rows_of(c, first + i), :] = raw[c][sources[first + i]]
            return carry

        lax.fori_loop(0, number, one, 0)

    if staged_entry:
        turns = [
            jnp.where(middle, inner, other), jnp.where(middle, other, mirror), jnp.where(middle, outer, inner), chip,
        ]
    else:
        turns = [lax.rem(chip + hop, chips) for hop in range(chips - 1, -1, -1)]
    find(2 * turns[0], 0)
    find(2 * turns[0] + 1, 0)
    loads[0].wait()
    pack(0, 2 * turns[0] * CAP, 2 * CAP)
    pl.semaphore_wait(barrier, greeted)

    row_copies = [
        pltpu.make_async_remote_copy(
            src_ref=template, dst_ref=whole.at[my_rows],
            send_sem=rows_send, recv_sem=rows_recv,
            device_id={"visit": visit}, device_id_type=pl.DeviceIdType.MESH,
        )
        for hop, visit in enumerate(visits)
    ]

    def landed(held, semaphore):
        pltpu.make_async_copy(held, held, semaphore).wait()

    def label_copy(peer):
        return pltpu.make_async_remote_copy(
            src_ref=labels_out.at[peer], dst_ref=labels_in.at[me],
            send_sem=label_send, recv_sem=label_recv,
            device_id={"patch": peer}, device_id_type=pl.DeviceIdType.MESH,
        )

    def block_copy(peer, c):
        return pltpu.make_async_remote_copy(
            src_ref=outgoing.at[rows_of(c, peer * CAP, CAP)], dst_ref=arrived.at[rows_of(c, me * CAP, CAP)],
            send_sem=block_send, recv_sem=block_recv.at[c],
            device_id={"patch": peer}, device_id_type=pl.DeviceIdType.MESH,
        )

    def send(peer, c):
        block_copy(peer, c).start()
        if c == 0:
            label_copy(peer).start()

    def send_chip(there, c):
        send(2 * there + 1, c)
        send(2 * there, c)

    early, late = range(len(sizes) - 3), range(len(sizes) - 3, len(sizes))

    def pack_rest():
        for turn in turns[1:]:
            lax.fori_loop(2 * turn, 2 * turn + 2, find, 0)
            pack(0, 2 * turn * CAP, 2 * CAP)
            if staged_entry:
                pack(1, 2 * turn * CAP, 2 * CAP)
        for c in range(2 if staged_entry else 1, len(sizes)):
            loads[c].wait()
            pack(c, 0, places)

    if staged_entry:

        @pl.when(middle)
        def _():
            send_chip(inner, 0)

        loads[1].wait()
        pack(1, 2 * turns[0] * CAP, 2 * CAP)

        @pl.when(middle)
        def _():
            send_chip(inner, 1)

        @pl.when(jnp.logical_not(middle))
        def _():
            for c in range(2):
                tell(told.at[0], 2 * inner + c)
            for visit in visits:
                tell_visit(told.at[3], visit)
            for copy in row_copies:
                copy.start()

        @pl.when(middle)
        def _():
            pl.semaphore_wait(told.at[0], 2)
            tell(told.at[1], 2 * outer + core)
            tell(told.at[1], 2 * inner + core)

        pack_rest()

        @pl.when(middle)
        def _():
            pl.semaphore_wait(told.at[1], 1)
            tell(told.at[2], 2 * outer + core)
            for steps in early, late:
                for c in steps:
                    send_chip(other, c)
                    send_chip(outer, c)
                    send(sibling, c)
                    if c > 1 and steps is early:
                        send_chip(inner, c)
            for c in late:
                if c > 1:
                    send_chip(inner, c)
            pl.semaphore_wait(told.at[4], 1)
            for copy in row_copies:
                copy.start()

        @pl.when(jnp.logical_not(middle))
        def _():
            pl.semaphore_wait(told.at[1], 1)
            send_chip(other, 0)
            pl.semaphore_wait(told.at[3], n_visit - 1)
            tell(told.at[4], 2 * inner + core)
            pl.semaphore_wait(told.at[2], 1)
            for steps in early, late:
                for c in steps:
                    send_chip(mirror, c)
                    if steps is early:
                        if c:
                            send_chip(other, c)
                        send_chip(inner, c)
                    send(sibling, c)
            for c in late:
                send_chip(other, c)
                send_chip(inner, c)

    else:
        for copy in row_copies:
            copy.start()
        for turn in turns[:1]:
            send_chip(turn, 0)
        pack_rest()
        for c in range(len(sizes)):
            for turn in turns[(1 if c == 0 else 0) : -1]:
                send_chip(turn, c)
            send(sibling, c)

    labels_in[me] = labels_out[me]
    for c in range(len(sizes)):
        arrived[rows_of(c, me * CAP, CAP), :] = outgoing[rows_of(c, me * CAP, CAP), :]
    for copy in small[3:]:
        copy.wait()
    scaled = jnp.concatenate(
        [(coeffs[0, k] * basis_cols[k : k + 1, :]).astype(BF16).astype(F32) for k in range(count)], axis=0
    )
    build_tables(basis_rows[...].astype(F32), scaled, column_tables, row_tables, staged)
    build_tables(psf_rows[0].astype(F32), psf_cols[0].astype(F32), psf_column_tables, tables_of, staged)
    clear_edges(smooth, count, height)

    def clear(r, carry):
        filtered[pl.ds(pl.multiple_of(r * EDGE, EDGE), EDGE), :] = jnp.zeros((EDGE, breadth), F32)
        return carry

    lax.fori_loop(0, height // EDGE + 2, clear, 0)
    own.wait()
    landed(whole.at[pl.ds(0, (n_visit - 1) * local_rows)], rows_recv)
    shift_into(
        lambda rows, t: whole[rows, t * LANE : (t + 1) * LANE].astype(F32),
        shifted, height, breadth // LANE, 32,
    )

    def per_pair(pair, carry):
        columns_pass(shifted, column_tables, smooth, pair, count, height)

        def per_row(r, inside):
            rows = pl.ds(pl.multiple_of(r * LANE, LANE), LANE)
            columns = pl.ds(pl.multiple_of(pair * WIN, WIN), WIN)
            total[rows, columns] = -rows_pass(smooth, row_tables, count, r)
            return inside

        return lax.fori_loop(0, height // LANE, per_row, carry)

    lax.fori_loop(0, breadth // WIN, per_pair, 0)

    landed(labels_in.at[pl.ds(0, n_patch - 1)], label_recv)
    for first in range(0, places, LANE // EDGE):
        lane = lax.broadcasted_iota(jnp.int32, (8, LANE), 1)
        named = jnp.full((8, LANE), -1, jnp.int32)
        for p in range(LANE // EDGE):
            place = first + p
            mark = jnp.broadcast_to(labels_in[place // CAP, place % CAP : place % CAP + 1, :], (8, LANE))
            named = jnp.where((lane >= p * EDGE) & (lane < (p + 1) * EDGE), mark, named)
        named = jnp.concatenate([named] * (EDGE // 8), axis=0)
        lane = lax.broadcasted_iota(jnp.int32, (EDGE, LANE), 1)
        same = lax.rem(lane, EDGE) == lax.broadcasted_iota(jnp.int32, (EDGE, LANE), 0)
        for s in range(slots):
            picks[s * EDGE : (s + 1) * EDGE, first * EDGE : first * EDGE + LANE] = jnp.where(
                same & (named == s), 1.0, 0.0
            ).astype(BF16)

    for c, reach in enumerate(sizes):
        landed(arrived.at[rows_of(c, 0, places - CAP)], block_recv.at[c])

        def add(r, carry, c=c):
            pieces = jnp.concatenate(
                [
                    arrived[pl.ds(pl.multiple_of(places * starts[c] + p * sizes[c] + r * EDGE, EDGE), EDGE), :]
                    for p in range(places)
                ],
                axis=0,
            )
            summed = jnp.dot(picks[...], pieces, preferred_element_type=F32)
            for s in range(slots):
                rows = pl.ds(pl.multiple_of(s // wide * edge + starts[c] + r * EDGE, EDGE), EDGE)
                columns = slice(s % wide * edge, (s % wide + 1) * edge)
                total[rows, columns] += summed[s * EDGE : (s + 1) * EDGE]
            return carry

        lax.fori_loop(0, reach // EDGE, add, 0, unroll=reach < LANE)
        last = c == len(sizes) - 1
        held = last_difference if last else part_difference

        def shift(r, carry, c=c, held=held):
            lane = lax.broadcasted_iota(jnp.int32, (EDGE, LANE), 1)
            for h in range(halves):
                source = pl.ds(pl.multiple_of(h * edge + starts[c] + r * EDGE, EDGE), EDGE)
                rows = pl.ds(pl.multiple_of(h * sizes[c] + r * EDGE, EDGE), EDGE)
                before = jnp.zeros((EDGE, LANE), F32)
                for t in range(breadth // LANE):
                    rolled = pltpu.roll(total[source, t * LANE : (t + 1) * LANE], HALF, 1)
                    held[rows, t * LANE : (t + 1) * LANE] = jnp.where(lane < HALF, before, rolled).astype(BF16)
                    before = rolled
                held[rows, breadth:] = jnp.where(lane < HALF, before, 0.0).astype(BF16)
            return carry

        lax.fori_loop(0, reach // EDGE, shift, 0, unroll=reach < LANE)
        if last:
            continue

        blur_rows(part_difference, psf_column_tables, blur, reach, psf_count, halves, breadth // LANE)

        def gather(t, carry, c=c, reach=reach):
            columns = pl.ds(pl.multiple_of(t * WIN, WIN), WIN)
            for h in range(halves):
                rows = slice(h * edge + starts[c], h * edge + starts[c] + reach + 2 * EDGE)
                filtered[rows, columns] += jnp.dot(
                    tables_of[reach][...], blur[h, : psf_count * reach, columns], preferred_element_type=F32
                )
            return carry

        lax.fori_loop(0, breadth // WIN, gather, 0, unroll=halves * reach <= LANE)

    landed(whole.at[pl.ds(0, (n_visit - 1) * local_rows)], rows_send)
    landed(labels_out.at[pl.ds(0, n_patch - 1)], label_send)
    landed(outgoing.at[pl.ds(0, (places - CAP) * edge)], block_send)


def finish_kernel(edge, filtered, difference, column_tables, table, out, blur, ends, sem):
    height, breadth = out.shape
    halves = height // edge
    psf_count = column_tables.shape[1] // LANE
    reach = difference.shape[0] // halves

    def put(source, first, rows):
        pltpu.make_async_copy(source, out.at[pl.ds(first, rows)], sem).start()

    done = 0
    for h in range(halves):
        upto = (h + 1) * edge - reach - EDGE
        piece = edge // 4
        for first in range(done, upto, piece):
            rows = min(piece, upto - first)
            put(filtered.at[pl.ds(EDGE + first, rows)], first, rows)
        done = upto + reach + 2 * EDGE
    blur_rows(difference, column_tables, blur, reach, psf_count, halves, breadth // LANE)
    for h in range(halves):
        first = (h + 1) * edge - reach
        for t in range(breadth // WIN):
            columns = slice(t * WIN, (t + 1) * WIN)
            ends[h, :, columns] = filtered[first : first + reach + 2 * EDGE, columns] + jnp.dot(
                table[...], blur[h, :, columns], preferred_element_type=F32
            )
        rows = reach + 2 * EDGE if h < halves - 1 else reach + EDGE
        put(ends.at[h, pl.ds(0, rows)], first - EDGE, rows)
    pltpu.make_async_copy(out, out, sem).wait()


SMEM = pl.BlockSpec(memory_space=pltpu.SMEM)
HBM = pl.BlockSpec(memory_space=pltpu.HBM)
VMEM = pl.BlockSpec(memory_space=pltpu.VMEM)


def stencil_scratch(count, height, breadth):
    return [
        pltpu.VMEM((height, breadth + LANE), BF16),
        pltpu.VMEM((WIN, count * LANE), BF16),
        pltpu.VMEM((count, LANE, WIN), BF16),
        pltpu.VMEM((count, height + 2 * HALF, WIN), BF16),
    ]


def per_device(blocks, block_patch, block_slot, block_count, template, basis_rows, basis_cols, coeffs, psf_rows, psf_cols):
    n_patch = lax.axis_size("patch")
    n_visit = lax.axis_size("visit")
    local_rows, breadth = template.shape[1:]
    height = local_rows * n_visit
    entries, edge = blocks.shape[2:4]
    halves = height // edge
    slots = halves * (breadth // edge)
    places = n_patch * CAP
    count = basis_rows.shape[0]
    psf_count = psf_rows.shape[1]
    sizes = cuts(edge)
    reaches = sorted(set(sizes[:-1]) - {sizes[-1]})
    most = max(sizes)
    final = sizes[-1]
    dma = pltpu.SemaphoreType.DMA
    handed = pl.pallas_call(
        functools.partial(exchange_kernel, n_patch, n_visit),
        out_shape=(
            jax.ShapeDtypeStruct((height + 2 * EDGE, breadth), F32),
            jax.ShapeDtypeStruct((halves * final, breadth + LANE), BF16),
            jax.ShapeDtypeStruct((WIN, psf_count * LANE), BF16),
            jax.ShapeDtypeStruct((final + 2 * EDGE, psf_count * final), BF16),
        ),
        in_specs=[pl.BlockSpec(memory_space=pl.ANY)] + [HBM] * 9,
        out_specs=(VMEM,) * 4,
        scratch_shapes=[
            pltpu.SMEM((1, 1), jnp.int32),
            pltpu.SMEM((entries,), jnp.int32),
            pltpu.SMEM((entries,), jnp.int32),
            pltpu.SMEM(coeffs.shape, F32),
            pltpu.VMEM(basis_rows.shape, BF16),
            pltpu.VMEM(basis_cols.shape, F32),
            pltpu.VMEM(psf_rows.shape, BF16),
            pltpu.VMEM(psf_cols.shape, BF16),
            dma((8,)),
            pltpu.SMEM((places,), jnp.int32),
            pltpu.VMEM((pl.cdiv(max(count, psf_count), 8) * 8, WIN), F32),
            pltpu.VMEM((places * edge, edge), BF16),
            pltpu.VMEM((places * edge, edge), BF16),
            pltpu.VMEM((n_patch, CAP, LANE), jnp.int32),
            pltpu.VMEM((n_patch, CAP, LANE), jnp.int32),
            pltpu.VMEM((slots * EDGE, places * EDGE), BF16),
            pltpu.VMEM((height, breadth), BF16),
            pltpu.VMEM((height, breadth), F32),
        ]
        + stencil_scratch(count, height, breadth)
        + [
            pltpu.VMEM((halves, psf_count * most, breadth), BF16),
            pltpu.VMEM((halves * most, breadth + LANE), BF16),
        ]
        + [pltpu.VMEM((reach + 2 * EDGE, psf_count * reach), BF16) for reach in reaches]
        + [pltpu.VMEM((entries, size, edge), BF16) for size in sizes]
        + [
            dma((len(sizes),)),
            dma(()),
            dma(()),
            dma((len(sizes),)),
            dma(()),
            dma(()),
            dma(()),
            dma(()),
            pltpu.SemaphoreType.REGULAR((5,)),
        ],
        compiler_params=pltpu.CompilerParams(
            collective_id=0, has_side_effects=True, vmem_limit_bytes=VMEM_LIMIT
        ),
    )(
        block_count,
        *(
            pltpu.with_memory_space_constraint(value, pltpu.HBM)
            for value in (
                block_patch.reshape(entries), block_slot.reshape(entries), coeffs,
                basis_rows, basis_cols, psf_rows, psf_cols, blocks[0, 0], template[0],
            )
        )
    )
    filtered = pl.pallas_call(
        functools.partial(finish_kernel, edge),
        out_shape=jax.ShapeDtypeStruct((height, breadth), F32),
        in_specs=[VMEM] * 4,
        out_specs=HBM,
        scratch_shapes=[
            pltpu.VMEM((halves, psf_count * final, breadth), BF16),
            pltpu.VMEM((halves, final + 2 * EDGE, breadth), F32),
            dma(()),
        ],
        compiler_params=pltpu.CompilerParams(vmem_limit_bytes=16 * 1024 * 1024),
    )(*handed)
    return filtered[None, None]


def solution(mesh):
    return jax.shard_map(
        per_device,
        mesh=mesh,
        in_specs=(
            P("patch", "visit", None, None, None),
            P("patch", "visit", None, None),
            P("patch", "visit", None),
            P("patch", "visit"),
            P("patch", "visit", None),
            P(),
            P(),
            P("visit", None),
            P("visit", None, None),
            P("visit", None, None),
        ),
        out_specs=P("patch", "visit", None, None),
        check_vma=False,
    )
```

```python
import functools

import jax
import jax.numpy as jnp
from jax import lax
from jax.experimental import pallas as pl
from jax.experimental.pallas import tpu as pltpu
from jax.sharding import PartitionSpec as P

CAP = 2
MOST_ROWS = 512
LANE = 128
HALF = 64
EDGE = 16
WIN = 256
F32 = jnp.float32
BF16 = jnp.bfloat16
VMEM_LIMIT = 32 * 1024 * 1024


def toeplitz(row, half_len):
    wide = jnp.broadcast_to(row, (LANE, WIN))
    return pltpu.roll(wide, (HALF - half_len) // 8 * 8, 1, stride=1, stride_axis=0)


def spread(taps, staged):
    count, length = taps.shape
    staged[...] = jnp.zeros(staged.shape, F32)
    staged[:count, :length] = taps
    lead = (HALF - length // 2) % 8
    if lead:
        staged[...] = pltpu.roll(staged[...], lead, 1)


def shift_into(load_tile, shifted, height, tiles, step):
    def body(r, carry):
        rows = pl.ds(pl.multiple_of(r * step, step), step)
        lane = lax.broadcasted_iota(jnp.int32, (step, LANE), 1)
        before = jnp.zeros((step, LANE), F32)
        for t in range(tiles):
            rolled = pltpu.roll(load_tile(rows, t), HALF, 1)
            shifted[rows, t * LANE : (t + 1) * LANE] = jnp.where(lane < HALF, before, rolled).astype(BF16)
            before = rolled
        shifted[rows, tiles * LANE :] = jnp.where(lane < HALF, before, 0.0).astype(BF16)
        return carry

    lax.fori_loop(0, height // step, body, 0)


def columns_pass(shifted, tables, smooth, pair, count, height, margin=HALF):
    for side in range(2):
        start = pl.multiple_of((2 * pair + side) * LANE, LANE)
        window = shifted[:, pl.ds(start, WIN)]
        for group in range(0, count, 2):
            taken = min(2, count - group)
            got = jnp.dot(
                window, tables[:, group * LANE : (group + taken) * LANE], preferred_element_type=F32
            ).astype(BF16)
            for k in range(taken):
                smooth[group + k, margin : margin + height, side * LANE : (side + 1) * LANE] = got[
                    :, k * LANE : (k + 1) * LANE
                ]


def rows_pass(smooth, tables, count, r):
    start = pl.multiple_of(r * LANE, LANE)
    total = jnp.zeros((LANE, WIN), F32)
    for k in range(count):
        total = total + jnp.dot(tables[k], smooth[k, pl.ds(start, WIN), :], preferred_element_type=F32)
    return total


def spread_table(staged, half_len, reach, count):
    wide_rows = reach + 2 * EDGE
    lane = lax.broadcasted_iota(jnp.int32, (wide_rows, WIN), 1)
    joined = jnp.zeros((wide_rows, WIN), F32)
    for k in range(count):
        shift = (k * reach - EDGE - half_len - (HALF - half_len) % 8) % WIN
        wide = jnp.broadcast_to(staged[k : k + 1, :], (wide_rows, WIN))
        rolled = pltpu.roll(wide, shift, 1, stride=1, stride_axis=0)
        joined = jnp.where((lane >= k * reach) & (lane < (k + 1) * reach), rolled, joined)
    return joined[:, : count * reach].astype(BF16)


def build_tables(column_taps, row_taps, column_tables, row_tables, staged):
    spread(column_taps, staged)
    for k in range(column_taps.shape[0]):
        table = toeplitz(staged[k : k + 1, :], column_taps.shape[1] // 2)
        column_tables[:, k * LANE : (k + 1) * LANE] = table.T.astype(BF16)
    spread(row_taps, staged)
    half_len = row_taps.shape[1] // 2
    if isinstance(row_tables, dict):
        for reach, table in row_tables.items():
            table[...] = spread_table(staged, half_len, reach, row_taps.shape[0])
    else:
        for k in range(row_taps.shape[0]):
            row_tables[k] = toeplitz(staged[k : k + 1, :], half_len).astype(BF16)


def clear_edges(smooth, count, height):
    for k in range(count):
        smooth[k, :HALF, :] = jnp.zeros((HALF, smooth.shape[2]), BF16)
        smooth[k, HALF + height :, :] = jnp.zeros((HALF, smooth.shape[2]), BF16)


def cuts(edge):
    return [edge // 8, 3 * edge // 8, edge // 4, edge // 8, edge // 8]


def blur_rows(difference, tables, blur, reach, count, halves, tiles):
    high = halves * reach
    group = max(1, min(tiles, MOST_ROWS // high))

    def some(g, carry):
        begin = [pl.multiple_of((g * group + n) * LANE, LANE) for n in range(group)]
        windows = jnp.concatenate([difference[:high, pl.ds(start, WIN)] for start in begin], axis=0)
        got = jnp.dot(windows, tables[...], preferred_element_type=F32).astype(BF16)
        for n, start in enumerate(begin):
            for h in range(halves):
                rows = slice(n * high + h * reach, n * high + (h + 1) * reach)
                for k in range(count):
                    blur[h, k * reach : (k + 1) * reach, pl.ds(start, LANE)] = got[rows, k * LANE : (k + 1) * LANE]
        return carry

    lax.fori_loop(0, tiles // group, some, 0, unroll=high < LANE)


def exchange_kernel(
    n_patch, n_visit,
    live_in, patch_in, slot_in, coeffs_in, basis_rows_in, basis_cols_in, psf_rows_in, psf_cols_in, blocks, template,
    filtered, last_difference, psf_column_tables, last_table,
    live, patch, slot, coeffs, basis_rows, basis_cols, psf_rows, psf_cols, small_sems, sources, staged, outgoing, arrived, labels_out, labels_in, picks, whole, total, shifted, column_tables, row_tables, smooth, blur, part_difference, *rest,
):
    sizes = cuts(blocks.shape[1])
    reaches = sorted(set(sizes[:-1]) - {sizes[-1]})
    tables_of = dict(zip(reaches, rest[: len(reaches)]))
    tables_of[sizes[-1]] = last_table
    raw = rest[len(reaches) : len(reaches) + len(sizes)]
    load_sem, own_sem, block_send, block_recv, label_send, label_recv, rows_send, rows_recv, told = rest[
        len(reaches) + len(sizes) :
    ]
    me = lax.axis_index("patch")
    my_visit = lax.axis_index("visit")
    local_rows, breadth = template.shape
    height = local_rows * n_visit
    entries, edge = blocks.shape[:2]
    places = n_patch * CAP
    count = basis_rows.shape[0]
    psf_count = psf_rows.shape[1]
    wide = breadth // edge
    halves = height // edge
    slots = halves * wide
    chips = n_patch // 2
    chip, core = me // 2, lax.rem(me, 2)
    sibling = 2 * chip + 1 - core
    starts = [sum(sizes[:c]) for c in range(len(sizes))]
    visits = [lax.rem(my_visit + hop, n_visit) for hop in range(1, n_visit)]

    def tell(semaphore, peer):
        pl.semaphore_signal(semaphore, inc=1, device_id={"patch": peer}, device_id_type=pl.DeviceIdType.MESH)

    def tell_visit(semaphore, visit):
        pl.semaphore_signal(semaphore, inc=1, device_id={"visit": visit}, device_id_type=pl.DeviceIdType.MESH)

    small = [
        pltpu.make_async_copy(source, held, small_sems.at[i])
        for i, (source, held) in enumerate(
            (
                (live_in, live), (patch_in, patch), (slot_in, slot), (coeffs_in, coeffs),
                (basis_rows_in, basis_rows), (basis_cols_in, basis_cols),
                (psf_rows_in, psf_rows), (psf_cols_in, psf_cols),
            )
        )
    ]
    staged_entry = chips == 4
    near_side = chip < chips // 2
    middle = (chip == chips // 2) | (chip == chips // 2 - 1)
    inner = jnp.where(near_side, chip + 1, chip - 1)
    outer = jnp.where(near_side, chip - 1, chip + 1)
    other = jnp.where(near_side, chip + 2, chip - 2)
    mirror = chips - 1 - chip
    barrier = pltpu.get_barrier_semaphore()
    if staged_entry:

        @pl.when(middle)
        def _():
            for there in inner, outer:
                for c in range(2):
                    tell(barrier, 2 * there + c)

        tell(barrier, sibling)

        @pl.when(jnp.logical_not(middle))
        def _():
            for visit in visits:
                tell_visit(barrier, visit)

        greeted = 3 + jnp.where(middle, 0, n_visit - 1)
    else:
        for hop in range(1, n_patch):
            tell(barrier, lax.rem(me + hop, n_patch))
        for visit in visits:
            tell_visit(barrier, visit)
        greeted = n_patch + n_visit - 2
    for copy in small[:3]:
        copy.start()
    loads = [
        pltpu.make_async_copy(blocks.at[:, pl.ds(starts[c], sizes[c])], raw[c], load_sem.at[c])
        for c in range(len(sizes))
    ]
    for copy in loads + small[3:]:
        copy.start()
    my_rows = pl.ds(pl.multiple_of(my_visit * local_rows, local_rows), local_rows)
    own = pltpu.make_async_copy(template, whole.at[my_rows], own_sem)
    own.start()

    for copy in small[:3]:
        copy.wait()
    targets = [patch[i] for i in range(entries)]
    marks = [jnp.where(i < live[0, 0], slot[i], -1) for i in range(entries)]

    def find(d, carry):
        first, last, first_mark, last_mark = (jnp.int32(0), jnp.int32(-1), jnp.int32(-1), jnp.int32(-1))
        for i in range(entries):
            last = jnp.where(targets[i] == d, i, last)
            last_mark = jnp.where(targets[i] == d, marks[i], last_mark)
        for i in reversed(range(entries)):
            first = jnp.where(targets[i] == d, i, first)
            first_mark = jnp.where(targets[i] == d, marks[i], first_mark)
        labels = (first_mark, jnp.where(first < last, last_mark, -1))
        for c, (source, label) in enumerate(zip((first, jnp.maximum(last, 0)), labels)):
            sources[d * CAP + c] = source
            labels_out[d, c : c + 1, :] = jnp.full((1, LANE), label, jnp.int32)
        return carry

    def rows_of(c, place, number=1):
        return pl.ds(pl.multiple_of(places * starts[c] + place * sizes[c], EDGE), number * sizes[c])

    def pack(c, first, number):
        def one(i, carry):
            outgoing[rows_of(c, first + i), :] = raw[c][sources[first + i]]
            return carry

        lax.fori_loop(0, number, one, 0)

    if staged_entry:
        turns = [
            jnp.where(middle, inner, other), jnp.where(middle, other, mirror), jnp.where(middle, outer, inner), chip,
        ]
    else:
        turns = [lax.rem(chip + hop, chips) for hop in range(chips - 1, -1, -1)]
    find(2 * turns[0], 0)
    find(2 * turns[0] + 1, 0)
    loads[0].wait()
    pack(0, 2 * turns[0] * CAP, 2 * CAP)
    pl.semaphore_wait(barrier, greeted)

    row_copies = [
        pltpu.make_async_remote_copy(
            src_ref=template, dst_ref=whole.at[my_rows],
            send_sem=rows_send, recv_sem=rows_recv,
            device_id={"visit": visit}, device_id_type=pl.DeviceIdType.MESH,
        )
        for hop, visit in enumerate(visits)
    ]

    def landed(held, semaphore):
        pltpu.make_async_copy(held, held, semaphore).wait()

    def label_copy(peer):
        return pltpu.make_async_remote_copy(
            src_ref=labels_out.at[peer], dst_ref=labels_in.at[me],
            send_sem=label_send, recv_sem=label_recv,
            device_id={"patch": peer}, device_id_type=pl.DeviceIdType.MESH,
        )

    def block_copy(peer, c):
        return pltpu.make_async_remote_copy(
            src_ref=outgoing.at[rows_of(c, peer * CAP, CAP)], dst_ref=arrived.at[rows_of(c, me * CAP, CAP)],
            send_sem=block_send, recv_sem=block_recv.at[c],
            device_id={"patch": peer}, device_id_type=pl.DeviceIdType.MESH,
        )

    def send(peer, c):
        block_copy(peer, c).start()
        if c == 0:
            label_copy(peer).start()

    def send_chip(there, c):
        send(2 * there + 1, c)
        send(2 * there, c)

    early, late = range(len(sizes) - 3), range(len(sizes) - 3, len(sizes))

    def pack_rest():
        for turn in turns[1:]:
            lax.fori_loop(2 * turn, 2 * turn + 2, find, 0)
            pack(0, 2 * turn * CAP, 2 * CAP)
            if staged_entry:
                pack(1, 2 * turn * CAP, 2 * CAP)
        for c in range(2 if staged_entry else 1, len(sizes)):
            loads[c].wait()
            pack(c, 0, places)

    if staged_entry:

        @pl.when(middle)
        def _():
            send_chip(inner, 0)

        loads[1].wait()
        pack(1, 2 * turns[0] * CAP, 2 * CAP)

        @pl.when(middle)
        def _():
            send_chip(inner, 1)

        @pl.when(jnp.logical_not(middle))
        def _():
            for c in range(2):
                tell(told.at[0], 2 * inner + c)
            for visit in visits:
                tell_visit(told.at[3], visit)
            for copy in row_copies:
                copy.start()

        @pl.when(middle)
        def _():
            pl.semaphore_wait(told.at[0], 2)
            tell(told.at[1], 2 * outer + core)
            tell(told.at[1], 2 * inner + core)

        pack_rest()

        @pl.when(middle)
        def _():
            pl.semaphore_wait(told.at[1], 1)
            tell(told.at[2], 2 * outer + core)
            for steps in early, late:
                for c in steps:
                    send_chip(other, c)
                    send_chip(outer, c)
                    send(sibling, c)
                    if c > 1 and steps is early:
                        send_chip(inner, c)
            for c in late:
                if c > 1:
                    send_chip(inner, c)
            pl.semaphore_wait(told.at[4], 1)
            for copy in row_copies:
                copy.start()

        @pl.when(jnp.logical_not(middle))
        def _():
            pl.semaphore_wait(told.at[1], 1)
            send_chip(other, 0)
            pl.semaphore_wait(told.at[3], n_visit - 1)
            tell(told.at[4], 2 * inner + core)
            pl.semaphore_wait(told.at[2], 1)
            for steps in early, late:
                for c in steps:
                    send_chip(mirror, c)
                    if steps is early:
                        if c:
                            send_chip(other, c)
                        send_chip(inner, c)
                    send(sibling, c)
            for c in late:
                send_chip(other, c)
                send_chip(inner, c)

    else:
        for copy in row_copies:
            copy.start()
        for turn in turns[:1]:
            send_chip(turn, 0)
        pack_rest()
        for c in range(len(sizes)):
            for turn in turns[(1 if c == 0 else 0) : -1]:
                send_chip(turn, c)
            send(sibling, c)

    labels_in[me] = labels_out[me]
    for c in range(len(sizes)):
        arrived[rows_of(c, me * CAP, CAP), :] = outgoing[rows_of(c, me * CAP, CAP), :]
    for copy in small[3:]:
        copy.wait()
    scaled = jnp.concatenate(
        [(coeffs[0, k] * basis_cols[k : k + 1, :]).astype(BF16).astype(F32) for k in range(count)], axis=0
    )
    build_tables(basis_rows[...].astype(F32), scaled, column_tables, row_tables, staged)
    build_tables(psf_rows[0].astype(F32), psf_cols[0].astype(F32), psf_column_tables, tables_of, staged)
    clear_edges(smooth, count, height)

    def clear(r, carry):
        filtered[pl.ds(pl.multiple_of(r * EDGE, EDGE), EDGE), :] = jnp.zeros((EDGE, breadth), F32)
        return carry

    lax.fori_loop(0, height // EDGE + 2, clear, 0)
    own.wait()
    landed(whole.at[pl.ds(0, (n_visit - 1) * local_rows)], rows_recv)
    shift_into(
        lambda rows, t: whole[rows, t * LANE : (t + 1) * LANE].astype(F32),
        shifted, height, breadth // LANE, 32,
    )

    def per_pair(pair, carry):
        columns_pass(shifted, column_tables, smooth, pair, count, height)

        def per_row(r, inside):
            rows = pl.ds(pl.multiple_of(r * LANE, LANE), LANE)
            columns = pl.ds(pl.multiple_of(pair * WIN, WIN), WIN)
            total[rows, columns] = -rows_pass(smooth, row_tables, count, r)
            return inside

        return lax.fori_loop(0, height // LANE, per_row, carry)

    lax.fori_loop(0, breadth // WIN, per_pair, 0)

    landed(labels_in.at[pl.ds(0, n_patch - 1)], label_recv)
    for first in range(0, places, LANE // EDGE):
        lane = lax.broadcasted_iota(jnp.int32, (8, LANE), 1)
        named = jnp.full((8, LANE), -1, jnp.int32)
        for p in range(LANE // EDGE):
            place = first + p
            mark = jnp.broadcast_to(labels_in[place // CAP, place % CAP : place % CAP + 1, :], (8, LANE))
            named = jnp.where((lane >= p * EDGE) & (lane < (p + 1) * EDGE), mark, named)
        named = jnp.concatenate([named] * (EDGE // 8), axis=0)
        lane = lax.broadcasted_iota(jnp.int32, (EDGE, LANE), 1)
        same = lax.rem(lane, EDGE) == lax.broadcasted_iota(jnp.int32, (EDGE, LANE), 0)
        for s in range(slots):
            picks[s * EDGE : (s + 1) * EDGE, first * EDGE : first * EDGE + LANE] = jnp.where(
                same & (named == s), 1.0, 0.0
            ).astype(BF16)

    for c, reach in enumerate(sizes):
        landed(arrived.at[rows_of(c, 0, places - CAP)], block_recv.at[c])

        last = c == len(sizes) - 1
        held = last_difference if last else part_difference

        def add(r, carry, c=c, held=held):
            pieces = jnp.concatenate(
                [
                    arrived[pl.ds(pl.multiple_of(places * starts[c] + p * sizes[c] + r * EDGE, EDGE), EDGE), :]
                    for p in range(places)
                ],
                axis=0,
            )
            summed = jnp.dot(picks[...], pieces, preferred_element_type=F32)
            lane = lax.broadcasted_iota(jnp.int32, (EDGE, LANE), 1)
            for h in range(halves):
                source = pl.ds(pl.multiple_of(h * edge + starts[c] + r * EDGE, EDGE), EDGE)
                rows = pl.ds(pl.multiple_of(h * sizes[c] + r * EDGE, EDGE), EDGE)
                before = jnp.zeros((EDGE, LANE), F32)
                for t in range(breadth // LANE):
                    column = t * LANE
                    slot_rows = (h * wide + column // edge) * EDGE
                    value = (
                        total[source, column : column + LANE]
                        + summed[slot_rows : slot_rows + EDGE, column % edge : column % edge + LANE]
                    )
                    rolled = pltpu.roll(value, HALF, 1)
                    held[rows, column : column + LANE] = jnp.where(lane < HALF, before, rolled).astype(BF16)
                    before = rolled
                held[rows, breadth:] = jnp.where(lane < HALF, before, 0.0).astype(BF16)
            return carry

        lax.fori_loop(0, reach // EDGE, add, 0, unroll=reach < LANE)
        if last:
            continue

        blur_rows(part_difference, psf_column_tables, blur, reach, psf_count, halves, breadth // LANE)

        def gather(t, carry, c=c, reach=reach):
            columns = pl.ds(pl.multiple_of(t * WIN, WIN), WIN)
            for h in range(halves):
                rows = slice(h * edge + starts[c], h * edge + starts[c] + reach + 2 * EDGE)
                filtered[rows, columns] += jnp.dot(
                    tables_of[reach][...], blur[h, : psf_count * reach, columns], preferred_element_type=F32
                )
            return carry

        lax.fori_loop(0, breadth // WIN, gather, 0, unroll=halves * reach <= LANE)

    landed(whole.at[pl.ds(0, (n_visit - 1) * local_rows)], rows_send)
    landed(labels_out.at[pl.ds(0, n_patch - 1)], label_send)
    landed(outgoing.at[pl.ds(0, (places - CAP) * edge)], block_send)


def finish_kernel(edge, filtered, difference, column_tables, table, out, blur, ends, sem):
    height, breadth = out.shape
    halves = height // edge
    psf_count = column_tables.shape[1] // LANE
    reach = difference.shape[0] // halves

    def put(source, first, rows):
        pltpu.make_async_copy(source, out.at[pl.ds(first, rows)], sem).start()

    done = 0
    for h in range(halves):
        upto = (h + 1) * edge - reach - EDGE
        piece = edge // 4
        for first in range(done, upto, piece):
            rows = min(piece, upto - first)
            put(filtered.at[pl.ds(EDGE + first, rows)], first, rows)
        done = upto + reach + 2 * EDGE
    blur_rows(difference, column_tables, blur, reach, psf_count, halves, breadth // LANE)
    for h in range(halves):
        first = (h + 1) * edge - reach
        for t in range(breadth // WIN):
            columns = slice(t * WIN, (t + 1) * WIN)
            ends[h, :, columns] = filtered[first : first + reach + 2 * EDGE, columns] + jnp.dot(
                table[...], blur[h, :, columns], preferred_element_type=F32
            )
        rows = reach + 2 * EDGE if h < halves - 1 else reach + EDGE
        put(ends.at[h, pl.ds(0, rows)], first - EDGE, rows)
    pltpu.make_async_copy(out, out, sem).wait()


SMEM = pl.BlockSpec(memory_space=pltpu.SMEM)
HBM = pl.BlockSpec(memory_space=pltpu.HBM)
VMEM = pl.BlockSpec(memory_space=pltpu.VMEM)


def stencil_scratch(count, height, breadth):
    return [
        pltpu.VMEM((height, breadth + LANE), BF16),
        pltpu.VMEM((WIN, count * LANE), BF16),
        pltpu.VMEM((count, LANE, WIN), BF16),
        pltpu.VMEM((count, height + 2 * HALF, WIN), BF16),
    ]


def per_device(blocks, block_patch, block_slot, block_count, template, basis_rows, basis_cols, coeffs, psf_rows, psf_cols):
    n_patch = lax.axis_size("patch")
    n_visit = lax.axis_size("visit")
    local_rows, breadth = template.shape[1:]
    height = local_rows * n_visit
    entries, edge = blocks.shape[2:4]
    halves = height // edge
    slots = halves * (breadth // edge)
    places = n_patch * CAP
    count = basis_rows.shape[0]
    psf_count = psf_rows.shape[1]
    sizes = cuts(edge)
    reaches = sorted(set(sizes[:-1]) - {sizes[-1]})
    most = max(sizes)
    final = sizes[-1]
    dma = pltpu.SemaphoreType.DMA
    handed = pl.pallas_call(
        functools.partial(exchange_kernel, n_patch, n_visit),
        out_shape=(
            jax.ShapeDtypeStruct((height + 2 * EDGE, breadth), F32),
            jax.ShapeDtypeStruct((halves * final, breadth + LANE), BF16),
            jax.ShapeDtypeStruct((WIN, psf_count * LANE), BF16),
            jax.ShapeDtypeStruct((final + 2 * EDGE, psf_count * final), BF16),
        ),
        in_specs=[pl.BlockSpec(memory_space=pl.ANY)] + [HBM] * 9,
        out_specs=(VMEM,) * 4,
        scratch_shapes=[
            pltpu.SMEM((1, 1), jnp.int32),
            pltpu.SMEM((entries,), jnp.int32),
            pltpu.SMEM((entries,), jnp.int32),
            pltpu.SMEM(coeffs.shape, F32),
            pltpu.VMEM(basis_rows.shape, BF16),
            pltpu.VMEM(basis_cols.shape, F32),
            pltpu.VMEM(psf_rows.shape, BF16),
            pltpu.VMEM(psf_cols.shape, BF16),
            dma((8,)),
            pltpu.SMEM((places,), jnp.int32),
            pltpu.VMEM((pl.cdiv(max(count, psf_count), 8) * 8, WIN), F32),
            pltpu.VMEM((places * edge, edge), BF16),
            pltpu.VMEM((places * edge, edge), BF16),
            pltpu.VMEM((n_patch, CAP, LANE), jnp.int32),
            pltpu.VMEM((n_patch, CAP, LANE), jnp.int32),
            pltpu.VMEM((slots * EDGE, places * EDGE), BF16),
            pltpu.VMEM((height, breadth), BF16),
            pltpu.VMEM((height, breadth), F32),
        ]
        + stencil_scratch(count, height, breadth)
        + [
            pltpu.VMEM((halves, psf_count * most, breadth), BF16),
            pltpu.VMEM((halves * most, breadth + LANE), BF16),
        ]
        + [pltpu.VMEM((reach + 2 * EDGE, psf_count * reach), BF16) for reach in reaches]
        + [pltpu.VMEM((entries, size, edge), BF16) for size in sizes]
        + [
            dma((len(sizes),)),
            dma(()),
            dma(()),
            dma((len(sizes),)),
            dma(()),
            dma(()),
            dma(()),
            dma(()),
            pltpu.SemaphoreType.REGULAR((5,)),
        ],
        compiler_params=pltpu.CompilerParams(
            collective_id=0, has_side_effects=True, vmem_limit_bytes=VMEM_LIMIT
        ),
    )(
        block_count,
        *(
            pltpu.with_memory_space_constraint(value, pltpu.HBM)
            for value in (
                block_patch.reshape(entries), block_slot.reshape(entries), coeffs,
                basis_rows, basis_cols, psf_rows, psf_cols, blocks[0, 0], template[0],
            )
        )
    )
    filtered = pl.pallas_call(
        functools.partial(finish_kernel, edge),
        out_shape=jax.ShapeDtypeStruct((height, breadth), F32),
        in_specs=[VMEM] * 4,
        out_specs=HBM,
        scratch_shapes=[
            pltpu.VMEM((halves, psf_count * final, breadth), BF16),
            pltpu.VMEM((halves, final + 2 * EDGE, breadth), F32),
            dma(()),
        ],
        compiler_params=pltpu.CompilerParams(vmem_limit_bytes=16 * 1024 * 1024),
    )(*handed)
    return filtered[None, None]


def solution(mesh):
    return jax.shard_map(
        per_device,
        mesh=mesh,
        in_specs=(
            P("patch", "visit", None, None, None),
            P("patch", "visit", None, None),
            P("patch", "visit", None),
            P("patch", "visit"),
            P("patch", "visit", None),
            P(),
            P(),
            P("visit", None),
            P("visit", None, None),
            P("visit", None, None),
        ),
        out_specs=P("patch", "visit", None, None),
        check_vma=False,
    )
```

```python
import functools

import jax
import jax.numpy as jnp
from jax import lax
from jax.experimental import pallas as pl
from jax.experimental.pallas import tpu as pltpu
from jax.sharding import PartitionSpec as P

CAP = 2
MOST_ROWS = 512
LANE = 128
HALF = 64
EDGE = 16
WIN = 256
F32 = jnp.float32
BF16 = jnp.bfloat16
VMEM_LIMIT = 32 * 1024 * 1024


def toeplitz(row, half_len):
    wide = jnp.broadcast_to(row, (LANE, WIN))
    return pltpu.roll(wide, (HALF - half_len) // 8 * 8, 1, stride=1, stride_axis=0)


def spread(taps, staged):
    count, length = taps.shape
    staged[...] = jnp.zeros(staged.shape, F32)
    staged[:count, :length] = taps
    lead = (HALF - length // 2) % 8
    if lead:
        staged[...] = pltpu.roll(staged[...], lead, 1)


def shift_into(load_tile, shifted, height, tiles, step):
    def body(r, carry):
        rows = pl.ds(pl.multiple_of(r * step, step), step)
        lane = lax.broadcasted_iota(jnp.int32, (step, LANE), 1)
        before = jnp.zeros((step, LANE), F32)
        for t in range(tiles):
            rolled = pltpu.roll(load_tile(rows, t), HALF, 1)
            shifted[rows, t * LANE : (t + 1) * LANE] = jnp.where(lane < HALF, before, rolled).astype(BF16)
            before = rolled
        shifted[rows, tiles * LANE :] = jnp.where(lane < HALF, before, 0.0).astype(BF16)
        return carry

    lax.fori_loop(0, height // step, body, 0)


def columns_pass(shifted, tables, smooth, pair, count, height, margin=HALF):
    for side in range(2):
        start = pl.multiple_of((2 * pair + side) * LANE, LANE)
        window = shifted[:, pl.ds(start, WIN)]
        for group in range(0, count, 2):
            taken = min(2, count - group)
            got = jnp.dot(
                window, tables[:, group * LANE : (group + taken) * LANE], preferred_element_type=F32
            ).astype(BF16)
            for k in range(taken):
                smooth[group + k, margin : margin + height, side * LANE : (side + 1) * LANE] = got[
                    :, k * LANE : (k + 1) * LANE
                ]


def rows_pass(smooth, tables, count, r):
    start = pl.multiple_of(r * LANE, LANE)
    total = jnp.zeros((LANE, WIN), F32)
    for k in range(count):
        total = total + jnp.dot(tables[k], smooth[k, pl.ds(start, WIN), :], preferred_element_type=F32)
    return total


def spread_table(staged, half_len, reach, count):
    wide_rows = reach + 2 * EDGE
    lane = lax.broadcasted_iota(jnp.int32, (wide_rows, WIN), 1)
    joined = jnp.zeros((wide_rows, WIN), F32)
    for k in range(count):
        shift = (k * reach - EDGE - half_len - (HALF - half_len) % 8) % WIN
        wide = jnp.broadcast_to(staged[k : k + 1, :], (wide_rows, WIN))
        rolled = pltpu.roll(wide, shift, 1, stride=1, stride_axis=0)
        joined = jnp.where((lane >= k * reach) & (lane < (k + 1) * reach), rolled, joined)
    return joined[:, : count * reach].astype(BF16)


def build_tables(column_taps, row_taps, column_tables, row_tables, staged):
    spread(column_taps, staged)
    for k in range(column_taps.shape[0]):
        table = toeplitz(staged[k : k + 1, :], column_taps.shape[1] // 2)
        column_tables[:, k * LANE : (k + 1) * LANE] = table.T.astype(BF16)
    spread(row_taps, staged)
    half_len = row_taps.shape[1] // 2
    if isinstance(row_tables, dict):
        for reach, table in row_tables.items():
            table[...] = spread_table(staged, half_len, reach, row_taps.shape[0])
    else:
        for k in range(row_taps.shape[0]):
            row_tables[k] = toeplitz(staged[k : k + 1, :], half_len).astype(BF16)


def clear_edges(smooth, count, height):
    for k in range(count):
        smooth[k, :HALF, :] = jnp.zeros((HALF, smooth.shape[2]), BF16)
        smooth[k, HALF + height :, :] = jnp.zeros((HALF, smooth.shape[2]), BF16)


def cuts(edge):
    return [edge // 8, 3 * edge // 8, edge // 4, edge // 8, edge // 8]


def blur_rows(difference, tables, blur, reach, count, halves, tiles):
    high = halves * reach
    group = max(1, min(tiles, MOST_ROWS // high))

    def some(g, carry):
        begin = [pl.multiple_of((g * group + n) * LANE, LANE) for n in range(group)]
        windows = jnp.concatenate([difference[:high, pl.ds(start, WIN)] for start in begin], axis=0)
        got = jnp.dot(windows, tables[...], preferred_element_type=F32).astype(BF16)
        for n, start in enumerate(begin):
            for h in range(halves):
                rows = slice(n * high + h * reach, n * high + (h + 1) * reach)
                for k in range(count):
                    blur[h, k * reach : (k + 1) * reach, pl.ds(start, LANE)] = got[rows, k * LANE : (k + 1) * LANE]
        return carry

    lax.fori_loop(0, tiles // group, some, 0, unroll=high < LANE)


def exchange_kernel(
    n_patch, n_visit,
    live_in, patch_in, slot_in, coeffs_in, basis_rows_in, basis_cols_in, psf_rows_in, psf_cols_in, blocks, template,
    filtered, last_arrived, last_total, picks, psf_column_tables, last_table,
    live, patch, slot, coeffs, basis_rows, basis_cols, psf_rows, psf_cols, small_sems, sources, staged, outgoing, arrived, labels_out, labels_in, whole, total, shifted, column_tables, row_tables, smooth, blur, part_difference, *rest,
):
    sizes = cuts(blocks.shape[1])
    reaches = sorted(set(sizes[:-1]) - {sizes[-1]})
    tables_of = dict(zip(reaches, rest[: len(reaches)]))
    tables_of[sizes[-1]] = last_table
    raw = rest[len(reaches) : len(reaches) + len(sizes)]
    load_sem, own_sem, block_send, block_recv, label_send, label_recv, rows_send, rows_recv, told = rest[
        len(reaches) + len(sizes) :
    ]
    me = lax.axis_index("patch")
    my_visit = lax.axis_index("visit")
    local_rows, breadth = template.shape
    height = local_rows * n_visit
    entries, edge = blocks.shape[:2]
    places = n_patch * CAP
    count = basis_rows.shape[0]
    psf_count = psf_rows.shape[1]
    wide = breadth // edge
    halves = height // edge
    slots = halves * wide
    chips = n_patch // 2
    chip, core = me // 2, lax.rem(me, 2)
    sibling = 2 * chip + 1 - core
    starts = [sum(sizes[:c]) for c in range(len(sizes))]
    visits = [lax.rem(my_visit + hop, n_visit) for hop in range(1, n_visit)]

    def tell(semaphore, peer):
        pl.semaphore_signal(semaphore, inc=1, device_id={"patch": peer}, device_id_type=pl.DeviceIdType.MESH)

    def tell_visit(semaphore, visit):
        pl.semaphore_signal(semaphore, inc=1, device_id={"visit": visit}, device_id_type=pl.DeviceIdType.MESH)

    small = [
        pltpu.make_async_copy(source, held, small_sems.at[i])
        for i, (source, held) in enumerate(
            (
                (live_in, live), (patch_in, patch), (slot_in, slot), (coeffs_in, coeffs),
                (basis_rows_in, basis_rows), (basis_cols_in, basis_cols),
                (psf_rows_in, psf_rows), (psf_cols_in, psf_cols),
            )
        )
    ]
    staged_entry = chips == 4
    near_side = chip < chips // 2
    middle = (chip == chips // 2) | (chip == chips // 2 - 1)
    inner = jnp.where(near_side, chip + 1, chip - 1)
    outer = jnp.where(near_side, chip - 1, chip + 1)
    other = jnp.where(near_side, chip + 2, chip - 2)
    mirror = chips - 1 - chip
    barrier = pltpu.get_barrier_semaphore()
    if staged_entry:
        tell(barrier, sibling)

        @pl.when(middle)
        def _():
            for c in range(2):
                tell(barrier, 2 * inner + c)
                tell(barrier, 2 * outer + c)

        @pl.when(jnp.logical_not(middle))
        def _():
            for visit in visits:
                tell_visit(barrier, visit)

        greeted = 3 + jnp.where(middle, 0, n_visit - 1)
    else:
        for hop in range(1, n_patch):
            tell(barrier, lax.rem(me + hop, n_patch))
        for visit in visits:
            tell_visit(barrier, visit)
        greeted = n_patch + n_visit - 2
    for copy in small[:3]:
        copy.start()
    loads = [
        pltpu.make_async_copy(blocks.at[:, pl.ds(starts[c], sizes[c])], raw[c], load_sem.at[c])
        for c in range(len(sizes))
    ]
    for copy in loads + small[3:]:
        copy.start()
    my_rows = pl.ds(pl.multiple_of(my_visit * local_rows, local_rows), local_rows)
    own = pltpu.make_async_copy(template, whole.at[my_rows], own_sem)
    own.start()

    for copy in small[:3]:
        copy.wait()
    targets = [patch[i] for i in range(entries)]
    marks = [jnp.where(i < live[0, 0], slot[i], -1) for i in range(entries)]

    def find(d, carry):
        first, last, first_mark, last_mark = (jnp.int32(0), jnp.int32(-1), jnp.int32(-1), jnp.int32(-1))
        for i in range(entries):
            last = jnp.where(targets[i] == d, i, last)
            last_mark = jnp.where(targets[i] == d, marks[i], last_mark)
        for i in reversed(range(entries)):
            first = jnp.where(targets[i] == d, i, first)
            first_mark = jnp.where(targets[i] == d, marks[i], first_mark)
        labels = (first_mark, jnp.where(first < last, last_mark, -1))
        for c, (source, label) in enumerate(zip((first, jnp.maximum(last, 0)), labels)):
            sources[d * CAP + c] = source
            labels_out[d, c : c + 1, :] = jnp.full((1, LANE), label, jnp.int32)
        return carry

    def landing(c, place, number=1):
        if c == len(sizes) - 1:
            return last_arrived.at[pl.ds(pl.multiple_of(place * sizes[c], EDGE), number * sizes[c])]
        return arrived.at[rows_of(c, place, number)]

    def rows_of(c, place, number=1):
        return pl.ds(pl.multiple_of(places * starts[c] + place * sizes[c], EDGE), number * sizes[c])

    def pack(c, first, number):
        def one(i, carry):
            outgoing[rows_of(c, first + i), :] = raw[c][sources[first + i]]
            return carry

        lax.fori_loop(0, number, one, 0)

    if staged_entry:
        turns = [
            jnp.where(middle, inner, other), jnp.where(middle, other, mirror), jnp.where(middle, outer, inner), chip,
        ]
    else:
        turns = [lax.rem(chip + hop, chips) for hop in range(chips - 1, -1, -1)]
    find(2 * turns[0], 0)
    find(2 * turns[0] + 1, 0)
    loads[0].wait()
    pack(0, 2 * turns[0] * CAP, 2 * CAP)
    pl.semaphore_wait(barrier, greeted)

    row_copies = [
        pltpu.make_async_remote_copy(
            src_ref=template, dst_ref=whole.at[my_rows],
            send_sem=rows_send, recv_sem=rows_recv,
            device_id={"visit": visit}, device_id_type=pl.DeviceIdType.MESH,
        )
        for hop, visit in enumerate(visits)
    ]

    def landed(held, semaphore):
        pltpu.make_async_copy(held, held, semaphore).wait()

    def label_copy(peer):
        return pltpu.make_async_remote_copy(
            src_ref=labels_out.at[peer], dst_ref=labels_in.at[me],
            send_sem=label_send, recv_sem=label_recv,
            device_id={"patch": peer}, device_id_type=pl.DeviceIdType.MESH,
        )

    def block_copy(peer, c):
        return pltpu.make_async_remote_copy(
            src_ref=outgoing.at[rows_of(c, peer * CAP, CAP)], dst_ref=landing(c, me * CAP, CAP),
            send_sem=block_send, recv_sem=block_recv.at[c],
            device_id={"patch": peer}, device_id_type=pl.DeviceIdType.MESH,
        )

    def send(peer, c):
        block_copy(peer, c).start()
        if c == 0:
            label_copy(peer).start()

    def send_chip(there, c):
        send(2 * there + 1, c)
        send(2 * there, c)

    early, late = range(len(sizes) - 3), range(len(sizes) - 3, len(sizes))

    def pack_rest():
        for turn in turns[1:]:
            lax.fori_loop(2 * turn, 2 * turn + 2, find, 0)
            pack(0, 2 * turn * CAP, 2 * CAP)
            if staged_entry:
                pack(1, 2 * turn * CAP, 2 * CAP)
        for c in range(2 if staged_entry else 1, len(sizes)):
            loads[c].wait()
            pack(c, 0, places)

    if staged_entry:

        @pl.when(middle)
        def _():
            send_chip(inner, 0)

        loads[1].wait()
        pack(1, 2 * turns[0] * CAP, 2 * CAP)

        @pl.when(middle)
        def _():
            send_chip(inner, 1)

        @pl.when(jnp.logical_not(middle))
        def _():
            for c in range(2):
                tell(told.at[0], 2 * inner + c)
            for visit in visits:
                tell_visit(told.at[3], visit)
            for copy in row_copies:
                copy.start()

        @pl.when(middle)
        def _():
            pl.semaphore_wait(told.at[0], 2)
            tell(told.at[1], 2 * outer + core)
            tell(told.at[1], 2 * inner + core)

        pack_rest()

        @pl.when(middle)
        def _():
            pl.semaphore_wait(told.at[1], 1)
            tell(told.at[2], 2 * outer + core)
            for steps in early, late:
                for c in steps:
                    send_chip(other, c)
                    send_chip(outer, c)
                    send(sibling, c)
                    if c > 1 and steps is early:
                        send_chip(inner, c)
            for c in late:
                send_chip(inner, c)
            pl.semaphore_wait(told.at[4], 1)
            for copy in row_copies:
                copy.start()

        @pl.when(jnp.logical_not(middle))
        def _():
            pl.semaphore_wait(told.at[1], 1)
            send_chip(other, 0)
            pl.semaphore_wait(told.at[3], n_visit - 1)
            tell(told.at[4], 2 * inner + core)
            pl.semaphore_wait(told.at[2], 1)
            for steps in early, late:
                for c in steps:
                    send_chip(mirror, c)
                    if steps is early:
                        if c:
                            send_chip(other, c)
                        send_chip(inner, c)
                    send(sibling, c)
            for c in late:
                send_chip(other, c)
                send_chip(inner, c)

    else:
        for copy in row_copies:
            copy.start()
        for turn in turns[:1]:
            send_chip(turn, 0)
        pack_rest()
        for c in range(len(sizes)):
            for turn in turns[(1 if c == 0 else 0) : -1]:
                send_chip(turn, c)
            send(sibling, c)

    labels_in[me] = labels_out[me]
    for c in range(len(sizes)):
        landing(c, me * CAP, CAP)[...] = outgoing[rows_of(c, me * CAP, CAP), :]
    for copy in small[3:]:
        copy.wait()
    scaled = jnp.concatenate(
        [(coeffs[0, k] * basis_cols[k : k + 1, :]).astype(BF16).astype(F32) for k in range(count)], axis=0
    )
    build_tables(basis_rows[...].astype(F32), scaled, column_tables, row_tables, staged)
    build_tables(psf_rows[0].astype(F32), psf_cols[0].astype(F32), psf_column_tables, tables_of, staged)
    clear_edges(smooth, count, height)

    def clear(r, carry):
        filtered[pl.ds(pl.multiple_of(r * EDGE, EDGE), EDGE), :] = jnp.zeros((EDGE, breadth), F32)
        return carry

    lax.fori_loop(0, height // EDGE + 2, clear, 0)
    own.wait()
    landed(whole.at[pl.ds(0, (n_visit - 1) * local_rows)], rows_recv)
    shift_into(
        lambda rows, t: whole[rows, t * LANE : (t + 1) * LANE].astype(F32),
        shifted, height, breadth // LANE, 32,
    )

    def per_pair(pair, carry):
        columns_pass(shifted, column_tables, smooth, pair, count, height)

        def per_row(r, inside):
            rows = pl.ds(pl.multiple_of(r * LANE, LANE), LANE)
            columns = pl.ds(pl.multiple_of(pair * WIN, WIN), WIN)
            total[rows, columns] = -rows_pass(smooth, row_tables, count, r)
            return inside

        return lax.fori_loop(0, height // LANE, per_row, carry)

    lax.fori_loop(0, breadth // WIN, per_pair, 0)
    for h in range(halves):
        last_total[h * sizes[-1] : (h + 1) * sizes[-1], :] = total[(h + 1) * edge - sizes[-1] : (h + 1) * edge, :]

    landed(labels_in.at[pl.ds(0, n_patch - 1)], label_recv)
    for first in range(0, places, LANE // EDGE):
        lane = lax.broadcasted_iota(jnp.int32, (8, LANE), 1)
        named = jnp.full((8, LANE), -1, jnp.int32)
        for p in range(LANE // EDGE):
            place = first + p
            mark = jnp.broadcast_to(labels_in[place // CAP, place % CAP : place % CAP + 1, :], (8, LANE))
            named = jnp.where((lane >= p * EDGE) & (lane < (p + 1) * EDGE), mark, named)
        named = jnp.concatenate([named] * (EDGE // 8), axis=0)
        lane = lax.broadcasted_iota(jnp.int32, (EDGE, LANE), 1)
        same = lax.rem(lane, EDGE) == lax.broadcasted_iota(jnp.int32, (EDGE, LANE), 0)
        for s in range(slots):
            picks[s * EDGE : (s + 1) * EDGE, first * EDGE : first * EDGE + LANE] = jnp.where(
                same & (named == s), 1.0, 0.0
            ).astype(BF16)

    for c, reach in enumerate(sizes):
        landed(landing(c, 0, places - CAP), block_recv.at[c])
        if c == len(sizes) - 1:
            continue

        def add(r, carry, c=c):
            pieces = jnp.concatenate(
                [
                    arrived[pl.ds(pl.multiple_of(places * starts[c] + p * sizes[c] + r * EDGE, EDGE), EDGE), :]
                    for p in range(places)
                ],
                axis=0,
            )
            summed = jnp.dot(picks[...], pieces, preferred_element_type=F32)
            for s in range(slots):
                rows = pl.ds(pl.multiple_of(s // wide * edge + starts[c] + r * EDGE, EDGE), EDGE)
                columns = slice(s % wide * edge, (s % wide + 1) * edge)
                total[rows, columns] += summed[s * EDGE : (s + 1) * EDGE]
            return carry

        lax.fori_loop(0, reach // EDGE, add, 0, unroll=reach < LANE)

        def shift(r, carry, c=c, held=part_difference):
            lane = lax.broadcasted_iota(jnp.int32, (EDGE, LANE), 1)
            for h in range(halves):
                source = pl.ds(pl.multiple_of(h * edge + starts[c] + r * EDGE, EDGE), EDGE)
                rows = pl.ds(pl.multiple_of(h * sizes[c] + r * EDGE, EDGE), EDGE)
                before = jnp.zeros((EDGE, LANE), F32)
                for t in range(breadth // LANE):
                    rolled = pltpu.roll(total[source, t * LANE : (t + 1) * LANE], HALF, 1)
                    held[rows, t * LANE : (t + 1) * LANE] = jnp.where(lane < HALF, before, rolled).astype(BF16)
                    before = rolled
                held[rows, breadth:] = jnp.where(lane < HALF, before, 0.0).astype(BF16)
            return carry

        lax.fori_loop(0, reach // EDGE, shift, 0, unroll=reach < LANE)
        blur_rows(part_difference, psf_column_tables, blur, reach, psf_count, halves, breadth // LANE)

        def gather(t, carry, c=c, reach=reach):
            columns = pl.ds(pl.multiple_of(t * WIN, WIN), WIN)
            for h in range(halves):
                rows = slice(h * edge + starts[c], h * edge + starts[c] + reach + 2 * EDGE)
                filtered[rows, columns] += jnp.dot(
                    tables_of[reach][...], blur[h, : psf_count * reach, columns], preferred_element_type=F32
                )
            return carry

        lax.fori_loop(0, breadth // WIN, gather, 0, unroll=halves * reach <= LANE)

    landed(whole.at[pl.ds(0, (n_visit - 1) * local_rows)], rows_send)
    landed(labels_out.at[pl.ds(0, n_patch - 1)], label_send)
    landed(outgoing.at[pl.ds(0, (places - CAP) * edge)], block_send)


def finish_kernel(edge, filtered, arrived, total, picks, column_tables, table, out, difference, blur, ends, sem):
    height, breadth = out.shape
    halves = height // edge
    psf_count = column_tables.shape[1] // LANE
    reach = difference.shape[0] // halves
    places = arrived.shape[0] // reach
    wide = breadth // edge

    def put(source, first, rows):
        pltpu.make_async_copy(source, out.at[pl.ds(first, rows)], sem).start()

    done = 0
    for h in range(halves):
        upto = (h + 1) * edge - reach - EDGE
        piece = edge // 4
        for first in range(done, upto, piece):
            rows = min(piece, upto - first)
            put(filtered.at[pl.ds(EDGE + first, rows)], first, rows)
        done = upto + reach + 2 * EDGE
    lane = lax.broadcasted_iota(jnp.int32, (EDGE, LANE), 1)
    for r in range(0, reach, EDGE):
        pieces = jnp.concatenate([arrived[p * reach + r : p * reach + r + EDGE, :] for p in range(places)], axis=0)
        summed = jnp.dot(picks[...], pieces, preferred_element_type=F32)
        for h in range(halves):
            rows = slice(h * reach + r, h * reach + r + EDGE)
            before = jnp.zeros((EDGE, LANE), F32)
            for t in range(breadth // LANE):
                start = t * LANE
                slot = h * wide + start // edge
                value = (
                    total[rows, start : start + LANE]
                    + summed[slot * EDGE : (slot + 1) * EDGE, start % edge : start % edge + LANE]
                )
                rolled = pltpu.roll(value, HALF, 1)
                difference[rows, start : start + LANE] = jnp.where(lane < HALF, before, rolled).astype(BF16)
                before = rolled
            difference[rows, breadth:] = jnp.where(lane < HALF, before, 0.0).astype(BF16)
    blur_rows(difference, column_tables, blur, reach, psf_count, halves, breadth // LANE)
    for h in range(halves):
        first = (h + 1) * edge - reach
        for t in range(breadth // WIN):
            columns = slice(t * WIN, (t + 1) * WIN)
            ends[h, :, columns] = filtered[first : first + reach + 2 * EDGE, columns] + jnp.dot(
                table[...], blur[h, :, columns], preferred_element_type=F32
            )
        rows = reach + 2 * EDGE if h < halves - 1 else reach + EDGE
        put(ends.at[h, pl.ds(0, rows)], first - EDGE, rows)
    pltpu.make_async_copy(out, out, sem).wait()


SMEM = pl.BlockSpec(memory_space=pltpu.SMEM)
HBM = pl.BlockSpec(memory_space=pltpu.HBM)
VMEM = pl.BlockSpec(memory_space=pltpu.VMEM)


def stencil_scratch(count, height, breadth):
    return [
        pltpu.VMEM((height, breadth + LANE), BF16),
        pltpu.VMEM((WIN, count * LANE), BF16),
        pltpu.VMEM((count, LANE, WIN), BF16),
        pltpu.VMEM((count, height + 2 * HALF, WIN), BF16),
    ]


def per_device(blocks, block_patch, block_slot, block_count, template, basis_rows, basis_cols, coeffs, psf_rows, psf_cols):
    n_patch = lax.axis_size("patch")
    n_visit = lax.axis_size("visit")
    local_rows, breadth = template.shape[1:]
    height = local_rows * n_visit
    entries, edge = blocks.shape[2:4]
    halves = height // edge
    slots = halves * (breadth // edge)
    places = n_patch * CAP
    count = basis_rows.shape[0]
    psf_count = psf_rows.shape[1]
    sizes = cuts(edge)
    reaches = sorted(set(sizes[:-1]) - {sizes[-1]})
    most = max(sizes)
    final = sizes[-1]
    dma = pltpu.SemaphoreType.DMA
    handed = pl.pallas_call(
        functools.partial(exchange_kernel, n_patch, n_visit),
        out_shape=(
            jax.ShapeDtypeStruct((height + 2 * EDGE, breadth), F32),
            jax.ShapeDtypeStruct((places * final, edge), BF16),
            jax.ShapeDtypeStruct((halves * final, breadth), F32),
            jax.ShapeDtypeStruct((slots * EDGE, places * EDGE), BF16),
            jax.ShapeDtypeStruct((WIN, psf_count * LANE), BF16),
            jax.ShapeDtypeStruct((final + 2 * EDGE, psf_count * final), BF16),
        ),
        in_specs=[pl.BlockSpec(memory_space=pl.ANY)] + [HBM] * 9,
        out_specs=(VMEM,) * 6,
        scratch_shapes=[
            pltpu.SMEM((1, 1), jnp.int32),
            pltpu.SMEM((entries,), jnp.int32),
            pltpu.SMEM((entries,), jnp.int32),
            pltpu.SMEM(coeffs.shape, F32),
            pltpu.VMEM(basis_rows.shape, BF16),
            pltpu.VMEM(basis_cols.shape, F32),
            pltpu.VMEM(psf_rows.shape, BF16),
            pltpu.VMEM(psf_cols.shape, BF16),
            dma((8,)),
            pltpu.SMEM((places,), jnp.int32),
            pltpu.VMEM((pl.cdiv(max(count, psf_count), 8) * 8, WIN), F32),
            pltpu.VMEM((places * edge, edge), BF16),
            pltpu.VMEM((places * edge, edge), BF16),
            pltpu.VMEM((n_patch, CAP, LANE), jnp.int32),
            pltpu.VMEM((n_patch, CAP, LANE), jnp.int32),
            pltpu.VMEM((height, breadth), BF16),
            pltpu.VMEM((height, breadth), F32),
        ]
        + stencil_scratch(count, height, breadth)
        + [
            pltpu.VMEM((halves, psf_count * most, breadth), BF16),
            pltpu.VMEM((halves * most, breadth + LANE), BF16),
        ]
        + [pltpu.VMEM((reach + 2 * EDGE, psf_count * reach), BF16) for reach in reaches]
        + [pltpu.VMEM((entries, size, edge), BF16) for size in sizes]
        + [
            dma((len(sizes),)),
            dma(()),
            dma(()),
            dma((len(sizes),)),
            dma(()),
            dma(()),
            dma(()),
            dma(()),
            pltpu.SemaphoreType.REGULAR((5,)),
        ],
        compiler_params=pltpu.CompilerParams(
            collective_id=0, has_side_effects=True, vmem_limit_bytes=VMEM_LIMIT
        ),
    )(
        block_count,
        *(
            pltpu.with_memory_space_constraint(value, pltpu.HBM)
            for value in (
                block_patch.reshape(entries), block_slot.reshape(entries), coeffs,
                basis_rows, basis_cols, psf_rows, psf_cols, blocks[0, 0], template[0],
            )
        )
    )
    filtered = pl.pallas_call(
        functools.partial(finish_kernel, edge),
        out_shape=jax.ShapeDtypeStruct((height, breadth), F32),
        in_specs=[VMEM] * 6,
        out_specs=HBM,
        scratch_shapes=[
            pltpu.VMEM((halves * final, breadth + LANE), BF16),
            pltpu.VMEM((halves, psf_count * final, breadth), BF16),
            pltpu.VMEM((halves, final + 2 * EDGE, breadth), F32),
            dma(()),
        ],
        compiler_params=pltpu.CompilerParams(vmem_limit_bytes=16 * 1024 * 1024),
    )(*handed)
    return filtered[None, None]


def solution(mesh):
    return jax.shard_map(
        per_device,
        mesh=mesh,
        in_specs=(
            P("patch", "visit", None, None, None),
            P("patch", "visit", None, None),
            P("patch", "visit", None),
            P("patch", "visit"),
            P("patch", "visit", None),
            P(),
            P(),
            P("visit", None),
            P("visit", None, None),
            P("visit", None, None),
        ),
        out_specs=P("patch", "visit", None, None),
        check_vma=False,
    )
```

```python
import functools

import jax
import jax.numpy as jnp
from jax import lax
from jax.experimental import pallas as pl
from jax.experimental.pallas import tpu as pltpu
from jax.sharding import PartitionSpec as P

CAP = 2
MOST_ROWS = 512
LANE = 128
HALF = 64
EDGE = 16
WIN = 256
F32 = jnp.float32
BF16 = jnp.bfloat16
VMEM_LIMIT = 32 * 1024 * 1024


def toeplitz(row, half_len):
    wide = jnp.broadcast_to(row, (LANE, WIN))
    return pltpu.roll(wide, (HALF - half_len) // 8 * 8, 1, stride=1, stride_axis=0)


def spread(taps, staged):
    count, length = taps.shape
    staged[...] = jnp.zeros(staged.shape, F32)
    staged[:count, :length] = taps
    lead = (HALF - length // 2) % 8
    if lead:
        staged[...] = pltpu.roll(staged[...], lead, 1)


def shift_into(load_tile, shifted, height, tiles, step):
    def body(r, carry):
        rows = pl.ds(pl.multiple_of(r * step, step), step)
        lane = lax.broadcasted_iota(jnp.int32, (step, LANE), 1)
        before = jnp.zeros((step, LANE), F32)
        for t in range(tiles):
            rolled = pltpu.roll(load_tile(rows, t), HALF, 1)
            shifted[rows, t * LANE : (t + 1) * LANE] = jnp.where(lane < HALF, before, rolled).astype(BF16)
            before = rolled
        shifted[rows, tiles * LANE :] = jnp.where(lane < HALF, before, 0.0).astype(BF16)
        return carry

    lax.fori_loop(0, height // step, body, 0)


def columns_pass(shifted, tables, smooth, pair, count, height, margin=HALF):
    for side in range(2):
        start = pl.multiple_of((2 * pair + side) * LANE, LANE)
        window = shifted[:, pl.ds(start, WIN)]
        for group in range(0, count, 2):
            taken = min(2, count - group)
            got = jnp.dot(
                window, tables[:, group * LANE : (group + taken) * LANE], preferred_element_type=F32
            ).astype(BF16)
            for k in range(taken):
                smooth[group + k, margin : margin + height, side * LANE : (side + 1) * LANE] = got[
                    :, k * LANE : (k + 1) * LANE
                ]


def rows_pass(smooth, tables, count, r):
    start = pl.multiple_of(r * LANE, LANE)
    total = jnp.zeros((LANE, WIN), F32)
    for k in range(count):
        total = total + jnp.dot(tables[k], smooth[k, pl.ds(start, WIN), :], preferred_element_type=F32)
    return total


def spread_table(staged, half_len, reach, count):
    wide_rows = reach + 2 * EDGE
    lane = lax.broadcasted_iota(jnp.int32, (wide_rows, WIN), 1)
    joined = jnp.zeros((wide_rows, WIN), F32)
    for k in range(count):
        shift = (k * reach - EDGE - half_len - (HALF - half_len) % 8) % WIN
        wide = jnp.broadcast_to(staged[k : k + 1, :], (wide_rows, WIN))
        rolled = pltpu.roll(wide, shift, 1, stride=1, stride_axis=0)
        joined = jnp.where((lane >= k * reach) & (lane < (k + 1) * reach), rolled, joined)
    return joined[:, : count * reach].astype(BF16)


def build_tables(column_taps, row_taps, column_tables, row_tables, staged):
    spread(column_taps, staged)
    for k in range(column_taps.shape[0]):
        table = toeplitz(staged[k : k + 1, :], column_taps.shape[1] // 2)
        column_tables[:, k * LANE : (k + 1) * LANE] = table.T.astype(BF16)
    spread(row_taps, staged)
    half_len = row_taps.shape[1] // 2
    if isinstance(row_tables, dict):
        for reach, table in row_tables.items():
            table[...] = spread_table(staged, half_len, reach, row_taps.shape[0])
    else:
        for k in range(row_taps.shape[0]):
            row_tables[k] = toeplitz(staged[k : k + 1, :], half_len).astype(BF16)


def clear_edges(smooth, count, height):
    for k in range(count):
        smooth[k, :HALF, :] = jnp.zeros((HALF, smooth.shape[2]), BF16)
        smooth[k, HALF + height :, :] = jnp.zeros((HALF, smooth.shape[2]), BF16)


def cuts(edge):
    return [edge // 8, 3 * edge // 8, edge // 4, edge // 8, edge // 8]


def blur_rows(difference, tables, blur, reach, count, halves, tiles):
    high = halves * reach
    group = max(1, min(tiles, MOST_ROWS // high))

    def some(g, carry):
        begin = [pl.multiple_of((g * group + n) * LANE, LANE) for n in range(group)]
        windows = jnp.concatenate([difference[:high, pl.ds(start, WIN)] for start in begin], axis=0)
        got = jnp.dot(windows, tables[...], preferred_element_type=F32).astype(BF16)
        for n, start in enumerate(begin):
            for h in range(halves):
                rows = slice(n * high + h * reach, n * high + (h + 1) * reach)
                for k in range(count):
                    blur[h, k * reach : (k + 1) * reach, pl.ds(start, LANE)] = got[rows, k * LANE : (k + 1) * LANE]
        return carry

    lax.fori_loop(0, tiles // group, some, 0, unroll=high < LANE)


def exchange_kernel(
    n_patch, n_visit,
    live_in, patch_in, slot_in, coeffs_in, basis_rows_in, basis_cols_in, psf_rows_in, psf_cols_in, blocks, template,
    filtered, last_arrived, last_total, picks, psf_column_tables, last_table,
    live, patch, slot, coeffs, basis_rows, basis_cols, psf_rows, psf_cols, small_sems, sources, staged, outgoing, arrived, labels_out, labels_in, whole, total, shifted, column_tables, row_tables, smooth, blur, part_difference, *rest,
):
    sizes = cuts(blocks.shape[1])
    reaches = sorted(set(sizes[:-1]) - {sizes[-1]})
    tables_of = dict(zip(reaches, rest[: len(reaches)]))
    tables_of[sizes[-1]] = last_table
    raw = rest[len(reaches) : len(reaches) + len(sizes)]
    load_sem, own_sem, block_send, block_recv, label_send, label_recv, rows_send, rows_recv, told = rest[
        len(reaches) + len(sizes) :
    ]
    me = lax.axis_index("patch")
    my_visit = lax.axis_index("visit")
    local_rows, breadth = template.shape
    height = local_rows * n_visit
    entries, edge = blocks.shape[:2]
    places = n_patch * CAP
    count = basis_rows.shape[0]
    psf_count = psf_rows.shape[1]
    wide = breadth // edge
    halves = height // edge
    slots = halves * wide
    chips = n_patch // 2
    chip, core = me // 2, lax.rem(me, 2)
    sibling = 2 * chip + 1 - core
    starts = [sum(sizes[:c]) for c in range(len(sizes))]
    visits = [lax.rem(my_visit + hop, n_visit) for hop in range(1, n_visit)]

    def tell(semaphore, peer):
        pl.semaphore_signal(semaphore, inc=1, device_id={"patch": peer}, device_id_type=pl.DeviceIdType.MESH)

    def tell_visit(semaphore, visit):
        pl.semaphore_signal(semaphore, inc=1, device_id={"visit": visit}, device_id_type=pl.DeviceIdType.MESH)

    small = [
        pltpu.make_async_copy(source, held, small_sems.at[i])
        for i, (source, held) in enumerate(
            (
                (live_in, live), (patch_in, patch), (slot_in, slot), (coeffs_in, coeffs),
                (basis_rows_in, basis_rows), (basis_cols_in, basis_cols),
                (psf_rows_in, psf_rows), (psf_cols_in, psf_cols),
            )
        )
    ]
    staged_entry = chips == 4
    near_side = chip < chips // 2
    middle = (chip == chips // 2) | (chip == chips // 2 - 1)
    inner = jnp.where(near_side, chip + 1, chip - 1)
    outer = jnp.where(near_side, chip - 1, chip + 1)
    other = jnp.where(near_side, chip + 2, chip - 2)
    mirror = chips - 1 - chip
    barrier = pltpu.get_barrier_semaphore()
    if staged_entry:
        tell(barrier, sibling)

        @pl.when(middle)
        def _():
            for c in range(2):
                tell(barrier, 2 * inner + c)
                tell(barrier, 2 * outer + c)

        @pl.when(jnp.logical_not(middle))
        def _():
            for visit in visits:
                tell_visit(barrier, visit)

        greeted = 3 + jnp.where(middle, 0, n_visit - 1)
    else:
        for hop in range(1, n_patch):
            tell(barrier, lax.rem(me + hop, n_patch))
        for visit in visits:
            tell_visit(barrier, visit)
        greeted = n_patch + n_visit - 2
    for copy in small[:3]:
        copy.start()
    loads = [
        pltpu.make_async_copy(blocks.at[:, pl.ds(starts[c], sizes[c])], raw[c], load_sem.at[min(c, 2)])
        for c in range(len(sizes))
    ]
    for copy in loads + small[3:]:
        copy.start()
    my_rows = pl.ds(pl.multiple_of(my_visit * local_rows, local_rows), local_rows)
    own = pltpu.make_async_copy(template, whole.at[my_rows], own_sem)
    own.start()

    for copy in small[:3]:
        copy.wait()
    targets = [patch[i] for i in range(entries)]
    marks = [jnp.where(i < live[0, 0], slot[i], -1) for i in range(entries)]

    def find(d, carry):
        first, last, first_mark, last_mark = (jnp.int32(0), jnp.int32(-1), jnp.int32(-1), jnp.int32(-1))
        for i in range(entries):
            last = jnp.where(targets[i] == d, i, last)
            last_mark = jnp.where(targets[i] == d, marks[i], last_mark)
        for i in reversed(range(entries)):
            first = jnp.where(targets[i] == d, i, first)
            first_mark = jnp.where(targets[i] == d, marks[i], first_mark)
        labels = (first_mark, jnp.where(first < last, last_mark, -1))
        for c, (source, label) in enumerate(zip((first, jnp.maximum(last, 0)), labels)):
            sources[d * CAP + c] = source
            labels_out[d, c : c + 1, :] = jnp.full((1, LANE), label, jnp.int32)
        return carry

    def landing(c, place, number=1):
        if c == len(sizes) - 1:
            return last_arrived.at[pl.ds(pl.multiple_of(place * sizes[c], EDGE), number * sizes[c])]
        return arrived.at[rows_of(c, place, number)]

    def rows_of(c, place, number=1):
        return pl.ds(pl.multiple_of(places * starts[c] + place * sizes[c], EDGE), number * sizes[c])

    def pack(c, first, number):
        def one(i, carry):
            outgoing[rows_of(c, first + i), :] = raw[c][sources[first + i]]
            return carry

        lax.fori_loop(0, number, one, 0)

    if staged_entry:
        turns = [
            jnp.where(middle, inner, other), jnp.where(middle, other, mirror), jnp.where(middle, outer, inner), chip,
        ]
    else:
        turns = [lax.rem(chip + hop, chips) for hop in range(chips - 1, -1, -1)]
    find(2 * turns[0], 0)
    find(2 * turns[0] + 1, 0)
    loads[0].wait()
    pack(0, 2 * turns[0] * CAP, 2 * CAP)
    pl.semaphore_wait(barrier, greeted)

    row_copies = [
        pltpu.make_async_remote_copy(
            src_ref=template, dst_ref=whole.at[my_rows],
            send_sem=rows_send, recv_sem=rows_recv,
            device_id={"visit": visit}, device_id_type=pl.DeviceIdType.MESH,
        )
        for hop, visit in enumerate(visits)
    ]

    def landed(held, semaphore):
        pltpu.make_async_copy(held, held, semaphore).wait()

    def label_copy(peer):
        return pltpu.make_async_remote_copy(
            src_ref=labels_out.at[peer], dst_ref=labels_in.at[me],
            send_sem=label_send, recv_sem=label_recv,
            device_id={"patch": peer}, device_id_type=pl.DeviceIdType.MESH,
        )

    def block_copy(peer, c):
        return pltpu.make_async_remote_copy(
            src_ref=outgoing.at[rows_of(c, peer * CAP, CAP)], dst_ref=landing(c, me * CAP, CAP),
            send_sem=block_send, recv_sem=block_recv.at[c],
            device_id={"patch": peer}, device_id_type=pl.DeviceIdType.MESH,
        )

    def send(peer, c):
        block_copy(peer, c).start()
        if c == 0:
            label_copy(peer).start()

    def send_chip(there, c):
        send(2 * there + 1, c)
        send(2 * there, c)

    early, late = range(len(sizes) - 3), range(len(sizes) - 3, len(sizes))

    def pack_rest():
        for turn in turns[1:]:
            lax.fori_loop(2 * turn, 2 * turn + 2, find, 0)
            pack(0, 2 * turn * CAP, 2 * CAP)
            if staged_entry:
                pack(1, 2 * turn * CAP, 2 * CAP)
        if not staged_entry:
            loads[1].wait()
        landed(blocks.at[:, pl.ds(starts[2], edge - starts[2])], load_sem.at[2])
        for c in range(2 if staged_entry else 1, len(sizes)):
            pack(c, 0, places)

    if staged_entry:

        @pl.when(middle)
        def _():
            send_chip(inner, 0)

        loads[1].wait()
        pack(1, 2 * turns[0] * CAP, 2 * CAP)

        @pl.when(middle)
        def _():
            send_chip(inner, 1)

        @pl.when(jnp.logical_not(middle))
        def _():
            for c in range(2):
                tell(told.at[0], 2 * inner + c)
            for visit in visits:
                tell_visit(told.at[2], visit)
            for copy in row_copies:
                copy.start()

        @pl.when(middle)
        def _():
            pl.semaphore_wait(told.at[0], 2)
            tell(told.at[1], 2 * outer + core)
            tell(told.at[1], 2 * inner + core)

        pack_rest()

        @pl.when(middle)
        def _():
            pl.semaphore_wait(told.at[1], 1)
            tell(told.at[0], 2 * outer + core)
            for steps in early, late:
                for c in steps:
                    send_chip(other, c)
                    send_chip(outer, c)
                    send(sibling, c)
                    if c > 1 and steps is early:
                        send_chip(inner, c)
            for c in late:
                send_chip(inner, c)
            pl.semaphore_wait(told.at[2], 1)
            for copy in row_copies:
                copy.start()

        @pl.when(jnp.logical_not(middle))
        def _():
            pl.semaphore_wait(told.at[1], 1)
            send_chip(other, 0)
            pl.semaphore_wait(told.at[2], n_visit - 1)
            tell(told.at[2], 2 * inner + core)
            pl.semaphore_wait(told.at[0], 1)
            for steps in early, late:
                for c in steps:
                    send_chip(mirror, c)
                    if steps is early:
                        if c:
                            send_chip(other, c)
                        send_chip(inner, c)
                    send(sibling, c)
            for c in late:
                send_chip(other, c)
                send_chip(inner, c)

    else:
        for copy in row_copies:
            copy.start()
        for turn in turns[:1]:
            send_chip(turn, 0)
        pack_rest()
        for c in range(len(sizes)):
            for turn in turns[(1 if c == 0 else 0) : -1]:
                send_chip(turn, c)
            send(sibling, c)

    labels_in[me] = labels_out[me]
    for c in range(len(sizes)):
        landing(c, me * CAP, CAP)[...] = outgoing[rows_of(c, me * CAP, CAP), :]
    for copy in small[3:]:
        copy.wait()
    scaled = jnp.concatenate(
        [(coeffs[0, k] * basis_cols[k : k + 1, :]).astype(BF16).astype(F32) for k in range(count)], axis=0
    )
    build_tables(basis_rows[...].astype(F32), scaled, column_tables, row_tables, staged)
    build_tables(psf_rows[0].astype(F32), psf_cols[0].astype(F32), psf_column_tables, tables_of, staged)
    clear_edges(smooth, count, height)

    def clear(r, carry):
        filtered[pl.ds(pl.multiple_of(r * EDGE, EDGE), EDGE), :] = jnp.zeros((EDGE, breadth), F32)
        return carry

    lax.fori_loop(0, height // EDGE + 2, clear, 0)
    own.wait()
    landed(whole.at[pl.ds(0, (n_visit - 1) * local_rows)], rows_recv)
    shift_into(
        lambda rows, t: whole[rows, t * LANE : (t + 1) * LANE].astype(F32),
        shifted, height, breadth // LANE, 32,
    )

    def per_pair(pair, carry):
        columns_pass(shifted, column_tables, smooth, pair, count, height)

        def per_row(r, inside):
            rows = pl.ds(pl.multiple_of(r * LANE, LANE), LANE)
            columns = pl.ds(pl.multiple_of(pair * WIN, WIN), WIN)
            total[rows, columns] = -rows_pass(smooth, row_tables, count, r)
            return inside

        return lax.fori_loop(0, height // LANE, per_row, carry)

    lax.fori_loop(0, breadth // WIN, per_pair, 0)
    for h in range(halves):
        last_total[h * sizes[-1] : (h + 1) * sizes[-1], :] = total[(h + 1) * edge - sizes[-1] : (h + 1) * edge, :]

    landed(labels_in.at[pl.ds(0, n_patch - 1)], label_recv)
    for first in range(0, places, LANE // EDGE):
        lane = lax.broadcasted_iota(jnp.int32, (8, LANE), 1)
        named = jnp.full((8, LANE), -1, jnp.int32)
        for p in range(LANE // EDGE):
            place = first + p
            mark = jnp.broadcast_to(labels_in[place // CAP, place % CAP : place % CAP + 1, :], (8, LANE))
            named = jnp.where((lane >= p * EDGE) & (lane < (p + 1) * EDGE), mark, named)
        named = jnp.concatenate([named] * (EDGE // 8), axis=0)
        lane = lax.broadcasted_iota(jnp.int32, (EDGE, LANE), 1)
        same = lax.rem(lane, EDGE) == lax.broadcasted_iota(jnp.int32, (EDGE, LANE), 0)
        for s in range(slots):
            picks[s * EDGE : (s + 1) * EDGE, first * EDGE : first * EDGE + LANE] = jnp.where(
                same & (named == s), 1.0, 0.0
            ).astype(BF16)

    for c, reach in enumerate(sizes):
        landed(landing(c, 0, places - CAP), block_recv.at[c])
        if c == len(sizes) - 1:
            continue

        def add(r, carry, c=c):
            pieces = jnp.concatenate(
                [
                    arrived[pl.ds(pl.multiple_of(places * starts[c] + p * sizes[c] + r * EDGE, EDGE), EDGE), :]
                    for p in range(places)
                ],
                axis=0,
            )
            summed = jnp.dot(picks[...], pieces, preferred_element_type=F32)
            for s in range(slots):
                rows = pl.ds(pl.multiple_of(s // wide * edge + starts[c] + r * EDGE, EDGE), EDGE)
                columns = slice(s % wide * edge, (s % wide + 1) * edge)
                total[rows, columns] += summed[s * EDGE : (s + 1) * EDGE]
            return carry

        lax.fori_loop(0, reach // EDGE, add, 0, unroll=reach < LANE)

        def shift(r, carry, c=c, held=part_difference):
            lane = lax.broadcasted_iota(jnp.int32, (EDGE, LANE), 1)
            for h in range(halves):
                source = pl.ds(pl.multiple_of(h * edge + starts[c] + r * EDGE, EDGE), EDGE)
                rows = pl.ds(pl.multiple_of(h * sizes[c] + r * EDGE, EDGE), EDGE)
                before = jnp.zeros((EDGE, LANE), F32)
                for t in range(breadth // LANE):
                    rolled = pltpu.roll(total[source, t * LANE : (t + 1) * LANE], HALF, 1)
                    held[rows, t * LANE : (t + 1) * LANE] = jnp.where(lane < HALF, before, rolled).astype(BF16)
                    before = rolled
                held[rows, breadth:] = jnp.where(lane < HALF, before, 0.0).astype(BF16)
            return carry

        lax.fori_loop(0, reach // EDGE, shift, 0, unroll=reach < LANE)
        blur_rows(part_difference, psf_column_tables, blur, reach, psf_count, halves, breadth // LANE)

        def gather(t, carry, c=c, reach=reach):
            columns = pl.ds(pl.multiple_of(t * WIN, WIN), WIN)
            for h in range(halves):
                rows = slice(h * edge + starts[c], h * edge + starts[c] + reach + 2 * EDGE)
                filtered[rows, columns] += jnp.dot(
                    tables_of[reach][...], blur[h, : psf_count * reach, columns], preferred_element_type=F32
                )
            return carry

        lax.fori_loop(0, breadth // WIN, gather, 0, unroll=halves * reach <= LANE)

    landed(whole.at[pl.ds(0, (n_visit - 1) * local_rows)], rows_send)
    landed(labels_out.at[pl.ds(0, n_patch - 1)], label_send)
    landed(outgoing.at[pl.ds(0, (places - CAP) * edge)], block_send)


def finish_kernel(edge, filtered, arrived, total, picks, column_tables, table, out, difference, blur, ends, sem):
    height, breadth = out.shape
    halves = height // edge
    psf_count = column_tables.shape[1] // LANE
    reach = difference.shape[0] // halves
    places = arrived.shape[0] // reach
    wide = breadth // edge

    def put(source, first, rows):
        pltpu.make_async_copy(source, out.at[pl.ds(first, rows)], sem).start()

    done = 0
    for h in range(halves):
        upto = (h + 1) * edge - reach - EDGE
        piece = edge // 4
        for first in range(done, upto, piece):
            rows = min(piece, upto - first)
            put(filtered.at[pl.ds(EDGE + first, rows)], first, rows)
        done = upto + reach + 2 * EDGE
    lane = lax.broadcasted_iota(jnp.int32, (EDGE, LANE), 1)
    for r in range(0, reach, EDGE):
        pieces = jnp.concatenate([arrived[p * reach + r : p * reach + r + EDGE, :] for p in range(places)], axis=0)
        summed = jnp.dot(picks[...], pieces, preferred_element_type=F32)
        for h in range(halves):
            rows = slice(h * reach + r, h * reach + r + EDGE)
            before = jnp.zeros((EDGE, LANE), F32)
            for t in range(breadth // LANE):
                start = t * LANE
                slot = h * wide + start // edge
                value = (
                    total[rows, start : start + LANE]
                    + summed[slot * EDGE : (slot + 1) * EDGE, start % edge : start % edge + LANE]
                )
                rolled = pltpu.roll(value, HALF, 1)
                difference[rows, start : start + LANE] = jnp.where(lane < HALF, before, rolled).astype(BF16)
                before = rolled
            difference[rows, breadth:] = jnp.where(lane < HALF, before, 0.0).astype(BF16)
    blur_rows(difference, column_tables, blur, reach, psf_count, halves, breadth // LANE)
    for h in range(halves):
        first = (h + 1) * edge - reach
        for t in range(breadth // WIN):
            columns = slice(t * WIN, (t + 1) * WIN)
            ends[h, :, columns] = filtered[first : first + reach + 2 * EDGE, columns] + jnp.dot(
                table[...], blur[h, :, columns], preferred_element_type=F32
            )
        rows = reach + 2 * EDGE if h < halves - 1 else reach + EDGE
        put(ends.at[h, pl.ds(0, rows)], first - EDGE, rows)
    pltpu.make_async_copy(out, out, sem).wait()


SMEM = pl.BlockSpec(memory_space=pltpu.SMEM)
HBM = pl.BlockSpec(memory_space=pltpu.HBM)
VMEM = pl.BlockSpec(memory_space=pltpu.VMEM)


def stencil_scratch(count, height, breadth):
    return [
        pltpu.VMEM((height, breadth + LANE), BF16),
        pltpu.VMEM((WIN, count * LANE), BF16),
        pltpu.VMEM((count, LANE, WIN), BF16),
        pltpu.VMEM((count, height + 2 * HALF, WIN), BF16),
    ]


def per_device(blocks, block_patch, block_slot, block_count, template, basis_rows, basis_cols, coeffs, psf_rows, psf_cols):
    n_patch = lax.axis_size("patch")
    n_visit = lax.axis_size("visit")
    local_rows, breadth = template.shape[1:]
    height = local_rows * n_visit
    entries, edge = blocks.shape[2:4]
    halves = height // edge
    slots = halves * (breadth // edge)
    places = n_patch * CAP
    count = basis_rows.shape[0]
    psf_count = psf_rows.shape[1]
    sizes = cuts(edge)
    reaches = sorted(set(sizes[:-1]) - {sizes[-1]})
    most = max(sizes)
    final = sizes[-1]
    dma = pltpu.SemaphoreType.DMA
    handed = pl.pallas_call(
        functools.partial(exchange_kernel, n_patch, n_visit),
        out_shape=(
            jax.ShapeDtypeStruct((height + 2 * EDGE, breadth), F32),
            jax.ShapeDtypeStruct((places * final, edge), BF16),
            jax.ShapeDtypeStruct((halves * final, breadth), F32),
            jax.ShapeDtypeStruct((slots * EDGE, places * EDGE), BF16),
            jax.ShapeDtypeStruct((WIN, psf_count * LANE), BF16),
            jax.ShapeDtypeStruct((final + 2 * EDGE, psf_count * final), BF16),
        ),
        in_specs=[pl.BlockSpec(memory_space=pl.ANY)] + [HBM] * 9,
        out_specs=(VMEM,) * 6,
        scratch_shapes=[
            pltpu.SMEM((1, 1), jnp.int32),
            pltpu.SMEM((entries,), jnp.int32),
            pltpu.SMEM((entries,), jnp.int32),
            pltpu.SMEM(coeffs.shape, F32),
            pltpu.VMEM(basis_rows.shape, BF16),
            pltpu.VMEM(basis_cols.shape, F32),
            pltpu.VMEM(psf_rows.shape, BF16),
            pltpu.VMEM(psf_cols.shape, BF16),
            dma((8,)),
            pltpu.SMEM((places,), jnp.int32),
            pltpu.VMEM((pl.cdiv(max(count, psf_count), 8) * 8, WIN), F32),
            pltpu.VMEM((places * edge, edge), BF16),
            pltpu.VMEM((places * edge, edge), BF16),
            pltpu.VMEM((n_patch, CAP, LANE), jnp.int32),
            pltpu.VMEM((n_patch, CAP, LANE), jnp.int32),
            pltpu.VMEM((height, breadth), BF16),
            pltpu.VMEM((height, breadth), F32),
        ]
        + stencil_scratch(count, height, breadth)
        + [
            pltpu.VMEM((halves, psf_count * most, breadth), BF16),
            pltpu.VMEM((halves * most, breadth + LANE), BF16),
        ]
        + [pltpu.VMEM((reach + 2 * EDGE, psf_count * reach), BF16) for reach in reaches]
        + [pltpu.VMEM((entries, size, edge), BF16) for size in sizes]
        + [
            dma((3,)),
            dma(()),
            dma(()),
            dma((len(sizes),)),
            dma(()),
            dma(()),
            dma(()),
            dma(()),
            pltpu.SemaphoreType.REGULAR((3,)),
        ],
        compiler_params=pltpu.CompilerParams(
            collective_id=0, has_side_effects=True, vmem_limit_bytes=VMEM_LIMIT
        ),
    )(
        block_count,
        *(
            pltpu.with_memory_space_constraint(value, pltpu.HBM)
            for value in (
                block_patch.reshape(entries), block_slot.reshape(entries), coeffs,
                basis_rows, basis_cols, psf_rows, psf_cols, blocks[0, 0], template[0],
            )
        )
    )
    filtered = pl.pallas_call(
        functools.partial(finish_kernel, edge),
        out_shape=jax.ShapeDtypeStruct((height, breadth), F32),
        in_specs=[VMEM] * 6,
        out_specs=HBM,
        scratch_shapes=[
            pltpu.VMEM((halves * final, breadth + LANE), BF16),
            pltpu.VMEM((halves, psf_count * final, breadth), BF16),
            pltpu.VMEM((halves, final + 2 * EDGE, breadth), F32),
            dma(()),
        ],
        compiler_params=pltpu.CompilerParams(vmem_limit_bytes=16 * 1024 * 1024),
    )(*handed)
    return filtered[None, None]


def solution(mesh):
    return jax.shard_map(
        per_device,
        mesh=mesh,
        in_specs=(
            P("patch", "visit", None, None, None),
            P("patch", "visit", None, None),
            P("patch", "visit", None),
            P("patch", "visit"),
            P("patch", "visit", None),
            P(),
            P(),
            P("visit", None),
            P("visit", None, None),
            P("visit", None, None),
        ),
        out_specs=P("patch", "visit", None, None),
        check_vma=False,
    )
```
